32 devices in a mesh: clip: 16 (over z, y, core), tm: 2 (over x).
Axes of the slice: x: 2, y: 2, z: 4, core: 2. Of those that a mesh axis runs over, the one named last changes fastest.
Arguments:
- visible: bfloat16 [2, 25088, 384], P(None, ('clip', 'tm')), may hold values from -6 to 6
- mask_flags: int32 [2, 25088], P(None, ('clip', 'tm')), may hold values 0 or 1
- frames: int32 [32], replicated, may hold values from 2 to 8, as said below
- assign: int32 [2, 16], P(None, 'clip'), may hold values from 0 to 31, as said below
- cotangent: bfloat16 [2, 25088, 384], P(None, ('clip', 'tm')), may hold values from -6 to 6
- mask_token: bfloat16 [384], P('clip'), may hold values from -5 to 5
- time_embed: bfloat16 [8, 384], P(None, 'clip'), may hold values from -4 to 4
- space_embed: bfloat16 [196, 384], P(None, 'clip'), may hold values from -4 to 4
- norm1_gain: bfloat16 [384], P('clip'), may hold values from 0.5 to 1.5
- norm1_bias: bfloat16 [384], P('clip'), may hold values from -2 to 2
- w_qkv: bfloat16 [384, 1152], P('clip'), may hold values from -0.3125 to 0.3125
- bias_query: bfloat16 [384], P('clip'), may hold values from -2 to 2
- bias_value: bfloat16 [384], P('clip'), may hold values from -2 to 2
- w_out: bfloat16 [384, 384], P('clip'), may hold values from -1.25 to 1.25
- bias_out: bfloat16 [384], P('clip'), may hold values from -2 to 2
- norm2_gain: bfloat16 [384], P('clip'), may hold values from 0.5 to 1.5
- norm2_bias: bfloat16 [384], P('clip'), may hold values from -2 to 2
- w_up: bfloat16 [384, 1536], P('clip'), may hold values from -0.3125 to 0.3125
- bias_up: bfloat16 [1536], P('clip'), may hold values from -3 to 3
- w_down: bfloat16 [1536, 384], P('clip'), may hold values from -0.21875 to 0.21875
- bias_down: bfloat16 [384], P('clip'), may hold values from -2 to 2
Outputs:
- block_output: bfloat16 [2, 25088, 384], P(None, ('clip', 'tm'))
- grad_visible: float32 [2, 25088, 384], P(None, ('clip', 'tm'))
- grad_mask_token: float32 [384], P('clip')
- grad_time_embed: float32 [8, 384], P(None, 'clip')
- grad_space_embed: float32 [196, 384], P(None, 'clip')
- grad_norm1_gain: float32 [384], P('clip')
- grad_norm1_bias: float32 [384], P('clip')
- grad_w_qkv: float32 [384, 1152], P('clip')
- grad_bias_query: float32 [384], P('clip')
- grad_bias_value: float32 [384], P('clip')
- grad_w_out: float32 [384, 384], P('clip')
- grad_bias_out: float32 [384], P('clip')
- grad_norm2_gain: float32 [384], P('clip')
- grad_norm2_bias: float32 [384], P('clip')
- grad_w_up: float32 [384, 1536], P('clip')
- grad_bias_up: float32 [1536], P('clip')
- grad_w_down: float32 [1536, 384], P('clip')
- grad_bias_down: float32 [384], P('clip')
The draws below stay inside these ranges and needn't reach their ends.
Inputs may be any that keep to these rules, and one draw needn't show every extreme that they name: Each entry is 2, 4 or 8; in every column of assign at least one of the 2 clips has 8 frames. `assign`: A permutation of the clip numbers 0 to 31.
All inputs are finite; a program needn't handle non-finite values. No bound on the sum of `mask_flags` on one device may be relied on, other than what follows from the above.
Results may differ from the reference program's by a relative error of at most 0.014.
Values may be sent and summed in bfloat16 or wider, within the bound.
A program may use at most 192 MiB of HBM per device.

```python
import jax
import jax.numpy as jnp
from jax import lax

D = 384
HEADS = 6
HEAD_SIZE = 64
FF = 1536
FT = 196
M_B = 2
FG = 8
TOK = 25088
CLIPS = 32
N_CLIP = 16


def clip_plan(key):
    folded = jax.random.fold_in(key, 11)
    pick_key, full_key, perm_key = jax.random.split(folded, 3)
    groups = CLIPS // M_B
    lottery = jax.random.randint(pick_key, (M_B, groups), 0, 10)
    lengths = jnp.where(lottery < 4, FG // 4, jnp.where(lottery < 7, FG // 2, FG))
    longest = jax.random.randint(full_key, (groups,), 0, M_B)
    batch_ids = jnp.arange(M_B, dtype=jnp.int32)
    lengths = jnp.where(batch_ids[:, None] == longest[None, :], FG, lengths).astype(jnp.int32)
    ordering = jax.random.permutation(perm_key, CLIPS).astype(jnp.int32)
    frame_counts = jnp.zeros((CLIPS,), jnp.int32).at[ordering].set(lengths.reshape(-1))
    return (frame_counts, ordering.reshape(M_B, groups))


def draw_frames(key, part):
    return clip_plan(key)[0]


def draw_assign(key, part):
    return clip_plan(key)[1]


def touch_ends(values, key, smallest, largest):
    spot = [jax.random.randint(jax.random.fold_in(key, axis), (), 0, length) for axis, length in enumerate(values.shape)]
    widest = values.shape.index(max(values.shape))
    beside = spot[:widest] + [(spot[widest] + 1) % values.shape[widest]] + spot[widest + 1:]
    return values.at[tuple(spot)].set(smallest).at[tuple(beside)].set(largest)


def block_levels(own_key, shape, shards, smallest, high):
    level, own = 1.0, jax.random.fold_in(own_key, 6)
    for position, parts in shards:
        draws = jnp.exp(jax.random.uniform(jax.random.fold_in(own, position), (parts,), jnp.float32, smallest / len(shards), high / len(shards)))
        level = level * jnp.repeat(draws, shape[position] // parts).reshape([-1 if axis == position else 1 for axis in range(len(shape))])
    return level


def gaussian(key, dims, width, reach, shards=(), held_as=jnp.bfloat16):
    array = width * jax.random.normal(key, dims, jnp.float32)
    if shards:
        array = array * block_levels(key, dims, shards, -0.22, 0.18)
    return jnp.clip(array, -reach, reach).astype(held_as)


def setup_inputs(seed: int = 0) -> dict:
    key_of = jax.random.split(jax.random.key(seed), 22)
    visible = gaussian(key_of[0], (M_B, TOK, D), 1.0, 6.0, ((1, 32),))
    mask_flags = touch_ends((jax.random.randint(key_of[1], (M_B, TOK), 0, 10) < 9).astype(jnp.int32), jax.random.fold_in(key_of[1], 1), 0, 1)
    frames = draw_frames(jax.random.fold_in(key_of[21], 71), 0)
    assign = draw_assign(jax.random.fold_in(key_of[21], 71), 0)
    cotangent = gaussian(key_of[4], (M_B, TOK, D), 1.0, 6.0, ((1, 32),))
    mask_token = gaussian(key_of[5], (D,), 1.0, 5.0, ((0, 16),))
    time_embed = gaussian(key_of[6], (FG, D), 0.7, 4.0, ((1, 16),))
    space_embed = gaussian(key_of[7], (FT, D), 0.7, 4.0, ((1, 16),))
    norm1_gain = jnp.clip(1.0 + 0.1 * jax.random.normal(key_of[8], (D,), jnp.float32), 0.5, 1.5).astype(jnp.bfloat16)
    norm1_bias = gaussian(key_of[9], (D,), 0.3, 2.0, ((0, 16),))
    w_qkv = gaussian(key_of[10], (D, 3 * D), D ** -0.5, 0.3125, ((0, 16),))
    bias_query = gaussian(key_of[11], (D,), 0.3, 2.0, ((0, 16),))
    bias_value = gaussian(key_of[12], (D,), 0.3, 2.0, ((0, 16),))
    w_out = gaussian(key_of[13], (D, D), (D // 16) ** -0.5, 1.25, ((0, 16),))
    bias_out = gaussian(key_of[14], (D,), 0.3, 2.0, ((0, 16),))
    norm2_gain = jnp.clip(1.0 + 0.1 * jax.random.normal(key_of[15], (D,), jnp.float32), 0.5, 1.5).astype(jnp.bfloat16)
    norm2_bias = gaussian(key_of[16], (D,), 0.3, 2.0, ((0, 16),))
    w_up = gaussian(key_of[17], (D, FF), D ** -0.5, 0.3125, ((0, 16),))
    bias_up = gaussian(key_of[18], (FF,), 0.5, 3.0, ((0, 16),))
    w_down = gaussian(key_of[19], (FF, D), (FF // 2) ** -0.5, 0.21875, ((0, 16),))
    bias_down = gaussian(key_of[20], (D,), 0.3, 2.0, ((0, 16),))
    return dict(visible=visible, mask_flags=mask_flags, frames=frames, assign=assign, cotangent=cotangent, mask_token=mask_token, time_embed=time_embed, space_embed=space_embed, norm1_gain=norm1_gain, norm1_bias=norm1_bias, w_qkv=w_qkv, bias_query=bias_query, bias_value=bias_value, w_out=w_out, bias_out=bias_out, norm2_gain=norm2_gain, norm2_bias=norm2_bias, w_up=w_up, bias_up=bias_up, w_down=w_down, bias_down=bias_down)


EPS = 1e-06
NEG_FILL = -1000000000.0
HIGHEST = lax.Precision.HIGHEST

@jax.custom_vjp
def low(v):
    return lax.optimization_barrier(v.astype(jnp.bfloat16)).astype(jnp.float32)

@jax.custom_vjp
def low_back(v):
    return v

def low_keep(v):
    return (low(v), None)

def low_pass(kept, grad):
    return (grad,)

def back_keep(v):
    return (v, None)

def back_low(kept, grad):
    return (low(grad),)
low.defvjp(low_keep, low_pass)
low_back.defvjp(back_keep, back_low)

def normalize(values, gain_vec, shift_vec):
    average = lax.optimization_barrier(jnp.mean(values, axis=-1, keepdims=True))
    centred = values - average
    variance = lax.optimization_barrier(jnp.mean(centred * centred, axis=-1, keepdims=True))
    return centred * lax.rsqrt(variance + EPS) * gain_vec + shift_vec

def position_weights(frame_ids, length, table_rows):
    denominator = jnp.maximum(length - 1, 1)
    numerator = frame_ids * (table_rows - 1)
    low_row = jnp.minimum(numerator // denominator, table_rows - 1)
    high_row = jnp.minimum(low_row + 1, table_rows - 1)
    fraction = (numerator % denominator).astype(jnp.float32) / denominator.astype(jnp.float32)
    columns = jnp.arange(table_rows, dtype=jnp.int32)
    low_hit = (columns[None, :] == low_row[:, None]).astype(jnp.float32)
    high_hit = (columns[None, :] == high_row[:, None]).astype(jnp.float32)
    return (1.0 - fraction)[:, None] * low_hit + fraction[:, None] * high_hit

def allowed_keys(frame_ids, length, frame_tokens):
    offsets = jnp.arange(3 * frame_tokens, dtype=jnp.int32) // frame_tokens - 1
    key_frames = frame_ids[:, None] + offsets[None, :]
    key_ok = (key_frames >= 0) & (key_frames < length)
    query_ok = frame_ids < length
    return key_ok | jnp.logical_not(query_ok)[:, None]

def window_stack(extended, frame_count):
    return jnp.stack([extended[0:frame_count], extended[1:frame_count + 1], extended[2:frame_count + 2]], axis=1)

def clip_forward(weights, seen, flags, length):
    mask_token, time_embed, space_embed, norm1_gain, norm1_bias, w_qkv, bias_query, bias_value, w_out, bias_out, norm2_gain, norm2_bias, w_up, bias_up, w_down, bias_down = weights
    frame_ids = jnp.arange(FG, dtype=jnp.int32)
    valid = (frame_ids < length).astype(jnp.float32)
    temporal = jnp.dot(position_weights(frame_ids, length, FG), time_embed, precision=HIGHEST)
    base = jnp.where(flags[:, :, None] == 1, mask_token, seen) + temporal[:, None, :] + space_embed[None]
    rows = (base * valid[:, None, None]).reshape(FG * FT, D)
    hidden_one = low(normalize(rows, norm1_gain, norm1_bias))
    projected = jnp.dot(hidden_one, w_qkv, precision=HIGHEST)
    queries = low(low_back(projected[:, :D] + bias_query)).reshape(FG, FT, HEADS, HEAD_SIZE)
    keys_all = low(low_back(projected[:, D:2 * D])).reshape(FG, FT, D)
    values_all = low(low_back(projected[:, 2 * D:] + bias_value)).reshape(FG, FT, D)
    pairs = jnp.concatenate([keys_all, values_all], axis=-1)
    extended = jnp.pad(pairs, ((1, 1), (0, 0), (0, 0)))
    windows = window_stack(extended, FG).reshape(FG, 3 * FT, 2 * D)
    key_win = windows[..., :D].reshape(FG, 3 * FT, HEADS, HEAD_SIZE)
    val_win = windows[..., D:].reshape(FG, 3 * FT, HEADS, HEAD_SIZE)
    scores = low_back(jnp.einsum('fqhd,fkhd->fhqk', queries, key_win, precision=HIGHEST) * HEAD_SIZE ** (-0.5))
    allowed = allowed_keys(frame_ids, length, FT)[:, None, None, :]
    probs = low(jax.nn.softmax(jnp.where(allowed, scores, NEG_FILL), axis=-1))
    attended = jnp.einsum('fhqk,fkhd->fqhd', probs, val_win, precision=HIGHEST).reshape(FG * FT, D)
    attended = low(low_back(attended))
    mixed = rows + low_back(jnp.dot(attended, w_out, precision=HIGHEST) + bias_out)
    hidden_two = low(normalize(mixed, norm2_gain, norm2_bias))
    up_pre = low_back(jnp.dot(hidden_two, w_up, precision=HIGHEST) + bias_up)
    activated = low(jax.nn.gelu(up_pre, approximate=False))
    result = mixed + low_back(jnp.dot(activated, w_down, precision=HIGHEST) + bias_down)
    return result.reshape(FG, FT, D) * valid[:, None, None]

def reference(visible, mask_flags, frames, assign, cotangent, mask_token, time_embed, space_embed, norm1_gain, norm1_bias, w_qkv, bias_query, bias_value, w_out, bias_out, norm2_gain, norm2_bias, w_up, bias_up, w_down, bias_down):
    params = tuple((weight_in.astype(jnp.float32) for weight_in in (mask_token, time_embed, space_embed, norm1_gain, norm1_bias, w_qkv, bias_query, bias_value, w_out, bias_out, norm2_gain, norm2_bias, w_up, bias_up, w_down, bias_down)))
    clip_ids = assign.reshape(-1).astype(jnp.int32)
    lengths = frames[clip_ids]
    count_all = M_B * N_CLIP
    seen_all = visible.astype(jnp.float32).reshape(count_all, FG, FT, D)
    flags_all = mask_flags.reshape(count_all, FG, FT)
    cot_all = cotangent.astype(jnp.float32).reshape(count_all, FG, FT, D)

    def one_clip(totals, inputs):
        seen_clip, flags_clip, cot_clip, length = inputs

        def forward(weights_in, seen_in):
            return clip_forward(weights_in, seen_in, flags_clip, length)
        outputs, pullback = jax.vjp(forward, params, seen_clip)
        grad_params, grad_seen = pullback(cot_clip)
        totals = tuple((total_one + grad_one for total_one, grad_one in zip(totals, grad_params)))
        return (totals, (outputs, grad_seen))
    zeros_init = tuple((jnp.zeros(weight_in.shape, jnp.float32) for weight_in in params))
    grads, (outputs, grad_seen) = lax.scan(one_clip, zeros_init, (seen_all, flags_all, cot_all, lengths))
    block_output = outputs.reshape(M_B, TOK, D).astype(jnp.bfloat16)
    grad_visible = grad_seen.reshape(M_B, TOK, D)
    return (block_output, grad_visible, grads[0], grads[1], grads[2], grads[3], grads[4], grads[5], grads[6], grads[7], grads[8], grads[9], grads[10], grads[11], grads[12], grads[13], grads[14], grads[15])
```

```python
import functools
import math

import jax
import jax.numpy as jnp
from jax import lax
from jax.experimental import pallas as pl
from jax.experimental.pallas import tpu as pltpu
from jax.sharding import PartitionSpec as P

D = 384
FF = 1536
FT = 196
FD = 4
MB = 2
NB = MB * FD
ROWS = 208
WIN = 3 * ROWS
EPS = 1e-06
NEG = -1000000000.0
SMALL = 256
SPACE = 24
UPB = 17
MESH = pl.DeviceIdType.MESH
f32 = jnp.float32
bf16 = jnp.bfloat16


def contract(a, b, ca, cb):
    return lax.dot_general(a, b, (((ca,), (cb,)), ((), ())), preferred_element_type=f32)


def norm_stats(x):
    c = x - jnp.mean(x, axis=-1, keepdims=True)
    r = lax.rsqrt(jnp.mean(c * c, axis=-1, keepdims=True) + EPS)
    return c * r, r


def norm_back(g, xhat, r, gain):
    d = g * gain
    first = jnp.mean(d, axis=-1, keepdims=True)
    second = jnp.mean(d * xhat, axis=-1, keepdims=True)
    return r * (d - first - xhat * second)


def col_sum(x):
    return jnp.sum(x.astype(f32), axis=0, keepdims=True)


def time_weights(shape, frame_dim, tm, lengths):
    block = lax.broadcasted_iota(jnp.int32, shape, frame_dim)
    row = lax.broadcasted_iota(jnp.int32, shape, 1 - frame_dim).astype(f32)
    length = jnp.where(block < FD, lengths[0].astype(f32), lengths[1].astype(f32))
    frame = (jnp.where(block < FD, block, block - FD) + FD * tm).astype(f32)
    den = jnp.maximum(length - 1.0, 1.0)
    num = frame * 7.0
    whole = jnp.floor((num + 0.5) / den)
    low = jnp.minimum(whole, 7.0)
    high = jnp.minimum(low + 1.0, 7.0)
    part = (num - whole * den) / den
    return jnp.where(row == low, 1.0 - part, 0.0) + jnp.where(row == high, part, 0.0)


def body(
    frames_ref, assign_ref, vis, mask, cot, small, bup, wqkv, wout, wup, wdown,
    out, gvis, gqkv_o, gout_o, gup_o, gdown_o, gsm, gbup_o,
    x0s, a1s, qs, kv, probs, os_, cots, gx1s, gos, gkv, gqs, temporal, sumgb, back_out, back_in,
    halo_sem, back_sem,
):
    tm = lax.axis_index("tm")
    peer = {"tm": 1 - tm}
    barrier = pltpu.get_barrier_semaphore()
    pl.semaphore_signal(barrier, inc=1, device_id=peer, device_id_type=MESH)
    pl.semaphore_wait(barrier, 1)

    lengths = [frames_ref[assign_ref[m, 0]] for m in range(MB)]
    lane = lax.broadcasted_iota(jnp.int32, (1, 128), 1)
    first_head = lane < 64
    row_ok = (lax.broadcasted_iota(jnp.int32, (ROWS, 1), 0) < FT).astype(f32)
    mask_cols = jnp.transpose(mask[...])

    def length_of(m):
        return jnp.where(m == 0, lengths[0], lengths[1])

    def valid_of(m, j):
        return jnp.where(FD * tm + j < length_of(m), 1.0, 0.0).astype(f32)

    def near_last(i):
        jj = i // MB
        return i - MB * jj, jj + tm * (FD - 1 - 2 * jj)

    def near_first(i):
        return near_last(NB - 1 - i)

    weights = time_weights((NB, 8), 0, tm, lengths)
    total = jnp.zeros((NB, D), f32)
    for t in range(8):
        total = total + weights[:, t : t + 1] * small[1 + t : 2 + t, :]
    temporal[...] = total
    pad = jnp.zeros((ROWS - FT, D), f32)
    for m in range(MB):
        for j in range(FD):
            b = m * FD + j
            valid = row_ok * valid_of(m, j)
            seen = jnp.concatenate([vis[m, FT * j : FT * (j + 1), :].astype(f32), pad], axis=0)
            base = jnp.where(mask_cols[:ROWS, b : b + 1] > 0.5, small[0:1, :], seen)
            base = base + temporal[b : b + 1, :] + small[SPACE : SPACE + ROWS, :]
            x0s[b] = base * valid
            top = jnp.concatenate([cot[m, FT * j : FT * (j + 1), :].astype(f32), pad], axis=0)
            cots[b] = (top * valid).astype(bf16)

    def project(b, carry):
        m = b // FD
        xhat, _ = norm_stats(x0s[b])
        a1 = (xhat * small[9:10, :] + small[10:11, :]).astype(bf16)
        a1s[b] = a1
        p = contract(a1, wqkv[...], 1, 0)
        q = (p[:, :D] + small[11:12, :]).astype(bf16).astype(f32)
        qs[b] = (q * 0.125).astype(bf16)
        kv[m, b - m * FD + 1, :, :D] = p[:, D : 2 * D].astype(bf16)
        kv[m, b - m * FD + 1, :, D:] = (p[:, 2 * D :] + small[12:13, :]).astype(bf16)
        return carry

    lax.fori_loop(0, NB, project, 0)

    halos = []
    for m in range(MB):
        halo = pltpu.make_async_remote_copy(
            src_ref=kv.at[m, FD - (FD - 1) * tm], dst_ref=kv.at[m, (FD + 1) * tm],
            send_sem=halo_sem.at[0, m], recv_sem=halo_sem.at[1, m], device_id=peer, device_id_type=MESH,
        )
        halo.start()
        halos.append(halo)
        kv[m, (FD + 1) * tm] = jnp.zeros((ROWS, 2 * D), bf16)

    key = lax.broadcasted_iota(jnp.int32, (1, WIN), 1)
    slot = (key >= ROWS).astype(jnp.int32) + (key >= 2 * ROWS).astype(jnp.int32)
    key_real = key - slot * ROWS < FT

    def stack_heads(x):
        zero = jnp.zeros_like(x)
        return jnp.concatenate([jnp.where(first_head, x, zero), jnp.where(first_head, zero, x)], axis=0)

    def join_heads(x):
        return jnp.where(first_head, x[:ROWS], x[ROWS:])

    def window(m, j, c):
        return kv[m, pl.ds(j, 3), :, c : c + 128].reshape(WIN, 128)

    def attend(i, carry):
        m, j = near_last(i)
        b = m * FD + j
        for k in range(MB):

            @pl.when(i == NB - MB + k)
            def _():
                halos[k].wait()

        frame = FD * tm + j
        length = length_of(m)
        key_frame = frame - 1 + slot
        allowed = ((key_frame >= 0) & (key_frame < length)) | (frame >= length)
        bias = jnp.where(allowed & key_real, 0.0, NEG)
        for p in range(3):
            c = 128 * p
            s = contract(stack_heads(qs[b, :, c : c + 128]), window(m, j, c), 1, 1) + bias
            e = jnp.exp(s - jnp.max(s, axis=-1, keepdims=True))
            pr = (e * (1.0 / jnp.sum(e, axis=-1, keepdims=True))).astype(bf16)
            probs[b, p] = pr
            os_[b, :, c : c + 128] = join_heads(contract(pr, window(m, j, D + c), 1, 0)).astype(bf16)
        return carry

    lax.fori_loop(0, NB, attend, 0)

    gout_o[...] = jnp.zeros_like(gout_o)
    gup_o[...] = jnp.zeros_like(gup_o)
    gdown_o[...] = jnp.zeros_like(gdown_o)
    gsm[...] = jnp.zeros_like(gsm)
    gbup_o[...] = jnp.zeros_like(gbup_o)

    def feed(b, carry):
        m = b // FD
        j = b - m * FD
        valid = row_ok * valid_of(m, j)
        o = os_[b]
        x1 = x0s[b] + contract(o, wout[...], 1, 0) + small[13:14, :]
        xhat, r = norm_stats(x1)
        a2 = (xhat * small[14:15, :] + small[15:16, :]).astype(bf16)
        u = contract(a2, wup[...], 1, 0) + bup[...]
        cdf = 0.5 + 0.5 * lax.erf(u * (1.0 / math.sqrt(2.0)))
        pdf = jnp.exp(u * u * -0.5) * (1.0 / math.sqrt(2.0 * math.pi))
        z = (u * cdf).astype(bf16)
        slope = cdf + u * pdf
        x2 = x1 + contract(z, wdown[...], 1, 0) + small[16:17, :]
        y = (x2 * valid)[:FT].astype(bf16)
        for k in range(FD):

            @pl.when(j == k)
            def _():
                out[m, FT * k : FT * (k + 1), :] = y

        g2 = cots[b]
        g2f = g2.astype(f32)
        gu = (contract(g2, wdown[...], 1, 1) * slope).astype(bf16)
        gbup_o[...] += col_sum(gu)
        gsm[16:17, :] += col_sum(g2)
        gdown_o[...] += contract(g2, z, 0, 0)
        gup_o[...] += contract(a2, gu, 0, 0)
        ga2 = contract(gu, wup[...], 1, 1)
        gsm[14:15, :] += col_sum(ga2 * xhat)
        gsm[15:16, :] += col_sum(ga2)
        gx1 = g2f + norm_back(ga2, xhat, r, small[14:15, :])
        gx1s[b] = gx1
        gy = gx1.astype(bf16)
        gsm[13:14, :] += col_sum(gy)
        gout_o[...] += contract(o, gy, 0, 0)
        gos[b] = contract(gy, wout[...], 1, 1).astype(bf16)
        return carry

    lax.fori_loop(0, NB, feed, 0)

    gkv[...] = jnp.zeros_like(gkv)
    backs = [
        pltpu.make_async_remote_copy(
            src_ref=back_out.at[m], dst_ref=back_in.at[m],
            send_sem=back_sem.at[0, m], recv_sem=back_sem.at[1, m], device_id=peer, device_id_type=MESH,
        )
        for m in range(MB)
    ]

    def attend_back(i, carry):
        m, j = near_first(i)
        b = m * FD + j
        for p in range(3):
            c = 128 * p
            q = stack_heads(qs[b, :, c : c + 128])
            o = os_[b, :, c : c + 128].astype(f32)
            go = stack_heads(gos[b, :, c : c + 128])
            delta = jnp.sum(go.astype(f32) * jnp.concatenate([o, o], axis=0), axis=-1, keepdims=True)
            pr = probs[b, p]
            gs = (pr.astype(f32) * (contract(go, window(m, j, D + c), 1, 1) - delta)).astype(bf16)
            gv = jnp.transpose(contract(go, pr, 0, 0)).reshape(3, ROWS, 128)
            gk = jnp.transpose(contract(q, gs, 0, 0)).reshape(3, ROWS, 128)
            gkv[m, pl.ds(j, 3), :, c : c + 128] += gk
            gkv[m, pl.ds(j, 3), :, D + c : D + c + 128] += gv
            gq = join_heads(contract(gs, window(m, j, c), 1, 0))
            gqs[b, :, c : c + 128] = (gq * 0.125).astype(bf16)
        for k in range(MB):

            @pl.when(i == MB - 1 - k)
            def _():
                back_out[k] = gkv[k, (FD + 1) * (1 - tm)].astype(bf16)
                backs[k].start()

        return carry

    lax.fori_loop(0, NB, attend_back, 0)

    gqkv_o[...] = jnp.zeros_like(gqkv_o)

    def finish(i, carry):
        m, j = near_last(i)
        b = m * FD + j
        for k in range(MB):

            @pl.when(i == NB - MB + k)
            def _():
                backs[k].wait()
                gkv[k, j + 1] += back_in[k].astype(f32)

        xhat, r = norm_stats(x0s[b])
        gp = jnp.concatenate([gqs[b], gkv[m, j + 1].astype(bf16)], axis=1)
        gsm[11:12, :] += col_sum(gp[:, :D])
        gsm[12:13, :] += col_sum(gp[:, 2 * D :])
        gqkv_o[...] += contract(a1s[b], gp, 0, 0)
        ga1 = contract(gp, wqkv[...], 1, 1)
        gsm[9:10, :] += col_sum(ga1 * xhat)
        gsm[10:11, :] += col_sum(ga1)
        gb = (gx1s[b] + norm_back(ga1, xhat, r, small[9:10, :])) * (row_ok * valid_of(m, j))
        column = jnp.zeros((ROWS, 1), f32)
        for k in range(NB):
            column = jnp.where(b == k, mask_cols[:ROWS, k : k + 1], column)
        masked = column > 0.5
        gsm[0:1, :] += col_sum(jnp.where(masked, gb, 0.0))
        gsm[SPACE : SPACE + ROWS, :] += gb
        sumgb[pl.ds(b, 1), :] = col_sum(gb)
        seen = jnp.where(masked, 0.0, gb)[:FT]
        for k in range(FD):

            @pl.when(j == k)
            def _():
                gvis[m, FT * k : FT * (k + 1), :] = seen

        return carry

    lax.fori_loop(0, NB, finish, 0)

    weights = time_weights((8, NB), 1, tm, lengths)
    total = jnp.zeros((8, D), f32)
    for b in range(NB):
        total = total + weights[:, b : b + 1] * sumgb[b : b + 1, :]
    gsm[1:9, :] = total


def local(
    visible, mask_flags, frames, assign, cotangent,
    mask_token, time_embed, space_embed, norm1_gain, norm1_bias, w_qkv, bias_query, bias_value,
    w_out, bias_out, norm2_gain, norm2_bias, w_up, bias_up, w_down, bias_down,
):
    part = mask_token.shape[0]
    column = lambda v: v[:, None]
    small = jnp.concatenate(
        [
            column(mask_token), time_embed.T, column(norm1_gain), column(norm1_bias), column(bias_query),
            column(bias_value), column(bias_out), column(norm2_gain), column(norm2_bias), column(bias_down),
            bias_up.reshape(part, 4), jnp.zeros((part, SPACE - UPB - 4), bf16), space_embed.T,
            jnp.zeros((part, SMALL - SPACE - FT), bf16),
        ],
        axis=1,
    )
    pack = jnp.concatenate([w_qkv, w_out, w_up, w_down.reshape(part, FF), small], axis=1)
    whole = lax.all_gather(pack, "clip", axis=0, tiled=True)
    cuts = (0, 3 * D, 4 * D, 4 * D + FF, 4 * D + 2 * FF, 4 * D + 2 * FF + SMALL)
    wqkv, wout, wup, wdown, wsmall = (whole[:, a:b] for a, b in zip(cuts[:-1], cuts[1:]))
    wdown = wdown.reshape(FF, D)
    bup = wsmall[:, UPB : UPB + 4].astype(f32).reshape(1, FF)
    table = wsmall.T.astype(f32)
    mask = jnp.pad(mask_flags.reshape(NB, FT).astype(f32), ((0, 0), (0, 256 - FT)))

    sds = jax.ShapeDtypeStruct
    smem = pl.BlockSpec(memory_space=pltpu.SMEM)
    vmem = pl.BlockSpec(memory_space=pltpu.VMEM)
    results = pl.pallas_call(
        body,
        out_shape=(
            sds(visible.shape, bf16), sds(visible.shape, f32), sds((D, 3 * D), f32), sds((D, D), f32),
            sds((D, FF), f32), sds((D, FF), f32), sds((SMALL, D), f32), sds((1, FF), f32),
        ),
        in_specs=[smem, smem] + [vmem] * 9,
        out_specs=[vmem] * 8,
        scratch_shapes=[
            pltpu.VMEM((NB, ROWS, D), f32),
            pltpu.VMEM((NB, ROWS, D), bf16),
            pltpu.VMEM((NB, ROWS, D), bf16),
            pltpu.VMEM((MB, FD + 2, ROWS, 2 * D), bf16),
            pltpu.VMEM((NB, 3, 2 * ROWS, WIN), bf16),
            pltpu.VMEM((NB, ROWS, D), bf16),
            pltpu.VMEM((NB, ROWS, D), bf16),
            pltpu.VMEM((NB, ROWS, D), f32),
            pltpu.VMEM((NB, ROWS, D), bf16),
            pltpu.VMEM((MB, FD + 2, ROWS, 2 * D), f32),
            pltpu.VMEM((NB, ROWS, D), bf16),
            pltpu.VMEM((NB, D), f32),
            pltpu.VMEM((NB, D), f32),
            pltpu.VMEM((MB, ROWS, 2 * D), bf16),
            pltpu.VMEM((MB, ROWS, 2 * D), bf16),
            pltpu.SemaphoreType.DMA((2, MB)),
            pltpu.SemaphoreType.DMA((2, MB)),
        ],
        compiler_params=pltpu.CompilerParams(
            collective_id=0, has_side_effects=True, vmem_limit_bytes=63 * 2**20
        ),
    )(frames, assign, visible, mask, cotangent, table, bup, wqkv, wout, wup, wdown)
    out, gvis, gqkv, gout, gup, gdown_t, gsm, gbup = results
    gsmall = gsm.T
    gsmall = gsmall.at[:, UPB : UPB + 4].set(gbup.reshape(D, 4))
    grads = jnp.concatenate([gqkv, gout, gup, gdown_t.T.reshape(D, FF), gsmall], axis=1)
    share = lax.psum_scatter(grads, "clip", scatter_dimension=0, tiled=True)
    share = lax.psum(share.astype(bf16), "tm").astype(f32)
    sqkv, sout, sup, sdown, ssmall = (share[:, a:b] for a, b in zip(cuts[:-1], cuts[1:]))
    return (
        out, gvis, ssmall[:, 0], ssmall[:, 1:9].T, ssmall[:, SPACE : SPACE + FT].T, ssmall[:, 9], ssmall[:, 10],
        sqkv, ssmall[:, 11], ssmall[:, 12], sout, ssmall[:, 13], ssmall[:, 14], ssmall[:, 15], sup,
        ssmall[:, UPB : UPB + 4].reshape(-1), sdown.reshape(-1, D), ssmall[:, 16],
    )


def solution(mesh):
    rows = P(None, ("clip", "tm"), None)
    vec = P("clip")
    mat = P("clip", None)
    cols = P(None, "clip")
    in_specs = (
        rows, P(None, ("clip", "tm")), P(), cols, rows,
        vec, cols, cols, vec, vec, mat, vec, vec, mat, vec, vec, vec, mat, vec, mat, vec,
    )
    out_specs = (
        rows, rows, vec, cols, cols, vec, vec, mat, vec, vec, mat, vec, vec, vec, mat, vec, mat, vec,
    )
    return jax.shard_map(local, mesh=mesh, in_specs=in_specs, out_specs=out_specs, check_vma=False)
```

```python
import functools
import math
from types import SimpleNamespace

import jax
import jax.numpy as jnp
from jax import lax
from jax.experimental import pallas as pl
from jax.experimental.pallas import tpu as pltpu
from jax.sharding import PartitionSpec as P

D = 384
FF = 1536
FT = 196
FD = 4
MB = 2
NB = MB * FD
ROWS = 208
WIN = 3 * ROWS
EPS = 1e-06
NEG = -1000000000.0
SMALL = 256
SPACE = 24
UPB = 17
MESH = pl.DeviceIdType.MESH
f32 = jnp.float32
bf16 = jnp.bfloat16

ITEMS = {"small": (SMALL, 1), "k": (D, 1), "v": (D, 1), "q": (D, 1), "out": (D, 1), "up": (FF, 1), "down": (D, 4)}
INDEX = {name: i for i, name in enumerate(ITEMS)}
VECTORS = (
    ("mask_token", 0), ("norm1_gain", 9), ("norm1_bias", 10), ("bias_query", 11), ("bias_value", 12),
    ("bias_out", 13), ("norm2_gain", 14), ("norm2_bias", 15), ("bias_down", 16),
)


def contract(a, b, ca, cb, precision=None):
    return lax.dot_general(
        a, b, (((ca,), (cb,)), ((), ())), preferred_element_type=f32, precision=precision
    )


def norm_stats(x):
    c = x - jnp.mean(x, axis=-1, keepdims=True)
    r = lax.rsqrt(jnp.mean(c * c, axis=-1, keepdims=True) + EPS)
    return c * r, r


def norm_back(g, xhat, r, gain):
    d = g * gain
    first = jnp.mean(d, axis=-1, keepdims=True)
    second = jnp.mean(d * xhat, axis=-1, keepdims=True)
    return r * (d - first - xhat * second)


def col_sum(x):
    return jnp.sum(x.astype(f32), axis=0, keepdims=True)


def iota(shape, dim):
    return lax.broadcasted_iota(jnp.int32, shape, dim)


def time_weights(shape, frame_dim, tm, lengths):
    block = iota(shape, frame_dim)
    row = iota(shape, 1 - frame_dim).astype(f32)
    length = jnp.where(block < FD, lengths[0].astype(f32), lengths[1].astype(f32))
    frame = (jnp.where(block < FD, block, block - FD) + FD * tm).astype(f32)
    den = jnp.maximum(length - 1.0, 1.0)
    num = frame * 7.0
    whole = jnp.floor((num + 0.5) / den)
    low = jnp.minimum(whole, 7.0)
    high = jnp.minimum(low + 1.0, 7.0)
    part = (num - whole * den) / den
    return jnp.where(row == low, 1.0 - part, 0.0) + jnp.where(row == high, part, 0.0)


def spread(rows, cols):
    return (iota((rows, cols), 1) // 4 == iota((rows, cols), 0)).astype(f32)


def every_fourth(x, cols):
    return jnp.where(iota((8, cols), 0) == 1 + iota((8, cols), 1) % 4, x, 0.0)


class Exchange:
    def __init__(self, r, n, part):
        self.r, self.high, self.part = r, n // 4, part
        me = lax.axis_index("clip")
        self.tm = lax.axis_index("tm")
        self.h, self.mid, self.lo = me // 4, (me // 2) % 2, me % 2

    def device(self, h, mid, lo):
        return {"clip": (h * 2 + mid) * 2 + lo}

    def others(self):
        return [(self.h + d) % self.high for d in range(1, self.high)]

    def greet(self):
        barrier = pltpu.get_barrier_semaphore()
        peers = [self.device(h, self.mid, self.lo) for h in self.others()]
        peers += [self.device(self.h, 1 - self.mid, self.lo), self.device(self.h, self.mid, 1 - self.lo)]
        peers.append({"tm": 1 - self.tm})
        for peer in peers:
            pl.semaphore_signal(barrier, inc=1, device_id=peer, device_id_type=MESH)
        pl.semaphore_wait(barrier, len(peers))

    def copy(self, src, dst, send, recv, device):
        return pltpu.make_async_remote_copy(
            src_ref=src, dst_ref=dst, send_sem=send, recv_sem=recv, device_id=device, device_id_type=MESH
        )

    def g1(self, name, source):
        r, i, buf = self.r, INDEX[name], self.r.whole[name]
        return [
            self.copy(
                source, buf.at[self.h, self.mid, self.lo], r.g1s.at[i, d], r.g1r.at[i, self.h],
                self.device(h, self.mid, self.lo),
            )
            for d, h in enumerate(self.others())
        ]

    def g1_arrivals(self, name, source):
        r, i, buf = self.r, INDEX[name], self.r.whole[name]
        for d, h in enumerate(self.others()):
            self.copy(
                source, buf.at[h, self.mid, self.lo], r.g1s.at[i, d], r.g1r.at[i, h],
                self.device(h, self.mid, self.lo),
            ).wait_recv()

    def g2(self, name, mid):
        r, i, part = self.r, INDEX[name], self.r.whole[name].at[:, mid, self.lo]
        return self.copy(part, part, r.g2s.at[i], r.g2r.at[i], self.device(self.h, 1 - self.mid, self.lo))

    def g3(self, name, lo):
        r, i, part = self.r, INDEX[name], self.r.whole[name].at[:, :, lo]
        return self.copy(part, part, r.g3s.at[i], r.g3r.at[i], self.device(self.h, self.mid, 1 - self.lo))

    def gather_1(self, name, source):
        for copy in self.g1(name, source):
            copy.start()

    def gather_2(self, name, source):
        self.g1_arrivals(name, source)
        self.g2(name, self.mid).start()

    def gather_3(self, name):
        self.g2(name, 1 - self.mid).wait_recv()
        self.g3(name, self.lo).start()

    def gather_4(self, name):
        self.g3(name, 1 - self.lo).wait_recv()

    def gather_sent(self, name, source):
        for copy in self.g1(name, source):
            copy.wait_send()
        self.g2(name, self.mid).wait_send()
        self.g3(name, self.lo).wait_send()

    def own(self, h, mid):
        return (h * 2 + mid) * 2 + self.lo

    def s1(self, name):
        r, i = self.r, INDEX[name]
        return self.copy(
            r.snd[name], r.rcv1[name], r.s1s.at[i], r.s1r.at[i], self.device(self.h, self.mid, 1 - self.lo)
        )

    def s2(self, name):
        r, i = self.r, INDEX[name]
        return self.copy(
            r.snd2[name], r.rcv2[name], r.s2s.at[i], r.s2r.at[i], self.device(self.h, 1 - self.mid, self.lo)
        )

    def s3(self, name, h, slot, d):
        r, i = self.r, INDEX[name]
        return self.copy(
            r.snd3[name].at[h], r.rcv3[name].at[slot], r.s3s.at[i, d], r.s3r.at[i, slot],
            self.device(h, self.mid, self.lo),
        )

    def s4(self, name):
        r, i = self.r, INDEX[name]
        return self.copy(r.snd4[name], r.rcv4[name], r.s4s.at[i], r.s4r.at[i], {"tm": 1 - self.tm})

    def sum_1(self, name):
        r, acc = self.r, self.r.acc[name]
        for h in range(self.high):
            for mid in range(2):
                r.snd[name][h, mid] = acc[(h * 2 + mid) * 2 + 1 - self.lo].astype(bf16)
        self.s1(name).start()

    def sum_2(self, name):
        r, acc = self.r, self.r.acc[name]
        self.s1(name).wait_recv()
        for h in range(self.high):
            away = 1 - self.mid
            r.snd2[name][h] = (acc[self.own(h, away)] + r.rcv1[name][h, away].astype(f32)).astype(bf16)
        self.s2(name).start()
        for h in range(self.high):
            acc[self.own(h, self.mid)] += r.rcv1[name][h, self.mid].astype(f32)

    def sum_3(self, name):
        r, acc = self.r, self.r.acc[name]
        self.s2(name).wait_recv()
        for d, h in enumerate(self.others()):
            r.snd3[name][h] = (acc[self.own(h, self.mid)] + r.rcv2[name][h].astype(f32)).astype(bf16)
            self.s3(name, h, self.h, d).start()

    def sum_4(self, name):
        r, acc = self.r, self.r.acc[name]
        total = acc[self.own(self.h, self.mid)] + r.rcv2[name][self.h].astype(f32)
        for d, h in enumerate(self.others()):
            self.s3(name, h, h, d).wait_recv()
            total = total + r.rcv3[name][h].astype(f32)
        r.snd4[name][...] = total.astype(bf16)
        self.s4(name).start()

    def sum_5(self, name):
        r = self.r
        self.s4(name).wait_recv()
        return r.snd4[name][...].astype(f32) + r.rcv4[name][...].astype(f32)

    def sum_sent(self, name):
        self.s1(name).wait_send()
        self.s2(name).wait_send()
        for d, h in enumerate(self.others()):
            self.s3(name, h, self.h, d).wait_send()
        self.s4(name).wait_send()


def body(names, fused, n, part, *refs):
    r = SimpleNamespace()
    for key, ref in zip(names, refs, strict=True):
        if "/" in key:
            group, item = key.split("/")
            if not hasattr(r, group):
                setattr(r, group, {})
            getattr(r, group)[item] = ref
        else:
            setattr(r, key, ref)
    tm = lax.axis_index("tm")
    peer = {"tm": 1 - tm}
    table, raw = r.table, r.raw

    lengths = [r.frames[r.assign[m, 0]] for m in range(MB)]
    first_head = iota((1, 128), 1) < 64
    row_ok = (iota((ROWS, 1), 0) < FT).astype(f32)
    pad = jnp.zeros((ROWS - FT, D), f32)

    def length_of(m):
        return jnp.where(m == 0, lengths[0], lengths[1])

    def valid_of(m, j):
        return jnp.where(FD * tm + j < length_of(m), 1.0, 0.0).astype(f32)

    def near_last(i):
        jj = i // MB
        return i - MB * jj, jj + tm * (FD - 1 - 2 * jj)

    def near_first(i):
        m = i // FD
        jj = FD - 1 - (i - m * FD)
        return m, jj + tm * (FD - 1 - 2 * jj)

    def when(i, steps):
        for k, step in steps.items():

            @pl.when(i == k)
            def _():
                step()

    load_seen = pltpu.make_async_copy(r.visible, raw, r.local_sem.at[0])
    load_top = pltpu.make_async_copy(r.cotangent, raw, r.local_sem.at[0])
    load_seen.start()
    if fused:
        x = Exchange(r, n, part)
        h, mid, lo = x.h, x.mid, x.lo
        sources = {
            "small": r.whole["small"].at[h, mid, lo], "q": r.w_qkv.at[:, 0:D], "k": r.w_qkv.at[:, D : 2 * D],
            "v": r.w_qkv.at[:, 2 * D : 3 * D], "out": r.w_out, "up": r.w_up, "down": r.w_down,
        }
        weights = [name for name in ITEMS if name != "small"]
        loads = {
            name: pltpu.make_async_copy(sources[name], r.whole[name].at[h, mid, lo], r.local_sem.at[1 + i])
            for i, name in enumerate(weights)
        }
        for load in loads.values():
            load.start()
        r.rows[...] = jnp.zeros_like(r.rows)
        for name, at in VECTORS:
            r.rows[at : at + 1, :part] = getattr(r, name)[...].astype(f32).reshape(1, part)
        r.rows[1:9, :part] = r.time_embed[...].astype(f32)
        r.rows[SPACE : SPACE + FT, :part] = r.space_embed[...].astype(f32)
        up = every_fourth(r.bias_up[...].astype(f32).reshape(1, 4 * part), 4 * part)
        up = contract(up.astype(bf16), spread(part, 4 * part).astype(bf16), 1, 1)
        r.rows[UPB : UPB + 4, :part] = up[1:5]
        r.whole["small"][h, mid, lo] = jnp.transpose(r.rows[...])[:part].astype(bf16)
        x.greet()
        for name in ("small", "k", "v", "q"):
            x.gather_1(name, sources[name])
    else:
        barrier = pltpu.get_barrier_semaphore()
        pl.semaphore_signal(barrier, inc=1, device_id=peer, device_id_type=MESH)
        pl.semaphore_wait(barrier, 1)

    flags = r.mask_flags[...].astype(f32)
    r.flag_rows[...] = jnp.zeros_like(r.flag_rows)
    for m in range(MB):
        for j in range(FD):
            r.flag_rows[m * FD + j : m * FD + j + 1, :FT] = flags[m : m + 1, FT * j : FT * (j + 1)]
    r.flag_cols[...] = jnp.transpose(r.flag_rows[...])

    def unpack(m, j):
        return jnp.concatenate([raw[m, FT * j : FT * (j + 1), :].astype(f32), pad], axis=0)

    load_seen.wait()
    for m in range(MB):
        for j in range(FD):
            r.x0s[m * FD + j] = unpack(m, j)
    load_top.start()
    load_top.wait()
    for m in range(MB):
        for j in range(FD):
            r.tops[m * FD + j] = (unpack(m, j) * (row_ok * valid_of(m, j))).astype(bf16)

    def settle(name, target):
        whole = r.whole[name]
        for i in range(n // 2):
            two = jnp.concatenate([whole[i // 2, i % 2, 0].astype(f32), whole[i // 2, i % 2, 1].astype(f32)], axis=0)
            target(slice(2 * part * i, 2 * part * (i + 1)), two)

    def place(ref, start):
        width = None

        def put(rows, value):
            ref[rows, start : start + value.shape[1]] = value.astype(ref.dtype)

        return put

    if fused:
        for load in loads.values():
            load.wait()
        for name in ("small", "k", "v", "q"):
            x.gather_2(name, sources[name])
        for name in ("out", "up", "down"):
            x.gather_1(name, sources[name])
        for name in ("small", "k", "v", "q"):
            x.gather_3(name)
        x.gather_4("small")
        settle("small", place(r.acc_small_cols, 0))
        table[...] = jnp.transpose(r.acc_small_cols[...])
        expand = spread(128, 512).astype(bf16)
        for k in range(3):
            four = contract(table[16:24, 128 * k : 128 * (k + 1)].astype(bf16), expand, 1, 0)
            r.bup[:, 512 * k : 512 * (k + 1)] = jnp.sum(every_fourth(four, 512), axis=0, keepdims=True)

    blend = time_weights((NB, 8), 0, tm, lengths)
    total = jnp.zeros((NB, D), f32)
    for t in range(8):
        total = total + blend[:, t : t + 1] * table[1 + t : 2 + t, :]
    r.temporal[...] = total
    for m in range(MB):
        for j in range(FD):
            b = m * FD + j
            base = jnp.where(r.flag_cols[:ROWS, b : b + 1] > 0.5, table[0:1, :], r.x0s[b])
            base = base + r.temporal[b : b + 1, :] + table[SPACE : SPACE + ROWS, :]
            r.x0s[b] = base * (row_ok * valid_of(m, j))

    if fused:
        for name, start in (("k", D), ("v", 2 * D), ("q", 0)):
            x.gather_4(name)
            settle(name, place(r.wqkv, start))

    kv = r.kv

    def project(b, carry):
        m = b // FD
        j = b - m * FD
        xhat, _ = norm_stats(r.x0s[b])
        a1 = (xhat * table[9:10, :] + table[10:11, :]).astype(bf16)
        p = contract(a1, r.wqkv[...], 1, 0)
        q = (p[:, :D] + table[11:12, :]).astype(bf16).astype(f32)
        r.qs[b] = (q * 0.125).astype(bf16)
        kv[m, j + 1, :, :D] = p[:, D : 2 * D].astype(bf16)
        kv[m, j + 1, :, D:] = (p[:, 2 * D :] + table[12:13, :]).astype(bf16)
        return carry

    lax.fori_loop(0, NB, project, 0)

    halos = []
    for m in range(MB):
        halo = pltpu.make_async_remote_copy(
            src_ref=kv.at[m, FD - (FD - 1) * tm], dst_ref=kv.at[m, (FD + 1) * tm],
            send_sem=r.halo_sem.at[0, m], recv_sem=r.halo_sem.at[1, m], device_id=peer, device_id_type=MESH,
        )
        halo.start()
        halos.append(halo)
        kv[m, (FD + 1) * tm] = jnp.zeros((ROWS, 2 * D), bf16)

    key = iota((1, WIN), 1)
    slot = (key >= ROWS).astype(jnp.int32) + (key >= 2 * ROWS).astype(jnp.int32)
    key_real = key - slot * ROWS < FT

    def stack_heads(v):
        zero = jnp.zeros_like(v)
        return jnp.concatenate([jnp.where(first_head, v, zero), jnp.where(first_head, zero, v)], axis=0)

    def join_heads(v):
        return jnp.where(first_head, v[:ROWS], v[ROWS:])

    def window(m, j, c):
        return kv[m, pl.ds(j, 3), :, c : c + 128].reshape(WIN, 128)

    def attend(i, carry):
        m, j = near_last(i)
        b = m * FD + j
        for k in range(MB):

            @pl.when(i == NB - MB + k)
            def _():
                halos[k].wait()

        if fused:
            when(
                i,
                {
                    1: lambda: x.gather_2("out", sources["out"]),
                    2: lambda: (x.gather_2("up", sources["up"]), x.gather_3("out")),
                    4: lambda: (x.gather_2("down", sources["down"]), x.gather_3("up")),
                    6: lambda: x.gather_3("down"),
                },
            )
        frame = FD * tm + j
        length = length_of(m)
        key_frame = frame - 1 + slot
        allowed = ((key_frame >= 0) & (key_frame < length)) | (frame >= length)
        bias = jnp.where(allowed & key_real, 0.0, NEG)
        for p in range(3):
            c = 128 * p
            s = contract(stack_heads(r.qs[b, :, c : c + 128]), window(m, j, c), 1, 1) + bias
            e = jnp.exp(s - jnp.max(s, axis=-1, keepdims=True))
            pr = (e * (1.0 / jnp.sum(e, axis=-1, keepdims=True))).astype(bf16)
            r.probs[b, p] = pr
            r.os[b, :, c : c + 128] = join_heads(contract(pr, window(m, j, D + c), 1, 0)).astype(bf16)
        return carry

    lax.fori_loop(0, NB, attend, 0)

    if fused:
        for name in ("out", "up", "down"):
            x.gather_4(name)
        settle("out", place(r.wout, 0))
        settle("up", place(r.wup, 0))

    def down():
        return (r.whole["down"] if fused else r.wdown)[...].reshape(FF, D)

    def clear(*keys):
        for name in keys:
            r.acc[name][...] = jnp.zeros_like(r.acc[name])

    def gather_grad(name, value):
        acc = r.acc[name]
        acc[...] += value.reshape(acc.shape)

    clear("out", "up", "down")
    gsm, gbup = r.gsm, r.gbup
    gsm[...] = jnp.zeros_like(gsm)
    gbup[...] = jnp.zeros_like(gbup)

    def feed(b, carry):
        m = b // FD
        j = b - m * FD
        valid = row_ok * valid_of(m, j)
        o = r.os[b]
        x1 = r.x0s[b] + contract(o, r.wout[...], 1, 0) + table[13:14, :]
        xhat, rstd = norm_stats(x1)
        a2 = (xhat * table[14:15, :] + table[15:16, :]).astype(bf16)
        u = contract(a2, r.wup[...], 1, 0) + r.bup[...]
        cdf = 0.5 + 0.5 * lax.erf(u * (1.0 / math.sqrt(2.0)))
        pdf = jnp.exp(u * u * -0.5) * (1.0 / math.sqrt(2.0 * math.pi))
        z = (u * cdf).astype(bf16)
        slope = cdf + u * pdf
        x2 = x1 + contract(z, down(), 1, 0) + table[16:17, :]
        y = (x2 * valid)[:FT].astype(bf16)
        for k in range(FD):

            @pl.when(j == k)
            def _():
                raw[m, FT * k : FT * (k + 1), :] = y

        g2 = r.tops[b]
        gu = (contract(g2, down(), 1, 1) * slope).astype(bf16)
        gbup[...] += col_sum(gu)
        gsm[16:17, :] += col_sum(g2)
        gather_grad("down", contract(z, g2, 0, 0))
        gather_grad("up", contract(a2, gu, 0, 0))
        ga2 = contract(gu, r.wup[...], 1, 1)
        gsm[14:15, :] += col_sum(ga2 * xhat)
        gsm[15:16, :] += col_sum(ga2)
        gx1 = g2.astype(f32) + norm_back(ga2, xhat, rstd, table[14:15, :])
        r.gx1s[b] = gx1
        gy = gx1.astype(bf16)
        gsm[13:14, :] += col_sum(gy)
        gather_grad("out", contract(o, gy, 0, 0))
        r.tops[b] = contract(gy, r.wout[...], 1, 1).astype(bf16)
        return carry

    lax.fori_loop(0, NB, feed, 0)

    store_out = pltpu.make_async_copy(raw, r.block_output, r.local_sem.at[0])
    store_out.start()
    if fused:
        for name in ("down", "up", "out"):
            x.sum_1(name)

    gkv = r.gkv
    backs = [
        pltpu.make_async_remote_copy(
            src_ref=r.back_out.at[m], dst_ref=r.back_in.at[m],
            send_sem=r.back_sem.at[0, m], recv_sem=r.back_sem.at[1, m], device_id=peer, device_id_type=MESH,
        )
        for m in range(MB)
    ]
    near = FD - (FD - 1) * tm
    away = (FD + 1) * (1 - tm)

    def attend_back(i, carry):
        m, j = near_first(i)
        b = m * FD + j
        if fused:
            when(
                i,
                {
                    1: lambda: x.sum_2("down"),
                    2: lambda: x.sum_2("up"),
                    3: lambda: (x.sum_2("out"), x.sum_3("down")),
                    5: lambda: x.sum_3("up"),
                    6: lambda: (x.sum_3("out"), x.sum_4("down")),
                    7: lambda: x.sum_4("up"),
                },
            )
        for k in range(MB):

            @pl.when(i == FD * k)
            def _():
                gkv[...] = jnp.zeros_like(gkv)

        for p in range(3):
            c = 128 * p
            q = stack_heads(r.qs[b, :, c : c + 128])
            o = r.os[b, :, c : c + 128].astype(f32)
            go = stack_heads(r.tops[b, :, c : c + 128])
            delta = jnp.sum(go.astype(f32) * jnp.concatenate([o, o], axis=0), axis=-1, keepdims=True)
            pr = r.probs[b, p]
            gs = (pr.astype(f32) * (contract(go, window(m, j, D + c), 1, 1) - delta)).astype(bf16)
            gv = jnp.transpose(contract(go, pr, 0, 0)).reshape(3, ROWS, 128)
            gk = jnp.transpose(contract(q, gs, 0, 0)).reshape(3, ROWS, 128)
            gkv[pl.ds(j, 3), :, c : c + 128] += gk
            gkv[pl.ds(j, 3), :, D + c : D + c + 128] += gv
            gq = join_heads(contract(gs, window(m, j, c), 1, 0))
            r.qs[b, :, c : c + 128] = (gq * 0.125).astype(bf16)
        for k in range(MB):

            @pl.when(i == FD * k)
            def _():
                r.back_out[k] = gkv[away].astype(bf16)
                backs[k].start()

            @pl.when(i == FD * k + FD - 1)
            def _():
                backs[k].wait()
                gkv[near] += r.back_in[k].astype(f32)
                kv[k, 1 : FD + 1] = gkv[1 : FD + 1].astype(bf16)

        return carry

    lax.fori_loop(0, NB, attend_back, 0)

    clear("q", "k", "v")

    def project_grad(b, carry):
        m = b // FD
        j = b - m * FD
        xhat, _ = norm_stats(r.x0s[b])
        a1 = (xhat * table[9:10, :] + table[10:11, :]).astype(bf16)
        gather_grad("k", contract(a1, kv[m, j + 1, :, :D], 0, 0))
        gather_grad("v", contract(a1, kv[m, j + 1, :, D:], 0, 0))
        gather_grad("q", contract(a1, r.qs[b], 0, 0))
        return carry

    lax.fori_loop(0, NB, project_grad, 0)
    store_out.wait()
    if fused:
        for name in ("k", "v", "q"):
            x.sum_1(name)

    def finish(b, carry):
        m = b // FD
        j = b - m * FD
        if fused:
            when(
                b,
                {
                    1: lambda: x.sum_4("out"),
                    3: lambda: x.sum_2("k"),
                    4: lambda: x.sum_2("v"),
                    5: lambda: x.sum_2("q"),
                },
            )
        xhat, rstd = norm_stats(r.x0s[b])
        gp = jnp.concatenate([r.qs[b], kv[m, j + 1]], axis=1)
        gsm[11:12, :] += col_sum(gp[:, :D])
        gsm[12:13, :] += col_sum(gp[:, 2 * D :])
        ga1 = contract(gp, r.wqkv[...], 1, 1)
        gsm[9:10, :] += col_sum(ga1 * xhat)
        gsm[10:11, :] += col_sum(ga1)
        gb = (r.gx1s[b] + norm_back(ga1, xhat, rstd, table[9:10, :])) * (row_ok * valid_of(m, j))
        column = jnp.zeros((ROWS, 1), f32)
        for k in range(NB):
            column = jnp.where(b == k, r.flag_cols[:ROWS, k : k + 1], column)
        masked = column > 0.5
        gsm[0:1, :] += col_sum(jnp.where(masked, gb, 0.0))
        gsm[SPACE : SPACE + ROWS, :] += gb
        r.sumgb[pl.ds(b, 1), :] = col_sum(gb)
        seen = jnp.where(masked, 0.0, gb)[:FT]
        for k in range(FD):

            @pl.when(j == k)
            def _():
                r.gvis[m, FT * k : FT * (k + 1), :] = seen

        return carry

    lax.fori_loop(0, NB, finish, 0)

    store_seen = pltpu.make_async_copy(r.gvis, r.grad_visible, r.local_sem.at[0])
    store_seen.start()
    blend = time_weights((8, NB), 1, tm, lengths)
    total = jnp.zeros((8, D), f32)
    for b in range(NB):
        total = total + blend[:, b : b + 1] * r.sumgb[b : b + 1, :]
    gsm[1:9, :] = total
    if not fused:
        store_seen.wait()
        return

    expand = spread(128, 512).astype(bf16)
    for k in range(3):
        four = every_fourth(gbup[:, 512 * k : 512 * (k + 1)], 512).astype(bf16)
        gsm[UPB : UPB + 4, 128 * k : 128 * (k + 1)] = contract(four, expand, 1, 1)[1:5]
    r.acc["small"][...] = jnp.transpose(gsm[...]).reshape(r.acc["small"].shape)
    x.sum_1("small")
    for name in ("k", "v", "q"):
        x.sum_3(name)
    x.sum_2("small")
    r.grad_w_down[...] = x.sum_5("down")
    r.grad_w_up[...] = x.sum_5("up")
    r.grad_w_out[...] = x.sum_5("out")
    for name in ("k", "v", "q"):
        x.sum_4(name)
    x.sum_3("small")
    r.grad_w_qkv[:, D : 2 * D] = x.sum_5("k")
    r.grad_w_qkv[:, 2 * D :] = x.sum_5("v")
    r.grad_w_qkv[:, :D] = x.sum_5("q")
    x.sum_4("small")
    shares = jnp.transpose(x.sum_5("small"))
    for name, at in VECTORS:
        getattr(r, "grad_" + name)[...] = shares[at : at + 1, :].reshape(part)
    r.grad_time_embed[...] = shares[1:9, :]
    r.grad_space_embed[...] = shares[SPACE : SPACE + FT, :]
    four = contract(shares[16:24, :], spread(part, 4 * part), 1, 0, lax.Precision.HIGHEST)
    r.grad_bias_up[...] = jnp.sum(every_fourth(four, 4 * part), axis=0).reshape(4 * part)
    store_seen.wait()
    for name in ITEMS:
        x.gather_sent(name, sources[name])
        x.sum_sent(name)


def call(fused, n, part, inputs, outputs, scratch, arrays):
    smem = pl.BlockSpec(memory_space=pltpu.SMEM)
    vmem = pl.BlockSpec(memory_space=pltpu.VMEM)
    hbm = pl.BlockSpec(memory_space=pl.ANY)
    spec = {"s": smem, "v": vmem, "h": hbm}
    names = list(inputs) + list(outputs) + list(scratch)
    return pl.pallas_call(
        functools.partial(body, names, fused, n, part),
        out_shape=tuple(shape for shape, _ in outputs.values()),
        in_specs=[spec[where] for where in inputs.values()],
        out_specs=tuple(spec[where] for _, where in outputs.values()),
        scratch_shapes=list(scratch.values()),
        compiler_params=pltpu.CompilerParams(
            collective_id=0, has_side_effects=True, vmem_limit_bytes=64 * 2**20 - 2**16
        ),
    )(*arrays)


def common_scratch():
    V, S = pltpu.VMEM, pltpu.SemaphoreType.DMA
    return {
        "raw": V((MB, FD * FT, D), bf16),
        "gvis": V((MB, FD * FT, D), f32),
        "flag_rows": V((NB, 256), f32),
        "flag_cols": V((256, NB), f32),
        "x0s": V((NB, ROWS, D), f32),
        "tops": V((NB, ROWS, D), bf16),
        "qs": V((NB, ROWS, D), bf16),
        "kv": V((MB, FD + 2, ROWS, 2 * D), bf16),
        "probs": V((NB, 3, 2 * ROWS, WIN), bf16),
        "os": V((NB, ROWS, D), bf16),
        "gx1s": V((NB, ROWS, D), f32),
        "gkv": V((FD + 2, ROWS, 2 * D), f32),
        "temporal": V((NB, D), f32),
        "sumgb": V((NB, D), f32),
        "back_out": V((MB, ROWS, 2 * D), bf16),
        "back_in": V((MB, ROWS, 2 * D), bf16),
        "halo_sem": S((2, MB)),
        "back_sem": S((2, MB)),
        "local_sem": S((8,)),
    }


def whole_weights(shards, part):
    s = shards
    column = lambda v: v[:, None]
    small = jnp.concatenate(
        [
            column(s.mask_token), s.time_embed.T, column(s.norm1_gain), column(s.norm1_bias), column(s.bias_query),
            column(s.bias_value), column(s.bias_out), column(s.norm2_gain), column(s.norm2_bias),
            column(s.bias_down), s.bias_up.reshape(part, 4), jnp.zeros((part, SPACE - UPB - 4), bf16),
            s.space_embed.T, jnp.zeros((part, SMALL - SPACE - FT), bf16),
        ],
        axis=1,
    )
    pack = jnp.concatenate([s.w_qkv, s.w_out, s.w_up, s.w_down.reshape(part, FF), small], axis=1)
    return lax.all_gather(pack, "clip", axis=0, tiled=True)


def local(*args):
    keys = (
        "visible", "mask_flags", "frames", "assign", "cotangent", "mask_token", "time_embed", "space_embed",
        "norm1_gain", "norm1_bias", "w_qkv", "bias_query", "bias_value", "w_out", "bias_out", "norm2_gain",
        "norm2_bias", "w_up", "bias_up", "w_down", "bias_down",
    )
    a = SimpleNamespace(**dict(zip(keys, args, strict=True)))
    n = lax.axis_size("clip")
    part = D // n
    V, S, sds = pltpu.VMEM, pltpu.SemaphoreType.DMA, jax.ShapeDtypeStruct
    scratch = common_scratch()
    big = {"block_output": (sds(a.visible.shape, bf16), "h"), "grad_visible": (sds(a.visible.shape, f32), "h")}

    if part % 8 == 0 and n % 4 == 0:
        high = n // 4
        inputs = {key: "v" for key in keys}
        inputs.update(frames="s", assign="s", visible="h", cotangent="h", w_qkv="h", w_out="h", w_up="h", w_down="h")
        outputs = dict(big)
        for key in keys[5:]:
            outputs["grad_" + key] = (sds(getattr(a, key).shape, f32), "v")
        scratch.update(
            {
                "rows": V((SMALL, 128), f32),
                "acc_small_cols": V((D, SMALL), f32),
                "table": V((SMALL, D), f32),
                "bup": V((1, FF), f32),
                "wqkv": V((D, 3 * D), bf16),
                "wout": V((D, D), bf16),
                "wup": V((D, FF), bf16),
                "gsm": V((SMALL, D), f32),
                "gbup": V((1, FF), f32),
            }
        )
        for name, (cols, times) in ITEMS.items():
            rows = times * part
            scratch["whole/" + name] = V((high, 2, 2, rows, cols), bf16)
            scratch["acc/" + name] = V((n, rows, cols), f32)
            scratch["snd/" + name] = V((high, 2, rows, cols), bf16)
            scratch["rcv1/" + name] = V((high, 2, rows, cols), bf16)
            for key in ("snd2/", "rcv2/", "snd3/", "rcv3/"):
                scratch[key + name] = V((high, rows, cols), bf16)
            for key in ("snd4/", "rcv4/"):
                scratch[key + name] = V((rows, cols), bf16)
        count = len(ITEMS)
        for key in ("g2s", "g2r", "g3s", "g3r", "s1s", "s1r", "s2s", "s2r", "s4s", "s4r"):
            scratch[key] = S((count,))
        for key in ("g1s", "g1r", "s3s", "s3r"):
            scratch[key] = S((count, high))
        return call(True, n, part, inputs, outputs, scratch, [getattr(a, key) for key in keys])

    whole = whole_weights(a, part)
    cuts = (0, 3 * D, 4 * D, 4 * D + FF, 4 * D + 2 * FF, 4 * D + 2 * FF + SMALL)
    wqkv, wout, wup, wdown, wsmall = (whole[:, i:j] for i, j in zip(cuts[:-1], cuts[1:]))
    values = {
        "frames": a.frames, "assign": a.assign, "visible": a.visible, "mask_flags": a.mask_flags,
        "cotangent": a.cotangent, "table": wsmall.T.astype(f32),
        "bup": wsmall[:, UPB : UPB + 4].astype(f32).reshape(1, FF),
        "wqkv": wqkv, "wout": wout, "wup": wup, "wdown": wdown.reshape(FF, D),
    }
    inputs = {key: "v" for key in values}
    inputs.update(frames="s", assign="s", visible="h", cotangent="h")
    outputs = dict(big)
    for name, (cols, times) in list(ITEMS.items())[1:]:
        outputs["acc/" + name] = (sds((1, times * D, cols), f32), "v")
    outputs["gsm"] = (sds((SMALL, D), f32), "v")
    outputs["gbup"] = (sds((1, FF), f32), "v")
    out, gvis, gk, gv, gq, gout, gup, gdown, gsm, gbup = call(
        False, n, part, inputs, outputs, scratch, list(values.values())
    )
    gsmall = gsm.T.at[:, UPB : UPB + 4].set(gbup.reshape(D, 4))
    grads = jnp.concatenate([gq[0], gk[0], gv[0], gout[0], gup[0], gdown.reshape(D, FF), gsmall], axis=1)
    share = lax.psum_scatter(grads, "clip", scatter_dimension=0, tiled=True)
    share = lax.psum(share.astype(bf16), "tm").astype(f32)
    sqkv, sout, sup, sdown, ssmall = (share[:, i:j] for i, j in zip(cuts[:-1], cuts[1:]))
    return (
        out, gvis, ssmall[:, 0], ssmall[:, 1:9].T, ssmall[:, SPACE : SPACE + FT].T, ssmall[:, 9], ssmall[:, 10],
        sqkv, ssmall[:, 11], ssmall[:, 12], sout, ssmall[:, 13], ssmall[:, 14], ssmall[:, 15], sup,
        ssmall[:, UPB : UPB + 4].reshape(-1), sdown.reshape(-1, D), ssmall[:, 16],
    )


def solution(mesh):
    rows = P(None, ("clip", "tm"), None)
    vec = P("clip")
    mat = P("clip", None)
    cols = P(None, "clip")
    in_specs = (
        rows, P(None, ("clip", "tm")), P(), cols, rows,
        vec, cols, cols, vec, vec, mat, vec, vec, mat, vec, vec, vec, mat, vec, mat, vec,
    )
    out_specs = (
        rows, rows, vec, cols, cols, vec, vec, mat, vec, vec, mat, vec, vec, vec, mat, vec, mat, vec,
    )
    return jax.shard_map(local, mesh=mesh, in_specs=in_specs, out_specs=out_specs, check_vma=False)
```

```python
import functools
import math
from types import SimpleNamespace

import jax
import jax.numpy as jnp
from jax import lax
from jax.experimental import pallas as pl
from jax.experimental.pallas import tpu as pltpu
from jax.sharding import PartitionSpec as P

D = 384
FF = 1536
FT = 196
FD = 4
MB = 2
NB = MB * FD
ROWS = 208
BOTH = MB * ROWS
WIN = 3 * ROWS
EPS = 1e-06
NEG = -1000000000.0
PAIRS = 3
PW = 128
SMALL = 256
TIME = 208
VEC = 216
UPB = 225
MESH = pl.DeviceIdType.MESH
f32 = jnp.float32
bf16 = jnp.bfloat16

ARRAYS = {"small": (SMALL, 1), "p0": (D, 1), "p1": (D, 1), "p2": (D, 1), "out": (D, 1), "up": (FF, 1), "down": (D, 4)}
ITEMS = {
    "small": ("small", None, None), "p0": ("p0", None, None), "p1": ("p1", None, None), "p2": ("p2", None, None),
    "out": ("out", None, None), "up0": ("up", None, 0), "up1": ("up", None, 1), "down0": ("down", 0, None),
    "down1": ("down", 1, None),
}
INDEX = {name: i for i, name in enumerate(ITEMS)}
HIDDEN = 384
CHUNKS = FF // HIDDEN
VECTORS = (
    "mask_token", "norm1_gain", "norm1_bias", "bias_query", "bias_value", "bias_out", "norm2_gain", "norm2_bias",
    "bias_down",
)
AT = {name: VEC + i for i, name in enumerate(VECTORS)}


def contract(a, b, ca, cb, precision=None):
    return lax.dot_general(
        a, b, (((ca,), (cb,)), ((), ())), preferred_element_type=f32, precision=precision
    )


def norm_stats(x):
    c = x - jnp.mean(x, axis=-1, keepdims=True)
    r = lax.rsqrt(jnp.mean(c * c, axis=-1, keepdims=True) + EPS)
    return c * r, r


def norm_back(g, xhat, r, gain):
    d = g * gain
    first = jnp.mean(d, axis=-1, keepdims=True)
    second = jnp.mean(d * xhat, axis=-1, keepdims=True)
    return r * (d - first - xhat * second)


def col_sum(x):
    return jnp.sum(x.astype(f32), axis=0, keepdims=True)


def iota(shape, dim):
    return lax.broadcasted_iota(jnp.int32, shape, dim)


def time_weights(shape, frame_dim, tm, lengths):
    block = iota(shape, frame_dim)
    row = iota(shape, 1 - frame_dim).astype(f32)
    length = jnp.where(block < FD, lengths[0].astype(f32), lengths[1].astype(f32))
    frame = (jnp.where(block < FD, block, block - FD) + FD * tm).astype(f32)
    den = jnp.maximum(length - 1.0, 1.0)
    num = frame * 7.0
    whole = jnp.floor((num + 0.5) / den)
    low = jnp.minimum(whole, 7.0)
    high = jnp.minimum(low + 1.0, 7.0)
    part = (num - whole * den) / den
    return jnp.where(row == low, 1.0 - part, 0.0) + jnp.where(row == high, part, 0.0)


def spread(rows, cols):
    return (iota((rows, cols), 1) // 4 == iota((rows, cols), 0)).astype(f32)


def every_fourth(x, cols):
    return jnp.where(iota((8, cols), 0) == 1 + iota((8, cols), 1) % 4, x, 0.0)


def half(length, which):
    return slice(0, length) if which is None else slice(which * length // 2, (which + 1) * length // 2)


def item_shape(name, part):
    array, rows, cols = ITEMS[name]
    width, times = ARRAYS[array]
    return times * part // (1 if rows is None else 2), width // (1 if cols is None else 2)


class Exchange:
    def __init__(self, r, n, part):
        self.r, self.high, self.part = r, n // 4, part
        me = lax.axis_index("clip")
        self.tm = lax.axis_index("tm")
        self.h, self.mid, self.lo = me // 4, (me // 2) % 2, me % 2

    def device(self, h, mid, lo):
        return {"clip": (h * 2 + mid) * 2 + lo}

    def others(self):
        return [(self.h + d) % self.high for d in range(1, self.high)]

    def greet(self):
        barrier = pltpu.get_barrier_semaphore()
        peers = [self.device(h, self.mid, self.lo) for h in self.others()]
        peers += [self.device(self.h, 1 - self.mid, self.lo), self.device(self.h, self.mid, 1 - self.lo)]
        peers.append({"tm": 1 - self.tm})
        for peer in peers:
            pl.semaphore_signal(barrier, inc=1, device_id=peer, device_id_type=MESH)
        pl.semaphore_wait(barrier, len(peers))

    def copy(self, src, dst, send, recv, device):
        return pltpu.make_async_remote_copy(
            src_ref=src, dst_ref=dst, send_sem=send, recv_sem=recv, device_id=device, device_id_type=MESH
        )

    def cut(self, name):
        array, rows, cols = ITEMS[name]
        width, times = ARRAYS[array]
        return half(times * self.part, rows), half(width, cols)

    def g1(self, name, sender, d, h):
        r, i = self.r, INDEX[name]
        rows, cols = self.cut(name)
        slot = r.whole[ITEMS[name][0]].at[sender, self.mid, self.lo, rows, cols]
        return self.copy(slot, slot, r.g1s.at[i, d], r.g1r.at[i, sender], self.device(h, self.mid, self.lo))

    def g2(self, name, mid):
        r, i = self.r, INDEX[name]
        rows, cols = self.cut(name)
        part = r.whole[ITEMS[name][0]].at[:, mid, self.lo, rows, cols]
        return self.copy(part, part, r.g2s.at[i], r.g2r.at[i], self.device(self.h, 1 - self.mid, self.lo))

    def g3(self, name, lo):
        r, i = self.r, INDEX[name]
        rows, cols = self.cut(name)
        part = r.whole[ITEMS[name][0]].at[:, :, lo, rows, cols]
        return self.copy(part, part, r.g3s.at[i], r.g3r.at[i], self.device(self.h, self.mid, 1 - self.lo))

    def gather_1(self, name):
        for d, h in enumerate(self.others()):
            self.g1(name, self.h, d, h).start()

    def gather_2(self, name):
        for d, h in enumerate(self.others()):
            self.g1(name, h, d, h).wait_recv()
        self.g2(name, self.mid).start()

    def gather_3(self, name):
        self.g2(name, 1 - self.mid).wait_recv()
        self.g3(name, self.lo).start()

    def gather_4(self, name):
        self.g3(name, 1 - self.lo).wait_recv()

    def gather_sent(self, name):
        for d, h in enumerate(self.others()):
            self.g1(name, self.h, d, h).wait_send()
        self.g2(name, self.mid).wait_send()
        self.g3(name, self.lo).wait_send()

    def acc(self, name, h, mid, lo):
        rows, cols = self.cut(name)
        return self.r.acc[ITEMS[name][0]].at[(h * 2 + mid) * 2 + lo, rows, cols]

    def own(self, name, h, mid):
        return self.acc(name, h, mid, self.lo)

    def s1(self, name):
        r, i = self.r, INDEX[name]
        return self.copy(
            r.snd[name], r.rcv1[name], r.s1s.at[i], r.s1r.at[i], self.device(self.h, self.mid, 1 - self.lo)
        )

    def s2(self, name):
        r, i = self.r, INDEX[name]
        return self.copy(
            r.snd[name].at[0], r.rcv2[name], r.s2s.at[i], r.s2r.at[i], self.device(self.h, 1 - self.mid, self.lo)
        )

    def s3(self, name, h, slot, d):
        r, i = self.r, INDEX[name]
        return self.copy(
            r.snd[name].at[1, h], r.rcv3[name].at[slot], r.s3s.at[i, d], r.s3r.at[i, slot],
            self.device(h, self.mid, self.lo),
        )

    def s4(self, name):
        r, i = self.r, INDEX[name]
        return self.copy(r.snd4[name], r.rcv4[name], r.s4s.at[i], r.s4r.at[i], {"tm": 1 - self.tm})

    def sum_1(self, name):
        for h in range(self.high):
            for mid in range(2):
                self.r.snd[name][mid, h] = self.acc(name, h, mid, 1 - self.lo)[...].astype(bf16)
        self.s1(name).start()

    def sum_2(self, name):
        r = self.r
        self.s1(name).wait()
        for h in range(self.high):
            value = self.own(name, h, 1 - self.mid)[...] + r.rcv1[name][1 - self.mid, h].astype(f32)
            r.snd[name][0, h] = value.astype(bf16)
        self.s2(name).start()
        for h in range(self.high):
            self.own(name, h, self.mid)[...] += r.rcv1[name][self.mid, h].astype(f32)

    def sum_3(self, name):
        r = self.r
        self.s2(name).wait_recv()
        for d, h in enumerate(self.others()):
            value = self.own(name, h, self.mid)[...] + r.rcv2[name][h].astype(f32)
            r.snd[name][1, h] = value.astype(bf16)
            self.s3(name, h, self.h, d).start()

    def sum_4(self, name):
        r = self.r
        total = self.own(name, self.h, self.mid)[...] + r.rcv2[name][self.h].astype(f32)
        for d, h in enumerate(self.others()):
            self.s3(name, h, h, d).wait_recv()
            total = total + r.rcv3[name][h].astype(f32)
        r.snd4[name][...] = total.astype(bf16)
        self.s4(name).start()

    def sum_5(self, name):
        r = self.r
        self.s4(name).wait_recv()
        return r.snd4[name][...].astype(f32) + r.rcv4[name][...].astype(f32)

    def sum_sent(self, name):
        self.s2(name).wait_send()
        for d, h in enumerate(self.others()):
            self.s3(name, h, self.h, d).wait_send()
        self.s4(name).wait_send()


def body(names, fused, n, part, *refs):
    r = SimpleNamespace()
    for key, ref in zip(names, refs, strict=True):
        if "/" in key:
            group, item = key.split("/")
            if not hasattr(r, group):
                setattr(r, group, {})
            getattr(r, group)[item] = ref
        else:
            setattr(r, key, ref)
    tm = lax.axis_index("tm")
    peer = {"tm": 1 - tm}
    table, raw = r.table, r.raw

    lengths = [r.frames[r.assign[m]] for m in range(MB)]
    first_head = iota((1, PW), 1) < 64
    row_ok = (iota((ROWS, 1), 0) < FT).astype(f32)
    pad = jnp.zeros((ROWS - FT, D), f32)

    def vector(name):
        return table[AT[name] : AT[name] + 1, :]

    def valid_of(m, j):
        return jnp.where(FD * tm + j < lengths[m], 1.0, 0.0).astype(f32)

    def valid_rows(j):
        return jnp.concatenate([row_ok * valid_of(m, j) for m in range(MB)], axis=0)

    def near_last(jj):
        return jj + tm * (FD - 1 - 2 * jj)

    def span(m):
        return slice(ROWS * m, ROWS * (m + 1))

    def steps_at(steps, t):
        if fused and t in steps:
            for stage, item in steps[t]:
                getattr(x, stage)(item)

    load_seen = pltpu.make_async_copy(r.visible, raw, r.local_sem.at[0])
    load_top = pltpu.make_async_copy(r.cotangent, raw, r.local_sem.at[0])
    if fused:
        x = Exchange(r, n, part)
        h, mid, lo = x.h, x.mid, x.lo
        loads = []
        for p in range(PAIRS):
            for t in range(3):
                c = D * t + PW * p
                loads.append((r.w_qkv.at[:, c : c + PW], r.whole["p%d" % p].at[h, mid, lo, :, PW * t : PW * (t + 1)]))
        for name in ("out", "up", "down"):
            loads.append((getattr(r, "w_" + name), r.whole[name].at[h, mid, lo]))
        loads = [pltpu.make_async_copy(src, dst, r.local_sem.at[1 + i]) for i, (src, dst) in enumerate(loads)]
        for load in loads:
            load.start()
        load_seen.start()
        r.rows[...] = jnp.zeros_like(r.rows)
        r.rows[0:8, :part] = r.time_embed[...].astype(f32)
        for i, name in enumerate(VECTORS):
            r.rows[8 + i : 9 + i, :part] = getattr(r, name)[...].astype(f32).reshape(1, part)
        up = every_fourth(r.bias_up[...].astype(f32).reshape(1, 4 * part), 4 * part)
        up = contract(up.astype(bf16), spread(part, 4 * part).astype(bf16), 1, 1)
        r.rows[UPB - TIME : UPB - TIME + 4, :part] = up[1:5]
        r.cols[...] = jnp.zeros_like(r.cols)
        r.cols[:, :FT] = r.space_embed[...].astype(f32)
        r.cols[:, TIME : TIME + 32] = jnp.transpose(r.rows[...])[:part]
        r.whole["small"][h, mid, lo] = r.cols[...].astype(bf16)
        x.greet()
        x.gather_1("small")
        for load in loads:
            load.wait()
        x.gather_1("p0")
    else:
        load_seen.start()
        barrier = pltpu.get_barrier_semaphore()
        pl.semaphore_signal(barrier, inc=1, device_id=peer, device_id_type=MESH)
        pl.semaphore_wait(barrier, 1)

    flags = r.mask_flags[...].astype(f32)
    r.flag_rows[...] = jnp.zeros_like(r.flag_rows)
    for m in range(MB):
        for j in range(FD):
            r.flag_rows[j : j + 1, ROWS * m : ROWS * m + FT] = flags[m : m + 1, FT * j : FT * (j + 1)]
    r.flag_cols[...] = jnp.transpose(r.flag_rows[...])

    def unpack(m, j):
        return jnp.concatenate([raw[m, FT * j : FT * (j + 1), :].astype(f32), pad], axis=0)

    load_seen.wait()
    for m in range(MB):
        for j in range(FD):
            r.x0s[j, span(m)] = unpack(m, j)
    load_top.start()

    def clear(*keys):
        for name in keys:
            r.acc[name][...] = jnp.zeros_like(r.acc[name])

    clear("out", "up", "down")
    gsm, gbup, qkv = r.gsm, r.gbup, r.qkv
    gsm[...] = jnp.zeros_like(gsm)
    gbup[...] = jnp.zeros_like(gbup)
    for m in range(MB):
        qkv[(FD + 1) * tm, m] = jnp.zeros((ROWS, 3 * D), bf16)

    def settle(name, target):
        whole = r.whole[name]
        for i in range(n // 2):
            two = jnp.concatenate([whole[i // 2, i % 2, 0].astype(f32), whole[i // 2, i % 2, 1].astype(f32)], axis=0)
            target(slice(2 * part * i, 2 * part * (i + 1)), two)

    def place(ref, start):
        def put(rows, value):
            ref[rows, start : start + value.shape[1]] = value.astype(ref.dtype)

        return put

    if fused:
        x.gather_2("small")
        x.gather_2("p0")
        x.gather_1("p1")
        x.gather_1("p2")
        x.gather_3("small")
        x.gather_3("p0")

    load_top.wait()
    for m in range(MB):
        for j in range(FD):
            r.tops[j, span(m)] = (unpack(m, j) * (row_ok * valid_of(m, j))).astype(bf16)

    if fused:
        x.gather_4("small")
        held = r.acc["small"]

        def hold(rows, value):
            held[rows.start // part : rows.stop // part] = value.reshape(2, part, SMALL)

        settle("small", hold)
        table[...] = jnp.transpose(held[...].reshape(D, SMALL))
        expand = spread(PW, 4 * PW).astype(bf16)
        for k in range(3):
            four = contract(table[UPB - 1 : UPB + 7, PW * k : PW * (k + 1)].astype(bf16), expand, 1, 0)
            r.bup[:, 4 * PW * k : 4 * PW * (k + 1)] = jnp.sum(every_fourth(four, 4 * PW), axis=0, keepdims=True)

    blend = time_weights((NB, 8), 0, tm, lengths)
    total = jnp.zeros((NB, D), f32)
    for t in range(8):
        total = total + blend[:, t : t + 1] * table[TIME + t : TIME + t + 1, :]
    r.temporal[...] = total
    for j in range(FD):
        for m in range(MB):
            b = m * FD + j
            base = jnp.where(r.flag_cols[span(m), j : j + 1] > 0.5, vector("mask_token"), r.x0s[j, span(m)])
            base = base + r.temporal[b : b + 1, :] + table[:ROWS, :]
            x0 = base * (row_ok * valid_of(m, j))
            r.x0s[j, span(m)] = x0
            xhat, _ = norm_stats(x0)
            r.a1s[j, span(m)] = (xhat * vector("norm1_gain") + vector("norm1_bias")).astype(bf16)

    key = iota((1, WIN), 1)
    slot = (key >= ROWS).astype(jnp.int32) + (key >= 2 * ROWS).astype(jnp.int32)
    key_real = key - slot * ROWS < FT
    ones = jnp.ones((WIN, PW), bf16)

    def stack_heads(v):
        zero = jnp.zeros_like(v)
        return jnp.concatenate([jnp.where(first_head, v, zero), jnp.where(first_head, zero, v)], axis=0)

    def join_heads(v):
        return jnp.where(first_head, v[:ROWS], v[ROWS:])

    def window(m, j, c):
        return qkv[pl.ds(j, 3), m, :, c : c + PW].reshape(WIN, PW)

    def halo(p):
        cols = slice(D * p + PW, D * (p + 1))
        return pltpu.make_async_remote_copy(
            src_ref=qkv.at[FD - (FD - 1) * tm, :, :, cols], dst_ref=qkv.at[(FD + 1) * tm, :, :, cols],
            send_sem=r.halo_sem.at[0, p], recv_sem=r.halo_sem.at[1, p], device_id=peer, device_id_type=MESH,
        )

    def project(p):
        q0 = D * p
        cols = slice(PW * p, PW * (p + 1))
        for jj in range(FD):
            j = near_last(FD - 1 - jj)
            y = contract(r.a1s[j], r.wqkv[:, q0 : q0 + D], 1, 0)
            q = (y[:, :PW] + vector("bias_query")[:, cols]).astype(bf16).astype(f32)
            v = y[:, 2 * PW :] + vector("bias_value")[:, cols]
            for m in range(MB):
                qkv[j + 1, m, :, q0 : q0 + PW] = (q[span(m)] * 0.125).astype(bf16)
                qkv[j + 1, m, :, q0 + PW : q0 + 2 * PW] = y[span(m), PW : 2 * PW].astype(bf16)
                qkv[j + 1, m, :, q0 + 2 * PW : q0 + D] = v[span(m)].astype(bf16)
            if jj == 0:
                halo(p).start()

    def attend(p, probs, scale, steps):
        q0 = D * p
        order = [(jj, m) for jj in range(FD) for m in range(MB)]
        scores, biases = {}, {}
        for t in range(NB + 2):
            steps_at(steps, t)
            if t < NB:
                jj, m = order[t]
                j = near_last(jj)
                if t == NB - MB:
                    halo(p).wait()
                frame = FD * tm + j
                key_frame = frame - 1 + slot
                allowed = ((key_frame >= 0) & (key_frame < lengths[m])) | (frame >= lengths[m])
                bias = jnp.where(allowed & key_real, 0.0, NEG)
                q = stack_heads(qkv[j + 1, m, :, q0 : q0 + PW])
                scores[t] = contract(q, window(m, j, q0 + PW), 1, 1) + bias
            if 0 <= t - 1 < NB:
                jj, m = order[t - 1]
                s = scores.pop(t - 1)
                e = jnp.exp(s - jnp.max(s, axis=-1, keepdims=True))
                probs[p, near_last(jj), m] = e.astype(bf16)
            if 0 <= t - 2 < NB:
                jj, m = order[t - 2]
                j = near_last(jj)
                values = jnp.concatenate([window(m, j, q0 + 2 * PW), ones], axis=1)
                both = contract(probs[p, j, m], values, 1, 0)
                inverse = 1.0 / join_heads(both[:, PW:])
                o = join_heads(both[:, :PW]) * inverse
                r.os[j, span(m), PW * p : PW * (p + 1)] = o
                scale[j, span(m), PW * p : PW * (p + 1)] = inverse

    forward_steps = [
        {
            0: [("gather_2", "p1"), ("gather_2", "p2"), ("gather_1", "out"), ("gather_1", "up0")],
            3: [("gather_3", "p1"), ("gather_3", "p2"), ("gather_1", "up1"), ("gather_1", "down0")],
            6: [("gather_2", "out"), ("gather_1", "down1")],
        },
        {
            1: [("gather_2", "up0"), ("gather_3", "out")],
            6: [("gather_2", "up1"), ("gather_3", "up0")],
        },
        {
            3: [("gather_2", "down0"), ("gather_3", "up1")],
            8: [("gather_2", "down1"), ("gather_3", "down0")],
        },
    ]

    def down(c):
        if not fused:
            return r.wdown[HIDDEN * c : HIDDEN * (c + 1), :]
        each = n // 4 // CHUNKS
        return r.whole["down"][each * c : each * (c + 1)].reshape(HIDDEN, D)

    def add_grad(name, value, c=None):
        acc = r.acc[name]
        if name == "up":
            acc[:, :, HIDDEN * c : HIDDEN * (c + 1)] += value.reshape(acc.shape[0], acc.shape[1], HIDDEN)
        elif name == "down":
            if fused:
                each = n // CHUNKS
                acc[each * c : each * (c + 1)] += value.reshape(each, acc.shape[1], D)
            else:
                acc[0, HIDDEN * c : HIDDEN * (c + 1)] += value
        else:
            acc[...] += value.reshape(acc.shape)

    def small_grad(name, value):
        gsm[AT[name] : AT[name] + 1, :] += col_sum(value)

    def feed(scale, j):
        valid = valid_rows(j)
        o = r.os[j].astype(bf16)
        x1 = r.x0s[j] + contract(o, r.wout[...], 1, 0) + vector("bias_out")
        xhat, rstd = norm_stats(x1)
        a2 = (xhat * vector("norm2_gain") + vector("norm2_bias")).astype(bf16)
        g2 = r.tops[j]

        def products(c):
            cols = slice(HIDDEN * c, HIDDEN * (c + 1))
            return contract(a2, r.wup[:, cols], 1, 0) + r.bup[:, cols], contract(g2, down(c), 1, 1)

        x2 = x1 + vector("bias_down")
        ga2 = jnp.zeros((BOTH, D), f32)
        ready = products(0)
        for c in range(CHUNKS):
            cols = slice(HIDDEN * c, HIDDEN * (c + 1))
            u, gz = ready
            if c + 1 < CHUNKS:
                ready = products(c + 1)
            cdf = 0.5 + 0.5 * lax.erf(u * (1.0 / math.sqrt(2.0)))
            pdf = jnp.exp(u * u * -0.5) * (1.0 / math.sqrt(2.0 * math.pi))
            z = (u * cdf).astype(bf16)
            gu = (gz * (cdf + u * pdf)).astype(bf16)
            gbup[:, cols] += col_sum(gu)
            x2 = x2 + contract(z, down(c), 1, 0)
            ga2 = ga2 + contract(gu, r.wup[:, cols], 1, 1)
            add_grad("down", contract(z, g2, 0, 0), c)
            add_grad("up", contract(a2, gu, 0, 0), c)
        y = (x2 * valid).astype(bf16)
        for k in range(FD):

            @pl.when(j == k)
            def _():
                for m in range(MB):
                    raw[m, FT * k : FT * (k + 1), :] = y[ROWS * m : ROWS * m + FT]

        small_grad("bias_down", g2)
        small_grad("norm2_gain", ga2 * xhat)
        small_grad("norm2_bias", ga2)
        gx1 = g2.astype(f32) + norm_back(ga2, xhat, rstd, vector("norm2_gain"))
        gy = gx1.astype(bf16)
        small_grad("bias_out", gy)
        add_grad("out", contract(o, gy, 0, 0))
        go = contract(gy, r.wout[...], 1, 1).astype(bf16).astype(f32)
        r.tops[j] = (go * scale[j]).astype(bf16)
        r.gx1s[j] = gx1

    gkv = r.gkv
    near = FD - (FD - 1) * tm
    away = (FD + 1) * (1 - tm)

    def back(p):
        return pltpu.make_async_remote_copy(
            src_ref=r.back_out, dst_ref=r.back_in.at[p % 2],
            send_sem=r.back_sem.at[0, p], recv_sem=r.back_sem.at[1, p], device_id=peer, device_id_type=MESH,
        )

    def attend_back(p, probs, steps):
        q0 = D * p
        cols = slice(PW * p, PW * (p + 1))
        gkv[...] = jnp.zeros_like(gkv)
        order = [(FD - 1 - jj, m) for jj in range(FD) for m in range(MB)]
        diffs, slopes = {}, {}
        for t in range(NB + 2):
            steps_at(steps, t)
            if t < NB:
                jj, m = order[t]
                j = near_last(jj)
                o = r.os[j, span(m), cols]
                go = stack_heads(r.tops[j, span(m), cols])
                delta = jnp.sum(go.astype(f32) * jnp.concatenate([o, o], axis=0), axis=-1, keepdims=True)
                diffs[t] = contract(go, window(m, j, q0 + 2 * PW), 1, 1) - delta
                gv = jnp.transpose(contract(go, probs[p, j, m], 0, 0)).reshape(3, ROWS, PW)
                gkv[pl.ds(j, 3), m, :, PW:] += gv
            if 0 <= t - 1 < NB:
                jj, m = order[t - 1]
                slopes[t - 1] = (probs[p, near_last(jj), m].astype(f32) * diffs.pop(t - 1)).astype(bf16)
            if 0 <= t - 2 < NB:
                jj, m = order[t - 2]
                j = near_last(jj)
                gs = slopes.pop(t - 2)
                q = stack_heads(qkv[j + 1, m, :, q0 : q0 + PW])
                gk = jnp.transpose(contract(q, gs, 0, 0)).reshape(3, ROWS, PW)
                gkv[pl.ds(j, 3), m, :, :PW] += gk
                gq = join_heads(contract(gs, window(m, j, q0 + PW), 1, 0))
                qkv[j + 1, m, :, q0 : q0 + PW] = (gq * 0.125).astype(bf16)
            if t == MB + 1:
                r.back_out[...] = gkv[away].astype(bf16)
                back(p).start()
        back(p).wait()
        gkv[near] += r.back_in[p % 2].astype(f32)
        qkv[1 : FD + 1, :, :, q0 + PW : q0 + D] = gkv[1 : FD + 1].astype(bf16)
        total = 0.0
        for j in range(FD):
            total = total + contract(r.a1s[j], qkv[j + 1, :, :, q0 : q0 + D].reshape(BOTH, D), 0, 0)
        acc = r.acc["p%d" % p]
        acc[...] = total.reshape(acc.shape)

    backward_steps = [
        {
            0: [("sum_2", "down0")],
            4: [("sum_2", "down1")],
            7: [("sum_3", "down0")],
        },
        {
            0: [("sum_2", "up0")],
            3: [("sum_3", "down1")],
            6: [("sum_2", "up1"), ("sum_3", "up0")],
            8: [("sum_4", "down0")],
        },
        {
            0: [("sum_2", "out"), ("sum_2", "p0")],
            3: [("sum_3", "up1"), ("sum_4", "down1")],
            6: [("sum_3", "out"), ("sum_2", "p1")],
            8: [("sum_4", "up0"), ("sum_3", "p0")],
        },
    ]

    def middle(probs):
        scale = r.gx1s
        for p in range(PAIRS):
            if fused:
                x.gather_4("p%d" % p)
                settle("p%d" % p, place(r.wqkv, D * p))
            project(p)
            attend(p, probs, scale, forward_steps[p])
        if fused:
            x.gather_3("down1")
            for name in ("out", "up0", "up1", "down0", "down1"):
                x.gather_4(name)
            settle("out", place(r.wout, 0))
            settle("up", place(r.wup, 0))

        def feed_step(j, carry):
            feed(scale, j)
            return carry

        lax.fori_loop(0, FD, feed_step, 0)
        pltpu.make_async_copy(raw, r.block_output, r.local_sem.at[0]).start()
        if fused:
            for name in ("down0", "down1", "up0", "up1", "out"):
                x.sum_1(name)
        for p in range(PAIRS):
            attend_back(p, probs, backward_steps[p])
            if fused:
                x.sum_1("p%d" % p)

    pl.run_scoped(middle, pltpu.VMEM((PAIRS, FD, MB, BOTH, WIN), bf16))
    pltpu.make_async_copy(raw, r.block_output, r.local_sem.at[0]).wait()

    final_steps = {
        0: [("sum_2", "p2"), ("sum_4", "up1")],
        1: [("sum_3", "p1"), ("sum_4", "out")],
        2: [("sum_4", "p0")],
        3: [("sum_3", "p2"), ("sum_4", "p1")],
    }

    def last(gvis):
        for j in range(FD):
            steps_at(final_steps, j)
            xhat, rstd = norm_stats(r.x0s[j])
            gp = qkv[j + 1].reshape(BOTH, 3 * D)
            sums = col_sum(gp)
            for p in range(PAIRS):
                cols = slice(PW * p, PW * (p + 1))
                gsm[AT["bias_query"] : AT["bias_query"] + 1, cols] += sums[:, D * p : D * p + PW]
                gsm[AT["bias_value"] : AT["bias_value"] + 1, cols] += sums[:, D * p + 2 * PW : D * (p + 1)]
            ga1 = contract(gp, r.wqkv[...], 1, 1)
            small_grad("norm1_gain", ga1 * xhat)
            small_grad("norm1_bias", ga1)
            gb = (r.gx1s[j] + norm_back(ga1, xhat, rstd, vector("norm1_gain"))) * valid_rows(j)
            masked = r.flag_cols[:BOTH, j : j + 1] > 0.5
            small_grad("mask_token", jnp.where(masked, gb, 0.0))
            seen = jnp.where(masked, 0.0, gb)
            for m in range(MB):
                gsm[:ROWS, :] += gb[span(m)]
                r.sumgb[m * FD + j : m * FD + j + 1, :] = col_sum(gb[span(m)])
                gvis[m, FT * j : FT * (j + 1), :] = seen[ROWS * m : ROWS * m + FT]
        store_seen = pltpu.make_async_copy(gvis, r.grad_visible, r.local_sem.at[0])
        store_seen.start()
        blend = time_weights((8, NB), 1, tm, lengths)
        total = jnp.zeros((8, D), f32)
        for b in range(NB):
            total = total + blend[:, b : b + 1] * r.sumgb[b : b + 1, :]
        gsm[TIME : TIME + 8, :] = total
        if fused:
            expand = spread(PW, 4 * PW).astype(bf16)
            for k in range(3):
                four = every_fourth(gbup[:, 4 * PW * k : 4 * PW * (k + 1)], 4 * PW).astype(bf16)
                gsm[UPB : UPB + 4, PW * k : PW * (k + 1)] = contract(four, expand, 1, 1)[1:5]
            r.acc["small"][...] = jnp.transpose(gsm[...]).reshape(r.acc["small"].shape)
            x.sum_1("small")
            for k in range(2):
                rows, cols = x.cut("down%d" % k)
                r.grad_w_down[rows, cols] = x.sum_5("down%d" % k)
                rows, cols = x.cut("up%d" % k)
                r.grad_w_up[rows, cols] = x.sum_5("up%d" % k)
            r.grad_w_out[...] = x.sum_5("out")
            x.sum_2("small")
            x.sum_4("p2")
            x.sum_3("small")
            for p in range(PAIRS):
                share = x.sum_5("p%d" % p)
                for t in range(3):
                    c = D * t + PW * p
                    r.grad_w_qkv[:, c : c + PW] = share[:, PW * t : PW * (t + 1)]
            x.sum_4("small")
            r.grad_small[...] = x.sum_5("small")
        store_seen.wait()
        if fused:
            for name in ITEMS:
                x.gather_sent(name)
                x.sum_sent(name)

    pl.run_scoped(last, pltpu.VMEM((MB, FD * FT, D), f32))


def unpack_body(names, part, *refs):
    r = SimpleNamespace(**dict(zip(names, refs, strict=True)))
    parts = [(r.out_in.at[m], r.buf_block.at[m], r.block_output.at[m]) for m in range(MB)]
    parts += [
        (r.seen_in.at[m, rows], r.buf_seen.at[m, rows], r.grad_visible.at[m, rows])
        for m in range(MB)
        for rows in (slice(0, FD * FT // 2), slice(FD * FT // 2, FD * FT))
    ]
    parts += [
        (getattr(r, "w_%s_in" % name), getattr(r, "buf_" + name), getattr(r, "grad_w_" + name))
        for name in ("qkv", "out", "up", "down")
    ]
    loads = [pltpu.make_async_copy(src, buf, r.sem.at[0, i]) for i, (src, buf, _) in enumerate(parts)]
    stores = [pltpu.make_async_copy(buf, dst, r.sem.at[1, i]) for i, (_, buf, dst) in enumerate(parts)]
    for load in loads:
        load.start()
    small = r.small_in[...]
    r.grad_space_embed[...] = small[:, :FT]
    r.wide[:part] = small
    rows = jnp.transpose(r.wide[:, PW:])
    r.grad_time_embed[...] = rows[TIME - PW : TIME - PW + 8, :part]
    for name in VECTORS:
        at = AT[name] - PW
        getattr(r, "grad_" + name)[...] = rows[at : at + 1, :part].reshape(part)
    four = rows[UPB - 1 - PW : UPB + 7 - PW, :part]
    four = contract(four, spread(part, 4 * part), 1, 0, lax.Precision.HIGHEST)
    r.grad_bias_up[...] = jnp.sum(every_fourth(four, 4 * part), axis=0).reshape(4 * part)
    for load, store in zip(loads, stores):
        load.wait()
        store.start()
    for store in stores:
        store.wait()


def call(fused, n, part, inputs, outputs, scratch, arrays):
    smem = pl.BlockSpec(memory_space=pltpu.SMEM)
    vmem = pl.BlockSpec(memory_space=pltpu.VMEM)
    hbm = pl.BlockSpec(memory_space=pl.ANY)
    spec = {"s": smem, "v": vmem, "h": hbm}
    names = list(inputs) + list(outputs) + list(scratch)
    return pl.pallas_call(
        functools.partial(body, names, fused, n, part),
        out_shape=tuple(shape for shape, _ in outputs.values()),
        in_specs=[spec[where] for where in inputs.values()],
        out_specs=tuple(spec[where] for _, where in outputs.values()),
        scratch_shapes=list(scratch.values()),
        compiler_params=pltpu.CompilerParams(
            collective_id=0, has_side_effects=True, vmem_limit_bytes=64 * 2**20 - 2**16
        ),
    )(*arrays)


def common_scratch():
    V, S = pltpu.VMEM, pltpu.SemaphoreType.DMA
    return {
        "raw": V((MB, FD * FT, D), bf16),
        "flag_rows": V((8, 512), f32),
        "flag_cols": V((512, 8), f32),
        "x0s": V((FD, BOTH, D), f32),
        "gx1s": V((FD, BOTH, D), f32),
        "tops": V((FD, BOTH, D), bf16),
        "os": V((FD, BOTH, D), f32),
        "a1s": V((FD, BOTH, D), bf16),
        "qkv": V((FD + 2, MB, ROWS, 3 * D), bf16),
        "gkv": V((FD + 2, MB, ROWS, 2 * PW), f32),
        "temporal": V((NB, D), f32),
        "sumgb": V((NB, D), f32),
        "gsm": V((SMALL, D), f32),
        "gbup": V((1, FF), f32),
        "back_out": V((MB, ROWS, 2 * PW), bf16),
        "back_in": V((2, MB, ROWS, 2 * PW), bf16),
        "halo_sem": S((2, PAIRS)),
        "back_sem": S((2, PAIRS)),
        "local_sem": S((16,)),
    }


def whole_weights(shards, part):
    s = shards
    small = jnp.concatenate(
        [s.space_embed.T, jnp.zeros((part, TIME - FT), bf16), s.time_embed.T]
        + [getattr(s, name)[:, None] for name in VECTORS]
        + [s.bias_up.reshape(part, 4), jnp.zeros((part, SMALL - UPB - 4), bf16)],
        axis=1,
    )
    pairs = [s.w_qkv[:, D * t + PW * p : D * t + PW * (p + 1)] for p in range(PAIRS) for t in range(3)]
    pack = jnp.concatenate(pairs + [s.w_out, s.w_up, s.w_down.reshape(part, FF), small], axis=1)
    return lax.all_gather(pack, "clip", axis=0, tiled=True)


def local(*args):
    keys = (
        "visible", "mask_flags", "frames", "assign", "cotangent", "mask_token", "time_embed", "space_embed",
        "norm1_gain", "norm1_bias", "w_qkv", "bias_query", "bias_value", "w_out", "bias_out", "norm2_gain",
        "norm2_bias", "w_up", "bias_up", "w_down", "bias_down",
    )
    a = SimpleNamespace(**dict(zip(keys, args, strict=True)))
    n = lax.axis_size("clip")
    part = D // n
    V, S, sds = pltpu.VMEM, pltpu.SemaphoreType.DMA, jax.ShapeDtypeStruct
    scratch = common_scratch()
    big = {"block_output": (sds(a.visible.shape, bf16), "h"), "grad_visible": (sds(a.visible.shape, f32), "h")}

    if part % 8 == 0 and n % 16 == 0:
        high = n // 4
        a.assign = a.assign.reshape(MB)
        a.space_embed = a.space_embed.T
        inputs = {key: "v" for key in keys}
        inputs.update(frames="s", assign="s", visible="h", cotangent="h", w_qkv="h", w_out="h", w_up="h", w_down="h")
        grads = {"grad_" + key: sds(getattr(a, key).shape, f32) for key in keys[5:]}
        outputs = dict(big)
        for key in ("grad_w_qkv", "grad_w_out", "grad_w_up", "grad_w_down"):
            outputs[key] = (grads[key], "v")
        outputs["grad_small"] = (sds((part, SMALL), f32), "v")
        scratch.update(
            {
                "rows": V((32, PW), f32),
                "cols": V((part, SMALL), f32),
                "table": V((SMALL, D), f32),
                "bup": V((1, FF), f32),
                "wqkv": V((D, 3 * D), bf16),
                "wout": V((D, D), bf16),
                "wup": V((D, FF), bf16),
            }
        )
        for name, (cols, times) in ARRAYS.items():
            scratch["whole/" + name] = V((high, 2, 2, times * part, cols), bf16)
            scratch["acc/" + name] = V((n, times * part, cols), f32)
        for name in ITEMS:
            shape = item_shape(name, part)
            scratch["snd/" + name] = V((2, high, *shape), bf16)
            scratch["rcv1/" + name] = V((2, high, *shape), bf16)
            scratch["rcv2/" + name] = V((high, *shape), bf16)
            scratch["rcv3/" + name] = V((high, *shape), bf16)
            scratch["snd4/" + name] = V(shape, bf16)
            scratch["rcv4/" + name] = V(shape, bf16)
        count = len(ITEMS)
        for key in ("g2s", "g2r", "g3s", "g3r", "s1s", "s1r", "s2s", "s2r", "s4s", "s4r"):
            scratch[key] = S((count,))
        for key in ("g1s", "g1r", "s3s", "s3r"):
            scratch[key] = S((count, high))
        results = call(True, n, part, inputs, outputs, scratch, [getattr(a, key) for key in keys])
        where = ["h"] * 6 + ["v"]
        finals = {"block_output": big["block_output"], "grad_visible": big["grad_visible"]}
        finals.update({key: (shape, "h" if "_w_" in key else "v") for key, shape in grads.items()})
        names = ["out_in", "seen_in", "w_qkv_in", "w_out_in", "w_up_in", "w_down_in", "small_in"]
        spec = {"v": pl.BlockSpec(memory_space=pltpu.VMEM), "h": pl.BlockSpec(memory_space=pl.ANY)}
        held = {"wide": V((PW, SMALL), f32), "sem": S((2, 10))}
        for name, key in (("out", "w_out"), ("qkv", "w_qkv"), ("up", "w_up"), ("down", "w_down")):
            held["buf_" + name] = V(grads["grad_" + key].shape, f32)
        held["buf_block"] = V(a.visible.shape, bf16)
        held["buf_seen"] = V(a.visible.shape, f32)
        final = pl.pallas_call(
            functools.partial(unpack_body, names + list(finals) + list(held), part),
            out_shape=tuple(shape for shape, _ in finals.values()),
            in_specs=[spec[w] for w in where],
            out_specs=tuple(spec[w] for _, w in finals.values()),
            scratch_shapes=list(held.values()),
        )(*results)
        final = dict(zip(finals, final, strict=True))
        final["grad_space_embed"] = final["grad_space_embed"].T
        return tuple(final.values())

    whole = whole_weights(a, part)
    cuts = (0, 3 * D, 4 * D, 4 * D + FF, 4 * D + 2 * FF, 4 * D + 2 * FF + SMALL)
    wqkv, wout, wup, wdown, wsmall = (whole[:, i:j] for i, j in zip(cuts[:-1], cuts[1:]))
    values = {
        "frames": a.frames, "assign": a.assign.reshape(MB), "visible": a.visible, "mask_flags": a.mask_flags,
        "cotangent": a.cotangent, "table": wsmall.T.astype(f32),
        "bup": wsmall[:, UPB : UPB + 4].astype(f32).reshape(1, FF),
        "wqkv": wqkv, "wout": wout, "wup": wup, "wdown": wdown.reshape(FF, D),
    }
    inputs = {key: "v" for key in values}
    inputs.update(frames="s", assign="s", visible="h", cotangent="h")
    outputs = dict(big)
    for name, (cols, times) in list(ARRAYS.items())[1:]:
        outputs["acc/" + name] = (sds((1, times * D, cols), f32), "v")
    outputs["gsm"] = (sds((SMALL, D), f32), "v")
    outputs["gbup"] = (sds((1, FF), f32), "v")
    scratch.pop("gsm")
    scratch.pop("gbup")
    out, gvis, g0, g1, g2, gout, gup, gdown, gsm, gbup = call(
        False, n, part, inputs, outputs, scratch, list(values.values())
    )
    gsmall = gsm.T.at[:, UPB : UPB + 4].set(gbup.reshape(D, 4))
    grads = jnp.concatenate([g0[0], g1[0], g2[0], gout[0], gup[0], gdown.reshape(D, FF), gsmall], axis=1)
    share = lax.psum_scatter(grads, "clip", scatter_dimension=0, tiled=True)
    share = lax.psum(share.astype(bf16), "tm").astype(f32)
    sqkv, sout, sup, sdown, ssmall = (share[:, i:j] for i, j in zip(cuts[:-1], cuts[1:]))
    sqkv = jnp.concatenate(
        [sqkv[:, D * p + PW * t : D * p + PW * (t + 1)] for t in range(3) for p in range(PAIRS)], axis=1
    )
    one = {name: ssmall[:, AT[name]] for name in VECTORS}
    return (
        out, gvis, one["mask_token"], ssmall[:, TIME : TIME + 8].T, ssmall[:, :FT].T, one["norm1_gain"],
        one["norm1_bias"], sqkv, one["bias_query"], one["bias_value"], sout, one["bias_out"], one["norm2_gain"],
        one["norm2_bias"], sup, ssmall[:, UPB : UPB + 4].reshape(-1), sdown.reshape(-1, D), one["bias_down"],
    )


def solution(mesh):
    rows = P(None, ("clip", "tm"), None)
    vec = P("clip")
    mat = P("clip", None)
    cols = P(None, "clip")
    in_specs = (
        rows, P(None, ("clip", "tm")), P(), cols, rows,
        vec, cols, cols, vec, vec, mat, vec, vec, mat, vec, vec, vec, mat, vec, mat, vec,
    )
    out_specs = (
        rows, rows, vec, cols, cols, vec, vec, mat, vec, vec, mat, vec, vec, vec, mat, vec, mat, vec,
    )
    return jax.shard_map(local, mesh=mesh, in_specs=in_specs, out_specs=out_specs, check_vma=False)
```

```python
import functools
import math
from types import SimpleNamespace

import jax
import jax.numpy as jnp
from jax import lax
from jax.experimental import pallas as pl
from jax.experimental.pallas import tpu as pltpu
from jax.sharding import PartitionSpec as P

D = 384
FF = 1536
FT = 196
FD = 4
MB = 2
NB = MB * FD
ROWS = 208
BOTH = MB * ROWS
WIN = 3 * ROWS
EPS = 1e-06
NEG = -1000000000.0
PAIRS = 3
PW = 128
SMALL = 256
TIME = 208
VEC = 216
UPB = 225
MESH = pl.DeviceIdType.MESH
f32 = jnp.float32
bf16 = jnp.bfloat16

OUT = 3
UP = 4
DOWN = 8
PIECES = 12
SMALLS = PIECES
HIDDEN = 384
CHUNKS = FF // HIDDEN
VECTORS = (
    "mask_token", "norm1_gain", "norm1_bias", "bias_query", "bias_value", "bias_out", "norm2_gain", "norm2_bias",
    "bias_down",
)
AT = {name: VEC + i for i, name in enumerate(VECTORS)}


def contract(a, b, ca, cb, precision=None):
    return lax.dot_general(
        a, b, (((ca,), (cb,)), ((), ())), preferred_element_type=f32, precision=precision
    )


def norm_stats(x):
    c = x - jnp.mean(x, axis=-1, keepdims=True)
    r = lax.rsqrt(jnp.mean(c * c, axis=-1, keepdims=True) + EPS)
    return c * r, r


def norm_back(g, xhat, r, gain):
    d = g * gain
    first = jnp.mean(d, axis=-1, keepdims=True)
    second = jnp.mean(d * xhat, axis=-1, keepdims=True)
    return r * (d - first - xhat * second)


def col_sum(x):
    return jnp.sum(x.astype(f32), axis=0, keepdims=True)


def iota(shape, dim):
    return lax.broadcasted_iota(jnp.int32, shape, dim)


def time_weights(shape, frame_dim, tm, lengths):
    block = iota(shape, frame_dim)
    row = iota(shape, 1 - frame_dim).astype(f32)
    length = jnp.where(block < FD, lengths[0].astype(f32), lengths[1].astype(f32))
    frame = (jnp.where(block < FD, block, block - FD) + FD * tm).astype(f32)
    den = jnp.maximum(length - 1.0, 1.0)
    num = frame * 7.0
    whole = jnp.floor((num + 0.5) / den)
    low = jnp.minimum(whole, 7.0)
    high = jnp.minimum(low + 1.0, 7.0)
    part = (num - whole * den) / den
    return jnp.where(row == low, 1.0 - part, 0.0) + jnp.where(row == high, part, 0.0)


class Exchange:
    def __init__(self, r, n, part):
        self.r, self.high, self.part = r, n // 4, part
        me = lax.axis_index("clip")
        self.tm = lax.axis_index("tm")
        self.h, self.mid, self.lo = me // 4, (me // 2) % 2, me % 2

    def device(self, h, mid, lo):
        return {"clip": (h * 2 + mid) * 2 + lo}

    def others(self):
        return [(self.h + d) % self.high for d in range(1, self.high)]

    def greet(self):
        barrier = pltpu.get_barrier_semaphore()
        peers = [self.device(h, self.mid, self.lo) for h in self.others()]
        peers += [self.device(self.h, 1 - self.mid, self.lo), self.device(self.h, self.mid, 1 - self.lo)]
        peers.append({"tm": 1 - self.tm})
        for peer in peers:
            pl.semaphore_signal(barrier, inc=1, device_id=peer, device_id_type=MESH)
        pl.semaphore_wait(barrier, len(peers))

    def copy(self, src, dst, send, recv, device):
        return pltpu.make_async_remote_copy(
            src_ref=src, dst_ref=dst, send_sem=send, recv_sem=recv, device_id=device, device_id_type=MESH
        )

    def of(self, key, i):
        if isinstance(i, int) and i == SMALLS:
            return getattr(self.r, "small_" + key)
        return getattr(self.r, "piece_" + key).at[i]

    def g1(self, i, sender, d, h):
        r, slot = self.r, self.of("whole", i).at[sender, self.mid, self.lo]
        return self.copy(slot, slot, r.g1s.at[i, d], r.g1r.at[i, sender], self.device(h, self.mid, self.lo))

    def g2(self, i, mid):
        r, part = self.r, self.of("whole", i).at[:, mid, self.lo]
        return self.copy(part, part, r.g2s.at[i], r.g2r.at[i], self.device(self.h, 1 - self.mid, self.lo))

    def g3(self, i, lo):
        r, part = self.r, self.of("whole", i).at[:, :, lo]
        return self.copy(part, part, r.g3s.at[i], r.g3r.at[i], self.device(self.h, self.mid, 1 - self.lo))

    def gather_1(self, i):
        for d, h in enumerate(self.others()):
            self.g1(i, self.h, d, h).start()

    def gather_2(self, i):
        for d, h in enumerate(self.others()):
            self.g1(i, h, d, h).wait_recv()
        self.g2(i, self.mid).start()

    def gather_3(self, i):
        self.g2(i, 1 - self.mid).wait_recv()
        self.g3(i, self.lo).start()

    def gather_4(self, i):
        self.g3(i, 1 - self.lo).wait_recv()

    def gather_sent(self, i):
        for d, h in enumerate(self.others()):
            self.g1(i, self.h, d, h).wait_send()
        self.g2(i, self.mid).wait_send()
        self.g3(i, self.lo).wait_send()

    def own(self, i, h, mid):
        return self.of("acc", i).at[(h * 2 + mid) * 2 + self.lo]

    def s1(self, i):
        r = self.r
        return self.copy(
            self.of("snd", i), self.of("rcv1", i), r.s1s.at[i], r.s1r.at[i], self.device(self.h, self.mid, 1 - self.lo)
        )

    def s2(self, i):
        r = self.r
        return self.copy(
            self.of("snd", i).at[0], self.of("rcv2", i), r.s2s.at[i], r.s2r.at[i],
            self.device(self.h, 1 - self.mid, self.lo),
        )

    def s3(self, i, h, slot, d):
        r = self.r
        return self.copy(
            self.of("snd", i).at[1, h], self.of("rcv3", i).at[slot], r.s3s.at[i, d], r.s3r.at[i, slot],
            self.device(h, self.mid, self.lo),
        )

    def s4(self, i):
        r = self.r
        return self.copy(self.of("snd4", i), self.of("rcv4", i), r.s4s.at[i], r.s4r.at[i], {"tm": 1 - self.tm})

    def sum_1(self, i):
        acc, snd = self.of("acc", i), self.of("snd", i)
        for h in range(self.high):
            for mid in range(2):
                snd[mid, h] = acc[(h * 2 + mid) * 2 + 1 - self.lo].astype(bf16)
        self.s1(i).start()

    def sum_2(self, i):
        snd, rcv = self.of("snd", i), self.of("rcv1", i)
        self.s1(i).wait()
        for h in range(self.high):
            snd[0, h] = (self.own(i, h, 1 - self.mid)[...] + rcv[1 - self.mid, h].astype(f32)).astype(bf16)
        self.s2(i).start()
        for h in range(self.high):
            self.own(i, h, self.mid)[...] += rcv[self.mid, h].astype(f32)

    def sum_3(self, i):
        snd, rcv = self.of("snd", i), self.of("rcv2", i)
        self.s2(i).wait_recv()
        for d, h in enumerate(self.others()):
            snd[1, h] = (self.own(i, h, self.mid)[...] + rcv[h].astype(f32)).astype(bf16)
            self.s3(i, h, self.h, d).start()

    def sum_4(self, i):
        rcv = self.of("rcv3", i)
        total = self.own(i, self.h, self.mid)[...] + self.of("rcv2", i)[self.h].astype(f32)
        for d, h in enumerate(self.others()):
            self.s3(i, h, h, d).wait_recv()
            total = total + rcv[h].astype(f32)
        self.of("snd4", i)[...] = total.astype(bf16)
        self.s4(i).start()

    def sum_5(self, i):
        self.s4(i).wait_recv()
        return self.of("snd4", i)[...].astype(f32) + self.of("rcv4", i)[...].astype(f32)

    def sum_sent(self, i):
        self.s2(i).wait_send()
        for d, h in enumerate(self.others()):
            self.s3(i, h, self.h, d).wait_send()
        self.s4(i).wait_send()


def body(names, fused, n, part, *refs):
    r = SimpleNamespace()
    for key, ref in zip(names, refs, strict=True):
        setattr(r, key, ref)
    tm = lax.axis_index("tm")
    peer = {"tm": 1 - tm}
    table = r.table

    lengths = [r.frames[r.assign[m]] for m in range(MB)]
    first_head = iota((1, PW), 1) < 64
    row_ok = (iota((ROWS, 1), 0) < FT).astype(f32)
    pad = jnp.zeros((ROWS - FT, D), f32)

    def vector(name):
        return table[AT[name] : AT[name] + 1, :]

    def valid_of(m, j):
        return jnp.where(FD * tm + j < lengths[m], 1.0, 0.0).astype(f32)

    def valid_rows(j):
        return jnp.concatenate([row_ok * valid_of(m, j) for m in range(MB)], axis=0)

    def near_last(jj):
        return jj + tm * (FD - 1 - 2 * jj)

    def span(m):
        return slice(ROWS * m, ROWS * (m + 1))

    def run_steps(steps, t):
        if fused and t in steps:
            for stage, item in steps[t]:
                getattr(x, stage)(item)

    def steps_at(steps, p, t):
        for k in range(PAIRS):
            if fused and t in steps[k]:

                @pl.when(p == k)
                def _():
                    run_steps(steps[k], t)

    def spread_pairs(ref, j, rows, value):
        for p in range(PAIRS):
            ref[p, j, rows] = value[:, PW * p : PW * (p + 1)].astype(ref.dtype)

    def join_pairs(ref, j):
        return jnp.concatenate([ref[p, j] for p in range(PAIRS)], axis=1)

    def settle(i, rows=None):
        whole = x.of("whole", i)
        for k in range(n // 2):
            two = jnp.concatenate([whole[k // 2, k % 2, 0].astype(f32), whole[k // 2, k % 2, 1].astype(f32)], axis=0)
            r.weights[i, 2 * part * k : 2 * part * (k + 1)] = two.astype(bf16)

    gsm, qkv = r.gsm, r.qkv
    if fused:
        x = Exchange(r, n, part)
        h, mid, lo = x.h, x.mid, x.lo

    def prelude(raw):
        load_seen = pltpu.make_async_copy(r.visible, raw, r.local_sem.at[0])
        load_top = pltpu.make_async_copy(r.cotangent, raw, r.local_sem.at[0])
        load_seen.start()
        if fused:
            loads = []
            for p in range(PAIRS):
                for t in range(3):
                    c = D * t + PW * p
                    loads.append((r.w_qkv.at[:, c : c + PW], (p, slice(PW * t, PW * (t + 1)))))
            loads.append((r.w_out, (OUT, slice(None))))
            for c in range(CHUNKS):
                loads.append((r.w_down.at[part * c : part * (c + 1)], (DOWN + c, slice(None))))
            loads = [
                pltpu.make_async_copy(src, r.piece_whole.at[i, h, mid, lo, :, cols], r.local_sem.at[1 + k])
                for k, (src, (i, cols)) in enumerate(loads)
            ]
            for load in loads:
                load.start()
            r.rows[...] = jnp.zeros_like(r.rows)
            r.rows[0:8, :part] = r.time_embed[...].astype(f32)
            for i, name in enumerate(VECTORS):
                r.rows[8 + i : 9 + i, :part] = getattr(r, name)[...].astype(f32).reshape(1, part)
            up = r.bias_up[...].astype(f32).reshape(1, 4 * part)
            for c in range(CHUNKS):
                r.rows[UPB - TIME + c : UPB - TIME + c + 1, :part] = up[:, part * c : part * (c + 1)]
            r.cols[...] = jnp.zeros_like(r.cols)
            r.cols[:, :FT] = r.space_embed[...].astype(f32)
            r.cols[:, TIME : TIME + 32] = jnp.transpose(r.rows[...])[:part]
            r.small_whole[h, mid, lo] = r.cols[...].astype(bf16)
            x.greet()
            x.gather_1(SMALLS)
            for load in loads:
                load.wait()
            for i in (0, 1, 2, OUT):
                x.gather_1(i)
            up = r.w_up[...].astype(f32)
            for c in range(CHUNKS):
                for i in range(n):
                    at = part * (4 * i + c)
                    r.shuffle[c, :, part * i : part * (i + 1)] = up[:, at : at + part]
                r.piece_whole[UP + c, h, mid, lo] = r.shuffle[c].astype(bf16)
            for c in range(CHUNKS):
                x.gather_1(UP + c)
                x.gather_1(DOWN + c)
        else:
            barrier = pltpu.get_barrier_semaphore()
            pl.semaphore_signal(barrier, inc=1, device_id=peer, device_id_type=MESH)
            pl.semaphore_wait(barrier, 1)

        flags = r.mask_flags[...].astype(f32)
        r.flag_rows[...] = jnp.zeros_like(r.flag_rows)
        for m in range(MB):
            for j in range(FD):
                r.flag_rows[j : j + 1, ROWS * m : ROWS * m + FT] = flags[m : m + 1, FT * j : FT * (j + 1)]
        r.flag_cols[...] = jnp.transpose(r.flag_rows[...])

        def unpack(m, j):
            return jnp.concatenate([raw[m, FT * j : FT * (j + 1), :].astype(f32), pad], axis=0)

        load_seen.wait()
        for m in range(MB):
            for j in range(FD):
                r.x0s[j, span(m)] = unpack(m, j)
        load_top.start()
        if fused:
            x.gather_2(SMALLS)
            x.gather_2(0)
        gsm[...] = jnp.zeros_like(gsm)
        for m in range(MB):
            qkv[:, (FD + 1) * tm, m] = jnp.zeros((PAIRS, ROWS, D), bf16)
        if fused:
            x.gather_3(SMALLS)
            x.gather_2(1)
            x.gather_3(0)
        load_top.wait()
        for m in range(MB):
            for j in range(FD):
                spread_pairs(r.tops, j, span(m), unpack(m, j) * (row_ok * valid_of(m, j)))

    pl.run_scoped(prelude, pltpu.VMEM((MB, FD * FT, D), bf16))
    r.piece_acc[OUT] = jnp.zeros_like(r.piece_acc[OUT])
    if fused:
        x.gather_4(SMALLS)
        for k in range(n // 2):
            for e in range(2):
                r.small_acc[2 * k + e] = r.small_whole[k // 2, k % 2, e].astype(f32)
        table[...] = jnp.transpose(r.small_acc[...].reshape(D, SMALL))
    for p in range(PAIRS):
        for k, name in enumerate(("bias_query", "bias_value")):
            r.pair_bias[p, k : k + 1] = vector(name)[:, PW * p : PW * (p + 1)]

    blend = time_weights((NB, 8), 0, tm, lengths)
    total = jnp.zeros((NB, D), f32)
    for t in range(8):
        total = total + blend[:, t : t + 1] * table[TIME + t : TIME + t + 1, :]
    r.temporal[...] = total
    for j in range(FD):
        for m in range(MB):
            b = m * FD + j
            base = jnp.where(r.flag_cols[span(m), j : j + 1] > 0.5, vector("mask_token"), r.x0s[j, span(m)])
            base = base + r.temporal[b : b + 1, :] + table[:ROWS, :]
            x0 = base * (row_ok * valid_of(m, j))
            r.x0s[j, span(m)] = x0
            xhat, _ = norm_stats(x0)
            r.a1s[j, span(m)] = (xhat * vector("norm1_gain") + vector("norm1_bias")).astype(bf16)

    key = iota((1, WIN), 1)
    slot = (key >= ROWS).astype(jnp.int32) + (key >= 2 * ROWS).astype(jnp.int32)
    key_real = key - slot * ROWS < FT
    ones = jnp.ones((WIN, PW), bf16)

    def stack_heads(v):
        zero = jnp.zeros_like(v)
        return jnp.concatenate([jnp.where(first_head, v, zero), jnp.where(first_head, zero, v)], axis=0)

    def join_heads(v):
        return jnp.where(first_head, v[:ROWS], v[ROWS:])

    def window(p, m, j, k):
        return qkv[p, pl.ds(j, 3), m, :, PW * k : PW * (k + 1)].reshape(WIN, PW)

    def halo(p):
        cols = slice(PW, D)
        return pltpu.make_async_remote_copy(
            src_ref=qkv.at[p, FD - (FD - 1) * tm, :, :, cols], dst_ref=qkv.at[p, (FD + 1) * tm, :, :, cols],
            send_sem=r.halo_sem.at[0, p], recv_sem=r.halo_sem.at[1, p], device_id=peer, device_id_type=MESH,
        )

    def project(p):
        for jj in range(FD):
            j = near_last(FD - 1 - jj)
            y = contract(r.a1s[j], r.weights[p], 1, 0)
            q = (y[:, :PW] + r.pair_bias[p, 0:1]).astype(bf16).astype(f32)
            v = y[:, 2 * PW :] + r.pair_bias[p, 1:2]
            for m in range(MB):
                qkv[p, j + 1, m, :, :PW] = (q[span(m)] * 0.125).astype(bf16)
                qkv[p, j + 1, m, :, PW : 2 * PW] = y[span(m), PW : 2 * PW].astype(bf16)
                qkv[p, j + 1, m, :, 2 * PW :] = v[span(m)].astype(bf16)

    def prepare(p):
        if fused:
            x.gather_4(p)
            settle(p)
        project(p)

    def attend(p, probs, scale, steps):
        order = [(jj, m) for jj in range(FD) for m in range(MB)]
        scores = {}
        for t in range(NB + 2):
            steps_at(steps, p, t)
            if t < NB:
                jj, m = order[t]
                j = near_last(jj)
                if t == NB - MB:

                    @pl.when(p < PAIRS - 1)
                    def _():
                        prepare(p + 1)

                    halo(p).wait()

                    @pl.when(p < PAIRS - 1)
                    def _():
                        halo(p + 1).start()

                frame = FD * tm + j
                key_frame = frame - 1 + slot
                allowed = ((key_frame >= 0) & (key_frame < lengths[m])) | (frame >= lengths[m])
                bias = jnp.where(allowed & key_real, 0.0, NEG)
                scores[t] = contract(stack_heads(qkv[p, j + 1, m, :, :PW]), window(p, m, j, 1), 1, 1) + bias
            if 0 <= t - 1 < NB:
                jj, m = order[t - 1]
                s = scores.pop(t - 1)
                e = jnp.exp(s - jnp.max(s, axis=-1, keepdims=True))
                probs[p, near_last(jj), m] = e.astype(bf16)
            if 0 <= t - 2 < NB:
                jj, m = order[t - 2]
                j = near_last(jj)
                values = jnp.concatenate([window(p, m, j, 2), ones], axis=1)
                both = contract(probs[p, j, m], values, 1, 0)
                inverse = 1.0 / join_heads(both[:, PW:])
                r.os[p, j, span(m)] = join_heads(both[:, :PW]) * inverse
                scale[p, j, span(m)] = inverse

    def pieces(stage, *items):
        return [(stage, i) for i in items]

    U, W = UP, DOWN
    forward_steps = [
        {
            0: pieces("gather_2", 2, OUT) + pieces("gather_3", 1),
            4: pieces("gather_2", U),
            8: pieces("gather_2", W) + pieces("gather_3", 2),
        },
        {
            0: pieces("gather_2", U + 1) + pieces("gather_3", OUT),
            5: pieces("gather_2", W + 1) + pieces("gather_3", U),
        },
        {
            0: pieces("gather_2", U + 2) + pieces("gather_3", W),
            5: pieces("gather_2", W + 2) + pieces("gather_3", U + 1),
        },
    ]

    def add_grad(i, value, first=False):
        acc = r.piece_acc
        value = value.reshape(acc.shape[1:])
        acc[i] = value if first else acc[i] + value

    def small_grad(name, value):
        gsm[AT[name] : AT[name] + 1, :] += col_sum(value)

    def mix(j):
        o = join_pairs(r.os, j).astype(bf16)
        return o, r.x0s[j] + contract(o, r.weights[OUT], 1, 0) + vector("bias_out")

    def feed_start(j, x2s, ga2s, a2s):
        _, x1 = mix(j)
        xhat, _ = norm_stats(x1)
        a2s[j] = (xhat * vector("norm2_gain") + vector("norm2_bias")).astype(bf16)
        x2s[j] = x1 + vector("bias_down")
        ga2s[j] = jnp.zeros((BOTH, D), f32)

    def feed(c, x2s, ga2s, a2s):
        bias = table[pl.ds(UPB + c, 1), :]

        def products(j):
            g2 = join_pairs(r.tops, j)
            return contract(a2s[j], r.weights[UP + c], 1, 0) + bias, g2, contract(g2, r.weights[DOWN + c], 1, 1)

        bias_grad = jnp.zeros((1, D), f32)
        ready = products(0)
        for j in range(FD):
            u, g2, gz = ready
            if j + 1 < FD:
                ready = products(j + 1)
            if fused:
                if j == 1:

                    @pl.when(c > 0)
                    def _():
                        x.sum_2(UP + c - 1)
                        x.sum_2(DOWN + c - 1)

                    @pl.when(c == 0)
                    def _():
                        run_steps({1: pieces("gather_2", U + 3, W + 3) + pieces("gather_3", W + 1)}, 1)

                if j == 2:

                    @pl.when(c > 1)
                    def _():
                        x.sum_3(UP + c - 2)
                        x.sum_3(DOWN + c - 2)

                if j == 3:

                    @pl.when(c > 2)
                    def _():
                        x.sum_4(UP + c - 3)
                        x.sum_4(DOWN + c - 3)

                    @pl.when(c < CHUNKS - 2)
                    def _():
                        x.gather_3(UP + c + 2)
                        x.gather_3(DOWN + c + 2)

            cdf = 0.5 + 0.5 * lax.erf(u * (1.0 / math.sqrt(2.0)))
            pdf = jnp.exp(u * u * -0.5) * (1.0 / math.sqrt(2.0 * math.pi))
            z = (u * cdf).astype(bf16)
            gu = (gz * (cdf + u * pdf)).astype(bf16)
            bias_grad = bias_grad + col_sum(gu)
            x2s[j] += contract(z, r.weights[DOWN + c], 1, 0)
            ga2s[j] += contract(gu, r.weights[UP + c], 1, 1)
            add_grad(DOWN + c, contract(z, g2, 0, 0), j == 0)
            add_grad(UP + c, contract(a2s[j], gu, 0, 0), j == 0)
        gsm[pl.ds(UPB + c, 1), :] = bias_grad
        if fused:
            x.sum_1(UP + c)
            x.sum_1(DOWN + c)

    def feed_end(j, raw, scale, x2s, ga2s):
        o, x1 = mix(j)
        xhat, rstd = norm_stats(x1)
        y = (x2s[j] * valid_rows(j)).astype(bf16)
        for k in range(FD):

            @pl.when(j == k)
            def _():
                for m in range(MB):
                    raw[m, FT * k : FT * (k + 1), :] = y[ROWS * m : ROWS * m + FT]

        g2, ga2 = join_pairs(r.tops, j), ga2s[j]
        small_grad("bias_down", g2)
        small_grad("norm2_gain", ga2 * xhat)
        small_grad("norm2_bias", ga2)
        gx1 = g2.astype(f32) + norm_back(ga2, xhat, rstd, vector("norm2_gain"))
        gy = gx1.astype(bf16)
        small_grad("bias_out", gy)
        add_grad(OUT, contract(o, gy, 0, 0))
        go = contract(gy, r.weights[OUT], 1, 1).astype(bf16).astype(f32)
        spread_pairs(r.tops, j, slice(0, BOTH), go * join_pairs(scale, j))
        spread_pairs(r.gx1s, j, slice(0, BOTH), gx1)

    near = FD - (FD - 1) * tm
    away = (FD + 1) * (1 - tm)

    def back(p):
        return pltpu.make_async_remote_copy(
            src_ref=r.back_out, dst_ref=r.back_in.at[p],
            send_sem=r.back_sem.at[0, p], recv_sem=r.back_sem.at[1, p], device_id=peer, device_id_type=MESH,
        )

    def attend_back(p, probs, gkv, steps):
        gkv[...] = jnp.zeros_like(gkv)
        order = [(FD - 1 - jj, m) for jj in range(FD) for m in range(MB)]
        diffs, slopes = {}, {}
        for t in range(NB + 2):
            steps_at(steps, p, t)
            if t < NB:
                jj, m = order[t]
                j = near_last(jj)
                o = r.os[p, j, span(m)]
                go = stack_heads(r.tops[p, j, span(m)])
                delta = jnp.sum(go.astype(f32) * jnp.concatenate([o, o], axis=0), axis=-1, keepdims=True)
                diffs[t] = contract(go, window(p, m, j, 2), 1, 1) - delta
                gv = jnp.transpose(contract(go, probs[p, j, m], 0, 0)).reshape(3, ROWS, PW)
                gkv[pl.ds(j, 3), m, :, PW:] += gv
            if 0 <= t - 1 < NB:
                jj, m = order[t - 1]
                slopes[t - 1] = (probs[p, near_last(jj), m].astype(f32) * diffs.pop(t - 1)).astype(bf16)
            if 0 <= t - 2 < NB:
                jj, m = order[t - 2]
                j = near_last(jj)
                gs = slopes.pop(t - 2)
                q = stack_heads(qkv[p, j + 1, m, :, :PW])
                gk = jnp.transpose(contract(q, gs, 0, 0)).reshape(3, ROWS, PW)
                gkv[pl.ds(j, 3), m, :, :PW] += gk
                gq = join_heads(contract(gs, window(p, m, j, 1), 1, 0))
                qkv[p, j + 1, m, :, :PW] = (gq * 0.125).astype(bf16)
            if t == MB + 1:
                r.back_out[...] = gkv[away].astype(bf16)
                back(p).start()
        back(p).wait_send()

        @pl.when(p > 0)
        def _():
            complete(p - 1)

        r.near_acc[...] = gkv[near]
        qkv[p, 1 : FD + 1, :, :, PW:] = gkv[1 : FD + 1].astype(bf16)

    def complete(p):
        back(p).wait_recv()
        qkv[p, near, :, :, PW:] = (r.near_acc[...] + r.back_in[p].astype(f32)).astype(bf16)
        total = 0.0
        for j in range(FD):
            total = total + contract(r.a1s[j], qkv[p, j + 1].reshape(BOTH, D), 0, 0)
        r.piece_acc[p] = total.reshape(r.piece_acc.shape[1:])
        if fused:
            x.sum_1(p)

    backward_steps = [
        {
            1: pieces("sum_2", OUT),
            6: pieces("sum_3", U + 3, W + 3),
            9: pieces("sum_4", U + 2, W + 2),
        },
        {
            3: pieces("sum_3", OUT),
            8: pieces("sum_4", U + 3, W + 3),
        },
        {
            2: pieces("sum_2", 0) + pieces("sum_4", OUT),
            9: pieces("sum_3", 0),
        },
    ]

    def middle(probs):
        scale = r.gx1s

        def forward(p, carry):
            attend(p, probs, scale, forward_steps)
            return carry

        prepare(0)
        halo(0).start()
        lax.fori_loop(0, PAIRS, forward, 0)
        if fused:
            x.gather_4(OUT)
            settle(OUT)

        def feeding(raw, x2s, ga2s, a2s):
            def start(j, carry):
                feed_start(j, x2s, ga2s, a2s)
                return carry

            def one(c, carry):
                if fused:
                    for i in (UP + c, DOWN + c):
                        x.gather_4(i)
                        settle(i)
                feed(c, x2s, ga2s, a2s)
                return carry

            def end(j, carry):
                feed_end(j, raw, scale, x2s, ga2s)
                return carry

            lax.fori_loop(0, FD, start, 0)
            lax.fori_loop(0, CHUNKS, one, 0)
            lax.fori_loop(0, 2, end, 0)
            run_steps({0: pieces("sum_2", U + 3, W + 3) + pieces("sum_3", U + 2, W + 2)}, 0)
            lax.fori_loop(2, FD, end, 0)
            store = pltpu.make_async_copy(raw, r.block_output, r.local_sem.at[0])
            store.start()
            run_steps({0: pieces("sum_1", OUT) + pieces("sum_4", U + 1, W + 1)}, 0)
            store.wait()

        pl.run_scoped(
            feeding, pltpu.VMEM((MB, FD * FT, D), bf16), pltpu.VMEM((FD, BOTH, D), f32),
            pltpu.VMEM((FD, BOTH, D), f32), pltpu.VMEM((FD, BOTH, D), bf16),
        )

        def backward(gkv):
            def step(p, carry):
                attend_back(p, probs, gkv, backward_steps)
                return carry

            lax.fori_loop(0, PAIRS, step, 0)
            complete(PAIRS - 1)

        pl.run_scoped(backward, pltpu.VMEM((FD + 2, MB, ROWS, 2 * PW), f32))

    pl.run_scoped(middle, pltpu.VMEM((PAIRS, FD, MB, BOTH, WIN), bf16))

    final_steps = {
        0: pieces("sum_2", 1),
        1: pieces("sum_2", 2),
        3: pieces("sum_4", 0),
    }

    def last(gvis):
        for j in range(FD):
            run_steps(final_steps, j)
            xhat, rstd = norm_stats(r.x0s[j])
            ga1 = 0.0
            for p in range(PAIRS):
                gp = qkv[p, j + 1].reshape(BOTH, D)
                sums = col_sum(gp)
                cols = slice(PW * p, PW * (p + 1))
                gsm[AT["bias_query"] : AT["bias_query"] + 1, cols] += sums[:, :PW]
                gsm[AT["bias_value"] : AT["bias_value"] + 1, cols] += sums[:, 2 * PW :]
                ga1 = ga1 + contract(gp, r.weights[p], 1, 1)
            small_grad("norm1_gain", ga1 * xhat)
            small_grad("norm1_bias", ga1)
            gb = (join_pairs(r.gx1s, j) + norm_back(ga1, xhat, rstd, vector("norm1_gain"))) * valid_rows(j)
            masked = r.flag_cols[:BOTH, j : j + 1] > 0.5
            small_grad("mask_token", jnp.where(masked, gb, 0.0))
            seen = jnp.where(masked, 0.0, gb)
            for m in range(MB):
                gsm[:ROWS, :] += gb[span(m)]
                r.sumgb[m * FD + j : m * FD + j + 1, :] = col_sum(gb[span(m)])
                gvis[m, FT * j : FT * (j + 1), :] = seen[ROWS * m : ROWS * m + FT]
        store_seen = pltpu.make_async_copy(gvis, r.grad_visible, r.local_sem.at[0])
        store_seen.start()
        blend = time_weights((8, NB), 1, tm, lengths)
        total = jnp.zeros((8, D), f32)
        for b in range(NB):
            total = total + blend[:, b : b + 1] * r.sumgb[b : b + 1, :]
        gsm[TIME : TIME + 8, :] = total
        if fused:
            r.small_acc[...] = jnp.transpose(gsm[...]).reshape(r.small_acc.shape)
            x.sum_1(SMALLS)
            x.sum_3(1)
            x.sum_2(SMALLS)
            x.sum_3(2)
            for c in range(CHUNKS):
                share = x.sum_5(UP + c)
                for i in range(n):
                    at = part * (4 * i + c)
                    r.grad_w_up[:, at : at + part] = share[:, part * i : part * (i + 1)]
                r.grad_w_down[part * c : part * (c + 1)] = x.sum_5(DOWN + c)
            r.grad_w_out[...] = x.sum_5(OUT)
            x.sum_3(SMALLS)
            x.sum_4(1)
            x.sum_4(2)
            for p in range(PAIRS):
                share = x.sum_5(p)
                for t in range(3):
                    c = D * t + PW * p
                    r.grad_w_qkv[:, c : c + PW] = share[:, PW * t : PW * (t + 1)]
            x.sum_4(SMALLS)
            r.grad_small[...] = x.sum_5(SMALLS)
        store_seen.wait()
        if fused:

            def sent(i, carry):
                x.gather_sent(i)
                x.sum_sent(i)
                return carry

            lax.fori_loop(0, PIECES, sent, 0)
            x.gather_sent(SMALLS)
            x.sum_sent(SMALLS)

    pl.run_scoped(last, pltpu.VMEM((MB, FD * FT, D), f32))


def unpack_body(names, part, *refs):
    r = SimpleNamespace(**dict(zip(names, refs, strict=True)))
    parts = [(r.out_in.at[m], r.buf_block.at[m], r.block_output.at[m]) for m in range(MB)]
    parts += [
        (r.seen_in.at[m, rows], r.buf_seen.at[m, rows], r.grad_visible.at[m, rows])
        for m in range(MB)
        for rows in (slice(0, FD * FT // 2), slice(FD * FT // 2, FD * FT))
    ]
    parts += [
        (getattr(r, "w_%s_in" % name), getattr(r, "buf_" + name), getattr(r, "grad_w_" + name))
        for name in ("qkv", "out", "up", "down")
    ]
    loads = [pltpu.make_async_copy(src, buf, r.sem.at[0, i]) for i, (src, buf, _) in enumerate(parts)]
    stores = [pltpu.make_async_copy(buf, dst, r.sem.at[1, i]) for i, (_, buf, dst) in enumerate(parts)]
    for load in loads:
        load.start()
    small = r.small_in[...]
    r.grad_space_embed[...] = small[:, :FT]
    r.wide[:part] = small
    rows = jnp.transpose(r.wide[:, PW:])
    r.grad_time_embed[...] = rows[TIME - PW : TIME - PW + 8, :part]
    for name in VECTORS:
        at = AT[name] - PW
        getattr(r, "grad_" + name)[...] = rows[at : at + 1, :part].reshape(part)
    for c in range(CHUNKS):
        r.line[0:1, part * c : part * (c + 1)] = rows[UPB + c - PW : UPB + c + 1 - PW, :part]
    r.grad_bias_up[...] = r.line[0:1, : 4 * part].reshape(4 * part)
    for load, store in zip(loads, stores):
        load.wait()
        store.start()
    for store in stores:
        store.wait()


def call(fused, n, part, inputs, outputs, scratch, arrays):
    smem = pl.BlockSpec(memory_space=pltpu.SMEM)
    vmem = pl.BlockSpec(memory_space=pltpu.VMEM)
    hbm = pl.BlockSpec(memory_space=pl.ANY)
    spec = {"s": smem, "v": vmem, "h": hbm}
    names = list(inputs) + list(outputs) + list(scratch)
    return pl.pallas_call(
        functools.partial(body, names, fused, n, part),
        out_shape=tuple(shape for shape, _ in outputs.values()),
        in_specs=[spec[where] for where in inputs.values()],
        out_specs=tuple(spec[where] for _, where in outputs.values()),
        scratch_shapes=list(scratch.values()),
        compiler_params=pltpu.CompilerParams(
            collective_id=0, has_side_effects=True, vmem_limit_bytes=64 * 2**20 - 2**16
        ),
    )(*arrays)


def common_scratch():
    V, S = pltpu.VMEM, pltpu.SemaphoreType.DMA
    return {
        "flag_rows": V((8, 512), f32),
        "flag_cols": V((512, 8), f32),
        "pair_bias": V((PAIRS, 8, PW), f32),
        "x0s": V((FD, BOTH, D), f32),
        "gx1s": V((PAIRS, FD, BOTH, PW), f32),
        "tops": V((PAIRS, FD, BOTH, PW), bf16),
        "os": V((PAIRS, FD, BOTH, PW), f32),
        "a1s": V((FD, BOTH, D), bf16),
        "qkv": V((PAIRS, FD + 2, MB, ROWS, D), bf16),
        "temporal": V((NB, D), f32),
        "sumgb": V((NB, D), f32),
        "back_out": V((MB, ROWS, 2 * PW), bf16),
        "back_in": V((PAIRS, MB, ROWS, 2 * PW), bf16),
        "near_acc": V((MB, ROWS, 2 * PW), f32),
        "halo_sem": S((2, PAIRS)),
        "back_sem": S((2, PAIRS)),
        "local_sem": S((24,)),
    }


def whole_weights(shards, part):
    s = shards
    small = jnp.concatenate(
        [s.space_embed.T, jnp.zeros((part, TIME - FT), bf16), s.time_embed.T]
        + [getattr(s, name)[:, None] for name in VECTORS]
        + [s.bias_up.reshape(part, 4), jnp.zeros((part, SMALL - UPB - 4), bf16)],
        axis=1,
    )
    pairs = [s.w_qkv[:, D * t + PW * p : D * t + PW * (p + 1)] for p in range(PAIRS) for t in range(3)]
    pack = jnp.concatenate(pairs + [s.w_out, s.w_up, s.w_down.reshape(part, FF), small], axis=1)
    return lax.all_gather(pack, "clip", axis=0, tiled=True)


def local(*args):
    keys = (
        "visible", "mask_flags", "frames", "assign", "cotangent", "mask_token", "time_embed", "space_embed",
        "norm1_gain", "norm1_bias", "w_qkv", "bias_query", "bias_value", "w_out", "bias_out", "norm2_gain",
        "norm2_bias", "w_up", "bias_up", "w_down", "bias_down",
    )
    a = SimpleNamespace(**dict(zip(keys, args, strict=True)))
    n = lax.axis_size("clip")
    part = D // n
    V, S, sds = pltpu.VMEM, pltpu.SemaphoreType.DMA, jax.ShapeDtypeStruct
    scratch = common_scratch()
    big = {"block_output": (sds(a.visible.shape, bf16), "h"), "grad_visible": (sds(a.visible.shape, f32), "h")}

    if part % 8 == 0 and n % 16 == 0:
        high = n // 4
        a.assign = a.assign.reshape(MB)
        a.space_embed = a.space_embed.T
        inputs = {key: "v" for key in keys}
        inputs.update(frames="s", assign="s", visible="h", cotangent="h", w_qkv="h", w_out="h", w_down="h")
        grads = {"grad_" + key: sds(getattr(a, key).shape, f32) for key in keys[5:]}
        outputs = dict(big)
        for key in ("grad_w_qkv", "grad_w_out", "grad_w_up", "grad_w_down"):
            outputs[key] = (grads[key], "v")
        outputs["grad_small"] = (sds((part, SMALL), f32), "v")
        scratch.update(
            {
                "rows": V((32, PW), f32),
                "cols": V((part, SMALL), f32),
                "table": V((SMALL, D), f32),
                "shuffle": V((CHUNKS, part, D), f32),
                "weights": V((PIECES, D, D), bf16),
                "gsm": V((SMALL, D), f32),
            }
        )
        for kind, count, width in (("piece_", (PIECES,), D), ("small_", (), SMALL)):
            scratch[kind + "whole"] = V((*count, high, 2, 2, part, width), bf16)
            scratch[kind + "acc"] = V((*count, n, part, width), f32)
            for key, lead in (("snd", (2, high)), ("rcv1", (2, high)), ("rcv2", (high,)), ("rcv3", (high,)), ("snd4", ()), ("rcv4", ())):
                scratch[kind + key] = V((*count, *lead, part, width), bf16)
        for key in ("g2s", "g2r", "g3s", "g3r", "s1s", "s1r", "s2s", "s2r", "s4s", "s4r"):
            scratch[key] = S((PIECES + 1,))
        for key in ("g1s", "g1r", "s3s", "s3r"):
            scratch[key] = S((PIECES + 1, high))
        results = call(True, n, part, inputs, outputs, scratch, [getattr(a, key) for key in keys])
        where = ["h"] * 6 + ["v"]
        finals = {"block_output": big["block_output"], "grad_visible": big["grad_visible"]}
        finals.update({key: (shape, "h" if "_w_" in key else "v") for key, shape in grads.items()})
        names = ["out_in", "seen_in", "w_qkv_in", "w_out_in", "w_up_in", "w_down_in", "small_in"]
        spec = {"v": pl.BlockSpec(memory_space=pltpu.VMEM), "h": pl.BlockSpec(memory_space=pl.ANY)}
        held = {"wide": V((PW, SMALL), f32), "line": V((8, 4 * part), f32), "sem": S((2, 10))}
        for name, key in (("out", "w_out"), ("qkv", "w_qkv"), ("up", "w_up"), ("down", "w_down")):
            held["buf_" + name] = V(grads["grad_" + key].shape, f32)
        held["buf_block"] = V(a.visible.shape, bf16)
        held["buf_seen"] = V(a.visible.shape, f32)
        final = pl.pallas_call(
            functools.partial(unpack_body, names + list(finals) + list(held), part),
            out_shape=tuple(shape for shape, _ in finals.values()),
            in_specs=[spec[w] for w in where],
            out_specs=tuple(spec[w] for _, w in finals.values()),
            scratch_shapes=list(held.values()),
        )(*results)
        final = dict(zip(finals, final, strict=True))
        final["grad_space_embed"] = final["grad_space_embed"].T
        return tuple(final.values())

    whole = whole_weights(a, part)
    cuts = (0, 3 * D, 4 * D, 4 * D + FF, 4 * D + 2 * FF, 4 * D + 2 * FF + SMALL)
    wqkv, wout, wup, wdown, wsmall = (whole[:, i:j] for i, j in zip(cuts[:-1], cuts[1:]))
    values = {
        "frames": a.frames, "assign": a.assign.reshape(MB), "visible": a.visible, "mask_flags": a.mask_flags,
        "cotangent": a.cotangent,
        "table": wsmall.T.at[UPB : UPB + 4].set(wsmall[:, UPB : UPB + 4].reshape(CHUNKS, HIDDEN)).astype(f32),
        "weights": jnp.stack(
            [wqkv[:, D * p : D * (p + 1)] for p in range(PAIRS)]
            + [wout]
            + [wup[:, HIDDEN * c : HIDDEN * (c + 1)] for c in range(CHUNKS)]
            + list(wdown.reshape(CHUNKS, HIDDEN, D))
        ),
    }
    inputs = {key: "v" for key in values}
    inputs.update(frames="s", assign="s", visible="h", cotangent="h")
    outputs = dict(big)
    outputs["piece_acc"] = (sds((PIECES, 1, D, D), f32), "v")
    outputs["gsm"] = (sds((SMALL, D), f32), "v")
    out, gvis, gpieces, gsm = call(False, n, part, inputs, outputs, scratch, list(values.values()))
    gpieces = gpieces[:, 0]
    gdown = gpieces[DOWN:].reshape(D, FF)
    gsmall = gsm.T.at[:, UPB : UPB + 4].set(gsm[UPB : UPB + 4].reshape(D, 4))
    grads = jnp.concatenate([*gpieces[:DOWN], gdown, gsmall], axis=1)
    share = lax.psum_scatter(grads, "clip", scatter_dimension=0, tiled=True)
    share = lax.psum(share.astype(bf16), "tm").astype(f32)
    sqkv, sout, sup, sdown, ssmall = (share[:, i:j] for i, j in zip(cuts[:-1], cuts[1:]))
    sqkv = jnp.concatenate(
        [sqkv[:, D * p + PW * t : D * p + PW * (t + 1)] for t in range(3) for p in range(PAIRS)], axis=1
    )
    one = {name: ssmall[:, AT[name]] for name in VECTORS}
    return (
        out, gvis, one["mask_token"], ssmall[:, TIME : TIME + 8].T, ssmall[:, :FT].T, one["norm1_gain"],
        one["norm1_bias"], sqkv, one["bias_query"], one["bias_value"], sout, one["bias_out"], one["norm2_gain"],
        one["norm2_bias"], sup, ssmall[:, UPB : UPB + 4].reshape(-1), sdown.reshape(-1, D), one["bias_down"],
    )


def solution(mesh):
    rows = P(None, ("clip", "tm"), None)
    vec = P("clip")
    mat = P("clip", None)
    cols = P(None, "clip")
    in_specs = (
        rows, P(None, ("clip", "tm")), P(), cols, rows,
        vec, cols, cols, vec, vec, mat, vec, vec, mat, vec, vec, vec, mat, vec, mat, vec,
    )
    out_specs = (
        rows, rows, vec, cols, cols, vec, vec, mat, vec, vec, mat, vec, vec, vec, mat, vec, mat, vec,
    )
    return jax.shard_map(local, mesh=mesh, in_specs=in_specs, out_specs=out_specs, check_vma=False)
```

```python
import functools
import math
from types import SimpleNamespace

import jax
import jax.numpy as jnp
from jax import lax
from jax.experimental import pallas as pl
from jax.experimental.pallas import tpu as pltpu
from jax.sharding import PartitionSpec as P

D = 384
FF = 1536
FT = 196
FD = 4
MB = 2
NB = MB * FD
ROWS = 208
BOTH = MB * ROWS
WIN = 3 * ROWS
EPS = 1e-06
NEG = -1000000000.0
PAIRS = 3
PW = 128
SMALL = 256
TIME = 208
VEC = 216
UPB = 225
MESH = pl.DeviceIdType.MESH
f32 = jnp.float32
bf16 = jnp.bfloat16

OUT = 3
UP = 4
DOWN = 8
PIECES = 12
SMALLS = PIECES
HIDDEN = 384
CHUNKS = FF // HIDDEN
VECTORS = (
    "mask_token", "norm1_gain", "norm1_bias", "bias_query", "bias_value", "bias_out", "norm2_gain", "norm2_bias",
    "bias_down",
)
AT = {name: VEC + i for i, name in enumerate(VECTORS)}


def contract(a, b, ca, cb, precision=None):
    return lax.dot_general(
        a, b, (((ca,), (cb,)), ((), ())), preferred_element_type=f32, precision=precision
    )


def norm_stats(x):
    c = x - jnp.mean(x, axis=-1, keepdims=True)
    r = lax.rsqrt(jnp.mean(c * c, axis=-1, keepdims=True) + EPS)
    return c * r, r


def norm_back(g, xhat, r, gain):
    d = g * gain
    first = jnp.mean(d, axis=-1, keepdims=True)
    second = jnp.mean(d * xhat, axis=-1, keepdims=True)
    return r * (d - first - xhat * second)


def col_sum(x):
    return jnp.sum(x.astype(f32), axis=0, keepdims=True)


def iota(shape, dim):
    return lax.broadcasted_iota(jnp.int32, shape, dim)


def time_weights(shape, frame_dim, tm, lengths):
    block = iota(shape, frame_dim)
    row = iota(shape, 1 - frame_dim).astype(f32)
    length = jnp.where(block < FD, lengths[0].astype(f32), lengths[1].astype(f32))
    frame = (jnp.where(block < FD, block, block - FD) + FD * tm).astype(f32)
    den = jnp.maximum(length - 1.0, 1.0)
    num = frame * 7.0
    whole = jnp.floor((num + 0.5) / den)
    low = jnp.minimum(whole, 7.0)
    high = jnp.minimum(low + 1.0, 7.0)
    part = (num - whole * den) / den
    return jnp.where(row == low, 1.0 - part, 0.0) + jnp.where(row == high, part, 0.0)


class Exchange:
    def __init__(self, r, n, part):
        self.r, self.high, self.part = r, n // 4, part
        me = lax.axis_index("clip")
        self.tm = lax.axis_index("tm")
        self.h, self.mid, self.lo = me // 4, (me // 2) % 2, me % 2

    def device(self, h, mid, lo):
        return {"clip": (h * 2 + mid) * 2 + lo}

    def others(self):
        return [(self.h + d) % self.high for d in range(1, self.high)]

    def greet(self):
        barrier = pltpu.get_barrier_semaphore()
        peers = [self.device(h, self.mid, self.lo) for h in self.others()]
        peers += [self.device(self.h, 1 - self.mid, self.lo), self.device(self.h, self.mid, 1 - self.lo)]
        peers.append({"tm": 1 - self.tm})
        for peer in peers:
            pl.semaphore_signal(barrier, inc=1, device_id=peer, device_id_type=MESH)
        pl.semaphore_wait(barrier, len(peers))

    def copy(self, src, dst, send, recv, device):
        return pltpu.make_async_remote_copy(
            src_ref=src, dst_ref=dst, send_sem=send, recv_sem=recv, device_id=device, device_id_type=MESH
        )

    def of(self, key, i):
        if isinstance(i, int) and i == SMALLS:
            return getattr(self.r, "small_" + key)
        return getattr(self.r, "piece_" + key).at[i]

    def g1(self, i, sender, d, h):
        r, slot = self.r, self.of("whole", i).at[sender, self.mid, self.lo]
        return self.copy(slot, slot, r.g1s.at[i, d], r.g1r.at[i, sender], self.device(h, self.mid, self.lo))

    def g2(self, i, mid):
        r, part = self.r, self.of("whole", i).at[:, mid, self.lo]
        return self.copy(part, part, r.g2s.at[i], r.g2r.at[i], self.device(self.h, 1 - self.mid, self.lo))

    def g3(self, i, lo):
        r, part = self.r, self.of("whole", i).at[:, :, lo]
        return self.copy(part, part, r.g3s.at[i], r.g3r.at[i], self.device(self.h, self.mid, 1 - self.lo))

    def gather_1(self, i):
        for d, h in enumerate(self.others()):
            self.g1(i, self.h, d, h).start()

    def gather_2(self, i):
        for d, h in enumerate(self.others()):
            self.g1(i, h, d, h).wait_recv()
        self.g2(i, self.mid).start()

    def gather_3(self, i):
        self.g2(i, 1 - self.mid).wait_recv()
        self.g3(i, self.lo).start()

    def gather_4(self, i):
        self.g3(i, 1 - self.lo).wait_recv()

    def gather_sent(self, i):
        for d, h in enumerate(self.others()):
            self.g1(i, self.h, d, h).wait_send()
        self.g2(i, self.mid).wait_send()
        self.g3(i, self.lo).wait_send()

    def own(self, i, h, mid):
        return self.of("acc", i).at[(h * 2 + mid) * 2 + self.lo]

    def s1(self, i):
        r = self.r
        return self.copy(
            self.of("snd", i), self.of("rcv1", i), r.s1s.at[i], r.s1r.at[i], self.device(self.h, self.mid, 1 - self.lo)
        )

    def s2(self, i):
        r = self.r
        return self.copy(
            self.of("snd", i).at[0], self.of("rcv2", i), r.s2s.at[i], r.s2r.at[i],
            self.device(self.h, 1 - self.mid, self.lo),
        )

    def s3(self, i, h, slot, d):
        r = self.r
        return self.copy(
            self.of("snd", i).at[1, h], self.of("rcv3", i).at[slot], r.s3s.at[i, d], r.s3r.at[i, slot],
            self.device(h, self.mid, self.lo),
        )

    def s4(self, i):
        r = self.r
        return self.copy(self.of("snd4", i), self.of("rcv4", i), r.s4s.at[i], r.s4r.at[i], {"tm": 1 - self.tm})

    def sum_1(self, i):
        acc, snd = self.of("acc", i), self.of("snd", i)
        for h in range(self.high):
            for mid in range(2):
                snd[mid, h] = acc[(h * 2 + mid) * 2 + 1 - self.lo].astype(bf16)
        self.s1(i).start()

    def sum_2(self, i):
        snd, rcv = self.of("snd", i), self.of("rcv1", i)
        self.s1(i).wait()
        for h in range(self.high):
            snd[0, h] = (self.own(i, h, 1 - self.mid)[...] + rcv[1 - self.mid, h].astype(f32)).astype(bf16)
        self.s2(i).start()
        for h in range(self.high):
            self.own(i, h, self.mid)[...] += rcv[self.mid, h].astype(f32)

    def sum_3(self, i):
        snd, rcv = self.of("snd", i), self.of("rcv2", i)
        self.s2(i).wait_recv()
        for d, h in enumerate(self.others()):
            snd[1, h] = (self.own(i, h, self.mid)[...] + rcv[h].astype(f32)).astype(bf16)
            self.s3(i, h, self.h, d).start()

    def sum_4(self, i):
        rcv = self.of("rcv3", i)
        total = self.own(i, self.h, self.mid)[...] + self.of("rcv2", i)[self.h].astype(f32)
        for d, h in enumerate(self.others()):
            self.s3(i, h, h, d).wait_recv()
            total = total + rcv[h].astype(f32)
        self.of("snd4", i)[...] = total.astype(bf16)
        self.s4(i).start()

    def sum_5(self, i):
        self.s4(i).wait_recv()
        return self.of("snd4", i)[...].astype(f32) + self.of("rcv4", i)[...].astype(f32)

    def sum_sent(self, i):
        self.s2(i).wait_send()
        for d, h in enumerate(self.others()):
            self.s3(i, h, self.h, d).wait_send()
        self.s4(i).wait_send()


def body(names, fused, n, part, *refs):
    r = SimpleNamespace()
    for key, ref in zip(names, refs, strict=True):
        setattr(r, key, ref)
    tm = lax.axis_index("tm")
    peer = {"tm": 1 - tm}
    table = r.table

    lengths = [r.frames[r.assign[m]] for m in range(MB)]
    first_head = iota((1, PW), 1) < 64
    row_ok = (iota((ROWS, 1), 0) < FT).astype(f32)
    pad = jnp.zeros((ROWS - FT, D), f32)

    def vector(name):
        return table[AT[name] : AT[name] + 1, :]

    def valid_of(m, j):
        return jnp.where(FD * tm + j < lengths[m], 1.0, 0.0).astype(f32)

    def valid_rows(j):
        return jnp.concatenate([row_ok * valid_of(m, j) for m in range(MB)], axis=0)

    def near_last(jj):
        return jj + tm * (FD - 1 - 2 * jj)

    def span(m):
        return slice(ROWS * m, ROWS * (m + 1))

    def run_steps(steps, t):
        if fused and t in steps:
            for stage, item in steps[t]:
                getattr(x, stage)(item)

    def steps_at(steps, p, t):
        for k in range(PAIRS):
            if fused and t in steps[k]:

                @pl.when(p == k)
                def _():
                    run_steps(steps[k], t)

    def spread_pairs(ref, j, rows, value):
        for p in range(PAIRS):
            ref[p, j, rows] = value[:, PW * p : PW * (p + 1)].astype(ref.dtype)

    def join_pairs(ref, j):
        return jnp.concatenate([ref[p, j] for p in range(PAIRS)], axis=1)

    def settle(i, rows=None):
        whole = x.of("whole", i)
        for k in range(n // 2):
            two = jnp.concatenate([whole[k // 2, k % 2, 0].astype(f32), whole[k // 2, k % 2, 1].astype(f32)], axis=0)
            r.weights[i, 2 * part * k : 2 * part * (k + 1)] = two.astype(bf16)

    gsm, qkv = r.gsm, r.qkv
    if fused:
        x = Exchange(r, n, part)
        h, mid, lo = x.h, x.mid, x.lo

    def prelude(raw):
        load_seen = pltpu.make_async_copy(r.visible, raw, r.local_sem.at[0])
        load_top = pltpu.make_async_copy(r.cotangent, raw, r.local_sem.at[0])
        load_seen.start()
        if fused:
            loads = []
            for p in range(PAIRS):
                for t in range(3):
                    c = D * t + PW * p
                    loads.append((r.w_qkv.at[:, c : c + PW], (p, slice(PW * t, PW * (t + 1)))))
            loads.append((r.w_out, (OUT, slice(None))))
            for c in range(CHUNKS):
                loads.append((r.w_down.at[part * c : part * (c + 1)], (DOWN + c, slice(None))))
            loads = [
                pltpu.make_async_copy(src, r.piece_whole.at[i, h, mid, lo, :, cols], r.local_sem.at[1 + k])
                for k, (src, (i, cols)) in enumerate(loads)
            ]
            for load in loads:
                load.start()
            r.rows[...] = jnp.zeros_like(r.rows)
            r.rows[0:8, :part] = r.time_embed[...].astype(f32)
            for i, name in enumerate(VECTORS):
                r.rows[8 + i : 9 + i, :part] = getattr(r, name)[...].astype(f32).reshape(1, part)
            up = r.bias_up[...].astype(f32).reshape(1, 4 * part)
            for c in range(CHUNKS):
                r.rows[UPB - TIME + c : UPB - TIME + c + 1, :part] = up[:, part * c : part * (c + 1)]
            r.cols[...] = jnp.zeros_like(r.cols)
            r.cols[:, :FT] = r.space_embed[...].astype(f32)
            r.cols[:, TIME : TIME + 32] = jnp.transpose(r.rows[...])[:part]
            r.small_whole[h, mid, lo] = r.cols[...].astype(bf16)
            x.greet()
            x.gather_1(SMALLS)
            for load in loads:
                load.wait()
            for i in (0, 1, 2, OUT):
                x.gather_1(i)
            up = r.w_up[...].astype(f32)
            for c in range(CHUNKS):
                for i in range(n):
                    at = part * (4 * i + c)
                    r.shuffle[c, :, part * i : part * (i + 1)] = up[:, at : at + part]
                r.piece_whole[UP + c, h, mid, lo] = r.shuffle[c].astype(bf16)
            for c in range(CHUNKS):
                x.gather_1(UP + c)
                x.gather_1(DOWN + c)
        else:
            barrier = pltpu.get_barrier_semaphore()
            pl.semaphore_signal(barrier, inc=1, device_id=peer, device_id_type=MESH)
            pl.semaphore_wait(barrier, 1)

        flags = r.mask_flags[...].astype(f32)
        r.flag_rows[...] = jnp.zeros_like(r.flag_rows)
        for m in range(MB):
            for j in range(FD):
                r.flag_rows[j : j + 1, ROWS * m : ROWS * m + FT] = flags[m : m + 1, FT * j : FT * (j + 1)]
        r.flag_cols[...] = jnp.transpose(r.flag_rows[...])

        def unpack(m, j):
            return jnp.concatenate([raw[m, FT * j : FT * (j + 1), :].astype(f32), pad], axis=0)

        load_seen.wait()
        for m in range(MB):
            for j in range(FD):
                r.x0s[j, span(m)] = unpack(m, j)
        load_top.start()
        if fused:
            x.gather_2(SMALLS)
            x.gather_2(0)
        gsm[...] = jnp.zeros_like(gsm)
        for m in range(MB):
            qkv[:, (FD + 1) * tm, m] = jnp.zeros((PAIRS, ROWS, D), bf16)
        if fused:
            x.gather_3(SMALLS)
            x.gather_2(1)
            x.gather_3(0)
        load_top.wait()
        for m in range(MB):
            for j in range(FD):
                spread_pairs(r.tops, j, span(m), unpack(m, j) * (row_ok * valid_of(m, j)))

    pl.run_scoped(prelude, pltpu.VMEM((MB, FD * FT, D), bf16))
    r.piece_acc[OUT] = jnp.zeros_like(r.piece_acc[OUT])
    if fused:
        x.gather_4(SMALLS)
        for k in range(n // 2):
            for e in range(2):
                r.small_acc[2 * k + e] = r.small_whole[k // 2, k % 2, e].astype(f32)
        table[...] = jnp.transpose(r.small_acc[...].reshape(D, SMALL))
    for p in range(PAIRS):
        for k, name in enumerate(("bias_query", "bias_value")):
            r.pair_bias[p, k : k + 1] = vector(name)[:, PW * p : PW * (p + 1)]

    blend = time_weights((NB, 8), 0, tm, lengths)
    total = jnp.zeros((NB, D), f32)
    for t in range(8):
        total = total + blend[:, t : t + 1] * table[TIME + t : TIME + t + 1, :]
    r.temporal[...] = total
    for j in range(FD):
        for m in range(MB):
            b = m * FD + j
            base = jnp.where(r.flag_cols[span(m), j : j + 1] > 0.5, vector("mask_token"), r.x0s[j, span(m)])
            base = base + r.temporal[b : b + 1, :] + table[:ROWS, :]
            x0 = base * (row_ok * valid_of(m, j))
            r.x0s[j, span(m)] = x0
            xhat, _ = norm_stats(x0)
            r.a1s[j, span(m)] = (xhat * vector("norm1_gain") + vector("norm1_bias")).astype(bf16)

    key = iota((1, WIN), 1)
    slot = (key >= ROWS).astype(jnp.int32) + (key >= 2 * ROWS).astype(jnp.int32)
    key_real = key - slot * ROWS < FT
    ones = jnp.ones((WIN, PW), bf16)

    def stack_heads(v):
        zero = jnp.zeros_like(v)
        return jnp.concatenate([jnp.where(first_head, v, zero), jnp.where(first_head, zero, v)], axis=0)

    def join_heads(v):
        return jnp.where(first_head, v[:ROWS], v[ROWS:])

    def window(p, m, j, k):
        return qkv[p, pl.ds(j, 3), m, :, PW * k : PW * (k + 1)].reshape(WIN, PW)

    def halo(p):
        cols = slice(PW, D)
        return pltpu.make_async_remote_copy(
            src_ref=qkv.at[p, FD - (FD - 1) * tm, :, :, cols], dst_ref=qkv.at[p, (FD + 1) * tm, :, :, cols],
            send_sem=r.halo_sem.at[0, p], recv_sem=r.halo_sem.at[1, p], device_id=peer, device_id_type=MESH,
        )

    def project(p):
        for jj in range(FD):
            j = near_last(FD - 1 - jj)
            y = contract(r.a1s[j], r.weights[p], 1, 0)
            q = (y[:, :PW] + r.pair_bias[p, 0:1]).astype(bf16).astype(f32)
            v = y[:, 2 * PW :] + r.pair_bias[p, 1:2]
            for m in range(MB):
                qkv[p, j + 1, m, :, :PW] = (q[span(m)] * 0.125).astype(bf16)
                qkv[p, j + 1, m, :, PW : 2 * PW] = y[span(m), PW : 2 * PW].astype(bf16)
                qkv[p, j + 1, m, :, 2 * PW :] = v[span(m)].astype(bf16)

    def prepare(p):
        if fused:
            x.gather_4(p)
            settle(p)
        project(p)

    def attend(p, probs, scale, steps):
        order = [(jj, m) for jj in range(FD) for m in range(MB)]
        scores = {}
        for t in range(NB + 2):
            steps_at(steps, p, t)
            if t < NB:
                jj, m = order[t]
                j = near_last(jj)
                if t == NB - MB:

                    @pl.when(p < PAIRS - 1)
                    def _():
                        prepare(p + 1)

                    halo(p).wait()

                    @pl.when(p < PAIRS - 1)
                    def _():
                        halo(p + 1).start()

                frame = FD * tm + j
                key_frame = frame - 1 + slot
                allowed = ((key_frame >= 0) & (key_frame < lengths[m])) | (frame >= lengths[m])
                bias = jnp.where(allowed & key_real, 0.0, NEG)
                scores[t] = contract(stack_heads(qkv[p, j + 1, m, :, :PW]), window(p, m, j, 1), 1, 1) + bias
            if 0 <= t - 1 < NB:
                jj, m = order[t - 1]
                s = scores.pop(t - 1)
                e = jnp.exp(s - jnp.max(s, axis=-1, keepdims=True))
                probs[p, near_last(jj), m] = e.astype(bf16)
            if 0 <= t - 2 < NB:
                jj, m = order[t - 2]
                j = near_last(jj)
                values = jnp.concatenate([window(p, m, j, 2), ones], axis=1)
                both = contract(probs[p, j, m], values, 1, 0)
                inverse = 1.0 / join_heads(both[:, PW:])
                r.os[p, j, span(m)] = join_heads(both[:, :PW]) * inverse
                scale[p, j, span(m)] = inverse

    def pieces(stage, *items):
        return [(stage, i) for i in items]

    U, W = UP, DOWN
    forward_steps = [
        {
            0: pieces("gather_2", 2, OUT) + pieces("gather_3", 1),
            4: pieces("gather_2", U),
            8: pieces("gather_2", W) + pieces("gather_3", 2),
        },
        {
            0: pieces("gather_2", U + 1) + pieces("gather_3", OUT),
            5: pieces("gather_2", W + 1) + pieces("gather_3", U),
        },
        {
            0: pieces("gather_2", U + 2) + pieces("gather_3", W),
            5: pieces("gather_2", W + 2) + pieces("gather_3", U + 1),
        },
    ]

    def add_grad(i, value, first=False):
        acc = r.piece_acc
        value = value.reshape(acc.shape[1:])
        acc[i] = value if first else acc[i] + value

    def small_grad(name, value):
        gsm[AT[name] : AT[name] + 1, :] += col_sum(value)

    def mix(j):
        o = join_pairs(r.os, j).astype(bf16)
        return o, r.x0s[j] + contract(o, r.weights[OUT], 1, 0) + vector("bias_out")

    def feed_start(j, x2s, ga2s, a2s):
        _, x1 = mix(j)
        xhat, _ = norm_stats(x1)
        a2s[j] = (xhat * vector("norm2_gain") + vector("norm2_bias")).astype(bf16)
        x2s[j] = x1 + vector("bias_down")
        ga2s[j] = jnp.zeros((BOTH, D), f32)

    def feed(c, x2s, ga2s, a2s):
        bias = table[pl.ds(UPB + c, 1), :]

        def products(j):
            g2 = join_pairs(r.tops, j)
            return contract(a2s[j], r.weights[UP + c], 1, 0) + bias, g2, contract(g2, r.weights[DOWN + c], 1, 1)

        bias_grad = jnp.zeros((1, D), f32)
        ready = products(0)
        for j in range(FD):
            u, g2, gz = ready
            if j + 1 < FD:
                ready = products(j + 1)
            if fused:
                if j == 2:

                    @pl.when(c > 0)
                    def _():
                        x.sum_2(UP + c - 1)
                        x.sum_2(DOWN + c - 1)

                if j == 1:

                    @pl.when(c == 0)
                    def _():
                        run_steps({1: pieces("gather_2", U + 3, W + 3) + pieces("gather_3", W + 1)}, 1)

                if j == 3:

                    @pl.when(c > 1)
                    def _():
                        x.sum_3(UP + c - 2)
                        x.sum_3(DOWN + c - 2)

                if j == 3:

                    @pl.when(c > 2)
                    def _():
                        x.sum_4(UP + c - 3)
                        x.sum_4(DOWN + c - 3)

                    @pl.when(c < CHUNKS - 2)
                    def _():
                        x.gather_3(UP + c + 2)
                        x.gather_3(DOWN + c + 2)

            cdf = 0.5 + 0.5 * lax.erf(u * (1.0 / math.sqrt(2.0)))
            pdf = jnp.exp(u * u * -0.5) * (1.0 / math.sqrt(2.0 * math.pi))
            z = (u * cdf).astype(bf16)
            gu = (gz * (cdf + u * pdf)).astype(bf16)
            bias_grad = bias_grad + col_sum(gu)
            x2s[j] += contract(z, r.weights[DOWN + c], 1, 0)
            ga2s[j] += contract(gu, r.weights[UP + c], 1, 1)
            add_grad(DOWN + c, contract(z, g2, 0, 0), j == 0)
            add_grad(UP + c, contract(a2s[j], gu, 0, 0), j == 0)
        gsm[pl.ds(UPB + c, 1), :] = bias_grad
        if fused:
            x.sum_1(UP + c)
            x.sum_1(DOWN + c)

    def feed_end(j, raw, scale, x2s, ga2s):
        o, x1 = mix(j)
        xhat, rstd = norm_stats(x1)
        y = (x2s[j] * valid_rows(j)).astype(bf16)
        for k in range(FD):

            @pl.when(j == k)
            def _():
                for m in range(MB):
                    raw[m, FT * k : FT * (k + 1), :] = y[ROWS * m : ROWS * m + FT]

        g2, ga2 = join_pairs(r.tops, j), ga2s[j]
        small_grad("bias_down", g2)
        small_grad("norm2_gain", ga2 * xhat)
        small_grad("norm2_bias", ga2)
        gx1 = g2.astype(f32) + norm_back(ga2, xhat, rstd, vector("norm2_gain"))
        gy = gx1.astype(bf16)
        small_grad("bias_out", gy)
        add_grad(OUT, contract(o, gy, 0, 0))
        go = contract(gy, r.weights[OUT], 1, 1).astype(bf16).astype(f32)
        spread_pairs(r.tops, j, slice(0, BOTH), go * join_pairs(scale, j))
        spread_pairs(r.gx1s, j, slice(0, BOTH), gx1)

    near = FD - (FD - 1) * tm
    away = (FD + 1) * (1 - tm)

    def back(p):
        return pltpu.make_async_remote_copy(
            src_ref=r.back_out, dst_ref=r.back_in.at[p],
            send_sem=r.back_sem.at[0, p], recv_sem=r.back_sem.at[1, p], device_id=peer, device_id_type=MESH,
        )

    def attend_back(p, probs, gkv, steps):
        gkv[...] = jnp.zeros_like(gkv)
        order = [(FD - 1 - jj, m) for jj in range(FD) for m in range(MB)]
        diffs, slopes = {}, {}
        for t in range(NB + 2):
            steps_at(steps, p, t)
            if t < NB:
                jj, m = order[t]
                j = near_last(jj)
                o = r.os[p, j, span(m)]
                go = stack_heads(r.tops[p, j, span(m)])
                delta = jnp.sum(go.astype(f32) * jnp.concatenate([o, o], axis=0), axis=-1, keepdims=True)
                diffs[t] = contract(go, window(p, m, j, 2), 1, 1) - delta
                gv = jnp.transpose(contract(go, probs[p, j, m], 0, 0)).reshape(3, ROWS, PW)
                gkv[pl.ds(j, 3), m, :, PW:] += gv
            if 0 <= t - 1 < NB:
                jj, m = order[t - 1]
                slopes[t - 1] = (probs[p, near_last(jj), m].astype(f32) * diffs.pop(t - 1)).astype(bf16)
            if 0 <= t - 2 < NB:
                jj, m = order[t - 2]
                j = near_last(jj)
                gs = slopes.pop(t - 2)
                q = stack_heads(qkv[p, j + 1, m, :, :PW])
                gk = jnp.transpose(contract(q, gs, 0, 0)).reshape(3, ROWS, PW)
                gkv[pl.ds(j, 3), m, :, :PW] += gk
                gq = join_heads(contract(gs, window(p, m, j, 1), 1, 0))
                qkv[p, j + 1, m, :, :PW] = (gq * 0.125).astype(bf16)
            if t == MB + 1:
                r.back_out[...] = gkv[away].astype(bf16)
                back(p).start()
        back(p).wait_send()

        @pl.when(p > 0)
        def _():
            complete(p - 1)

        r.near_acc[...] = gkv[near]
        qkv[p, 1 : FD + 1, :, :, PW:] = gkv[1 : FD + 1].astype(bf16)

    def complete(p):
        back(p).wait_recv()
        qkv[p, near, :, :, PW:] = (r.near_acc[...] + r.back_in[p].astype(f32)).astype(bf16)
        total = 0.0
        for j in range(FD):
            total = total + contract(r.a1s[j], qkv[p, j + 1].reshape(BOTH, D), 0, 0)
        r.piece_acc[p] = total.reshape(r.piece_acc.shape[1:])
        if fused:
            x.sum_1(p)

    backward_steps = [
        {
            1: pieces("sum_2", OUT),
            8: pieces("sum_3", U + 3, W + 3),
        },
        {
            0: pieces("sum_4", U + 2, W + 2),
            5: pieces("sum_3", OUT),
        },
        {
            1: pieces("sum_2", 0) + pieces("sum_4", U + 3, W + 3),
            8: pieces("sum_3", 0) + pieces("sum_4", OUT),
        },
    ]

    def middle(probs, raw):
        scale = r.gx1s

        def forward(p, carry):
            attend(p, probs, scale, forward_steps)
            return carry

        prepare(0)
        halo(0).start()
        lax.fori_loop(0, PAIRS, forward, 0)
        if fused:
            x.gather_4(OUT)
            settle(OUT)

        def feeding(x2s, ga2s, a2s):
            def start(j, carry):
                feed_start(j, x2s, ga2s, a2s)
                return carry

            def one(c, carry):
                if fused:
                    for i in (UP + c, DOWN + c):
                        x.gather_4(i)
                        settle(i)
                feed(c, x2s, ga2s, a2s)
                return carry

            def end(j, carry):
                feed_end(j, raw, scale, x2s, ga2s)
                return carry

            lax.fori_loop(0, FD, start, 0)
            lax.fori_loop(0, CHUNKS, one, 0)
            lax.fori_loop(0, 2, end, 0)
            run_steps({0: pieces("sum_2", U + 3, W + 3) + pieces("sum_3", U + 2, W + 2)}, 0)
            lax.fori_loop(2, FD, end, 0)
            pltpu.make_async_copy(raw, r.block_output, r.local_sem.at[0]).start()
            run_steps({0: pieces("sum_1", OUT) + pieces("sum_4", U + 1, W + 1)}, 0)

        pl.run_scoped(
            feeding, pltpu.VMEM((FD, BOTH, D), f32), pltpu.VMEM((FD, BOTH, D), f32), pltpu.VMEM((FD, BOTH, D), bf16)
        )

        def backward(gkv):
            def step(p, carry):
                attend_back(p, probs, gkv, backward_steps)
                return carry

            lax.fori_loop(0, PAIRS, step, 0)
            complete(PAIRS - 1)
            pltpu.make_async_copy(raw, r.block_output, r.local_sem.at[0]).wait()

        pl.run_scoped(backward, pltpu.VMEM((FD + 2, MB, ROWS, 2 * PW), f32))

    pl.run_scoped(
        middle, pltpu.VMEM((PAIRS, FD, MB, BOTH, WIN), bf16), pltpu.VMEM((MB, FD * FT, D), bf16)
    )

    final_steps = {
        0: pieces("sum_2", 1),
        1: pieces("sum_2", 2),
        3: pieces("sum_4", 0),
    }

    def last(gvis):
        for j in range(FD):
            run_steps(final_steps, j)
            xhat, rstd = norm_stats(r.x0s[j])
            ga1 = 0.0
            for p in range(PAIRS):
                gp = qkv[p, j + 1].reshape(BOTH, D)
                sums = col_sum(gp)
                cols = slice(PW * p, PW * (p + 1))
                gsm[AT["bias_query"] : AT["bias_query"] + 1, cols] += sums[:, :PW]
                gsm[AT["bias_value"] : AT["bias_value"] + 1, cols] += sums[:, 2 * PW :]
                ga1 = ga1 + contract(gp, r.weights[p], 1, 1)
            small_grad("norm1_gain", ga1 * xhat)
            small_grad("norm1_bias", ga1)
            gb = (join_pairs(r.gx1s, j) + norm_back(ga1, xhat, rstd, vector("norm1_gain"))) * valid_rows(j)
            masked = r.flag_cols[:BOTH, j : j + 1] > 0.5
            small_grad("mask_token", jnp.where(masked, gb, 0.0))
            seen = jnp.where(masked, 0.0, gb)
            for m in range(MB):
                gsm[:ROWS, :] += gb[span(m)]
                r.sumgb[m * FD + j : m * FD + j + 1, :] = col_sum(gb[span(m)])
                gvis[m, FT * j : FT * (j + 1), :] = seen[ROWS * m : ROWS * m + FT]
        store_seen = pltpu.make_async_copy(gvis, r.grad_visible, r.local_sem.at[0])
        store_seen.start()
        blend = time_weights((8, NB), 1, tm, lengths)
        total = jnp.zeros((8, D), f32)
        for b in range(NB):
            total = total + blend[:, b : b + 1] * r.sumgb[b : b + 1, :]
        gsm[TIME : TIME + 8, :] = total
        if fused:
            r.small_acc[...] = jnp.transpose(gsm[...]).reshape(r.small_acc.shape)
            x.sum_1(SMALLS)
            x.sum_3(1)
            x.sum_2(SMALLS)
            x.sum_3(2)
            for c in range(CHUNKS):
                share = x.sum_5(UP + c)
                for i in range(n):
                    at = part * (4 * i + c)
                    r.grad_w_up[:, at : at + part] = share[:, part * i : part * (i + 1)]
                r.grad_w_down[part * c : part * (c + 1)] = x.sum_5(DOWN + c)
            r.grad_w_out[...] = x.sum_5(OUT)
            x.sum_3(SMALLS)
            x.sum_4(1)
            x.sum_4(2)
            for p in range(PAIRS):
                share = x.sum_5(p)
                for t in range(3):
                    c = D * t + PW * p
                    r.grad_w_qkv[:, c : c + PW] = share[:, PW * t : PW * (t + 1)]
            x.sum_4(SMALLS)
            r.grad_small[...] = x.sum_5(SMALLS)
        store_seen.wait()
        if fused:

            def sent(i, carry):
                x.gather_sent(i)
                x.sum_sent(i)
                return carry

            lax.fori_loop(0, PIECES, sent, 0)
            x.gather_sent(SMALLS)
            x.sum_sent(SMALLS)

    pl.run_scoped(last, pltpu.VMEM((MB, FD * FT, D), f32))


def unpack_body(names, part, *refs):
    r = SimpleNamespace(**dict(zip(names, refs, strict=True)))
    parts = [(r.out_in.at[m], r.buf_block.at[m], r.block_output.at[m]) for m in range(MB)]
    parts += [
        (r.seen_in.at[m, rows], r.buf_seen.at[m, rows], r.grad_visible.at[m, rows])
        for m in range(MB)
        for rows in (slice(0, FD * FT // 2), slice(FD * FT // 2, FD * FT))
    ]
    parts += [
        (getattr(r, "w_%s_in" % name), getattr(r, "buf_" + name), getattr(r, "grad_w_" + name))
        for name in ("qkv", "out", "up", "down")
    ]
    loads = [pltpu.make_async_copy(src, buf, r.sem.at[0, i]) for i, (src, buf, _) in enumerate(parts)]
    stores = [pltpu.make_async_copy(buf, dst, r.sem.at[1, i]) for i, (_, buf, dst) in enumerate(parts)]
    load_small = pltpu.make_async_copy(r.small_in, r.buf_small, r.small_sem)
    load_small.start()
    for load in loads:
        load.start()
    load_small.wait()
    small = r.buf_small[...]
    r.tmp_space_embed[...] = small[:, :FT]
    r.wide[:part] = small
    rows = jnp.transpose(r.wide[:, PW:])
    r.tmp_time_embed[...] = rows[TIME - PW : TIME - PW + 8, :part]
    for name in VECTORS:
        at = AT[name] - PW
        getattr(r, "tmp_" + name)[...] = rows[at : at + 1, :part].reshape(part)
    for c in range(CHUNKS):
        r.line[0:1, part * c : part * (c + 1)] = rows[UPB + c - PW : UPB + c + 1 - PW, :part]
    r.tmp_bias_up[...] = r.line[0:1, : 4 * part].reshape(4 * part)
    tables = ("space_embed", "time_embed", "bias_up") + VECTORS
    hand_on = [
        pltpu.make_async_copy(getattr(r, "tmp_" + name), getattr(r, "grad_" + name), r.table_sem.at[i])
        for i, name in enumerate(tables)
    ]
    for copy in hand_on:
        copy.start()
    for load, store in zip(loads, stores):
        load.wait()
        store.start()
    for store in stores + hand_on:
        store.wait()


def call(fused, n, part, inputs, outputs, scratch, arrays):
    smem = pl.BlockSpec(memory_space=pltpu.SMEM)
    vmem = pl.BlockSpec(memory_space=pltpu.VMEM)
    hbm = pl.BlockSpec(memory_space=pl.ANY)
    spec = {"s": smem, "v": vmem, "h": hbm}
    names = list(inputs) + list(outputs) + list(scratch)
    return pl.pallas_call(
        functools.partial(body, names, fused, n, part),
        out_shape=tuple(shape for shape, _ in outputs.values()),
        in_specs=[spec[where] for where in inputs.values()],
        out_specs=tuple(spec[where] for _, where in outputs.values()),
        scratch_shapes=list(scratch.values()),
        compiler_params=pltpu.CompilerParams(
            collective_id=0, has_side_effects=True, vmem_limit_bytes=64 * 2**20 - 2**16
        ),
    )(*arrays)


def common_scratch():
    V, S = pltpu.VMEM, pltpu.SemaphoreType.DMA
    return {
        "flag_rows": V((8, 512), f32),
        "flag_cols": V((512, 8), f32),
        "pair_bias": V((PAIRS, 8, PW), f32),
        "x0s": V((FD, BOTH, D), f32),
        "gx1s": V((PAIRS, FD, BOTH, PW), f32),
        "tops": V((PAIRS, FD, BOTH, PW), bf16),
        "os": V((PAIRS, FD, BOTH, PW), f32),
        "a1s": V((FD, BOTH, D), bf16),
        "qkv": V((PAIRS, FD + 2, MB, ROWS, D), bf16),
        "temporal": V((NB, D), f32),
        "sumgb": V((NB, D), f32),
        "back_out": V((MB, ROWS, 2 * PW), bf16),
        "back_in": V((PAIRS, MB, ROWS, 2 * PW), bf16),
        "near_acc": V((MB, ROWS, 2 * PW), f32),
        "halo_sem": S((2, PAIRS)),
        "back_sem": S((2, PAIRS)),
        "local_sem": S((24,)),
    }


def whole_weights(shards, part):
    s = shards
    small = jnp.concatenate(
        [s.space_embed.T, jnp.zeros((part, TIME - FT), bf16), s.time_embed.T]
        + [getattr(s, name)[:, None] for name in VECTORS]
        + [s.bias_up.reshape(part, 4), jnp.zeros((part, SMALL - UPB - 4), bf16)],
        axis=1,
    )
    pairs = [s.w_qkv[:, D * t + PW * p : D * t + PW * (p + 1)] for p in range(PAIRS) for t in range(3)]
    pack = jnp.concatenate(pairs + [s.w_out, s.w_up, s.w_down.reshape(part, FF), small], axis=1)
    return lax.all_gather(pack, "clip", axis=0, tiled=True)


def local(*args):
    keys = (
        "visible", "mask_flags", "frames", "assign", "cotangent", "mask_token", "time_embed", "space_embed",
        "norm1_gain", "norm1_bias", "w_qkv", "bias_query", "bias_value", "w_out", "bias_out", "norm2_gain",
        "norm2_bias", "w_up", "bias_up", "w_down", "bias_down",
    )
    a = SimpleNamespace(**dict(zip(keys, args, strict=True)))
    n = lax.axis_size("clip")
    part = D // n
    V, S, sds = pltpu.VMEM, pltpu.SemaphoreType.DMA, jax.ShapeDtypeStruct
    scratch = common_scratch()
    big = {"block_output": (sds(a.visible.shape, bf16), "h"), "grad_visible": (sds(a.visible.shape, f32), "h")}

    if part % 8 == 0 and n % 16 == 0:
        high = n // 4
        a.assign = a.assign.reshape(MB)
        a.space_embed = a.space_embed.T
        inputs = {key: "v" for key in keys}
        inputs.update(frames="s", assign="s", visible="h", cotangent="h", w_qkv="h", w_out="h", w_down="h")
        grads = {"grad_" + key: sds(getattr(a, key).shape, f32) for key in keys[5:]}
        outputs = dict(big)
        for key in ("grad_w_qkv", "grad_w_out", "grad_w_up", "grad_w_down"):
            outputs[key] = (grads[key], "v")
        outputs["grad_small"] = (sds((part, SMALL), f32), "v")
        scratch.update(
            {
                "rows": V((32, PW), f32),
                "cols": V((part, SMALL), f32),
                "table": V((SMALL, D), f32),
                "shuffle": V((CHUNKS, part, D), f32),
                "weights": V((PIECES, D, D), bf16),
                "gsm": V((SMALL, D), f32),
            }
        )
        for kind, count, width in (("piece_", (PIECES,), D), ("small_", (), SMALL)):
            scratch[kind + "whole"] = V((*count, high, 2, 2, part, width), bf16)
            scratch[kind + "acc"] = V((*count, n, part, width), f32)
            for key, lead in (("snd", (2, high)), ("rcv1", (2, high)), ("rcv2", (high,)), ("rcv3", (high,)), ("snd4", ()), ("rcv4", ())):
                scratch[kind + key] = V((*count, *lead, part, width), bf16)
        for key in ("g2s", "g2r", "g3s", "g3r", "s1s", "s1r", "s2s", "s2r", "s4s", "s4r"):
            scratch[key] = S((PIECES + 1,))
        for key in ("g1s", "g1r", "s3s", "s3r"):
            scratch[key] = S((PIECES + 1, high))
        results = call(True, n, part, inputs, outputs, scratch, [getattr(a, key) for key in keys])
        where = ["h"] * 7
        finals = {"block_output": big["block_output"], "grad_visible": big["grad_visible"]}
        finals.update({key: (shape, "h") for key, shape in grads.items()})
        names = ["out_in", "seen_in", "w_qkv_in", "w_out_in", "w_up_in", "w_down_in", "small_in"]
        spec = {"v": pl.BlockSpec(memory_space=pltpu.VMEM), "h": pl.BlockSpec(memory_space=pl.ANY)}
        held = {"wide": V((PW, SMALL), f32), "line": V((8, 4 * part), f32), "sem": S((2, 10))}
        for name, key in (("out", "w_out"), ("qkv", "w_qkv"), ("up", "w_up"), ("down", "w_down")):
            held["buf_" + name] = V(grads["grad_" + key].shape, f32)
        for key, shape in grads.items():
            if "_w_" not in key:
                held["tmp_" + key[5:]] = V(shape.shape, f32)
        held.update({"buf_small": V((part, SMALL), f32), "small_sem": S(()), "table_sem": S((len(grads),))})
        held["buf_block"] = V(a.visible.shape, bf16)
        held["buf_seen"] = V(a.visible.shape, f32)
        final = pl.pallas_call(
            functools.partial(unpack_body, names + list(finals) + list(held), part),
            out_shape=tuple(shape for shape, _ in finals.values()),
            in_specs=[spec[w] for w in where],
            out_specs=tuple(spec[w] for _, w in finals.values()),
            scratch_shapes=list(held.values()),
        )(*results)
        final = dict(zip(finals, final, strict=True))
        final["grad_space_embed"] = final["grad_space_embed"].T
        return tuple(final.values())

    whole = whole_weights(a, part)
    cuts = (0, 3 * D, 4 * D, 4 * D + FF, 4 * D + 2 * FF, 4 * D + 2 * FF + SMALL)
    wqkv, wout, wup, wdown, wsmall = (whole[:, i:j] for i, j in zip(cuts[:-1], cuts[1:]))
    values = {
        "frames": a.frames, "assign": a.assign.reshape(MB), "visible": a.visible, "mask_flags": a.mask_flags,
        "cotangent": a.cotangent,
        "table": wsmall.T.at[UPB : UPB + 4].set(wsmall[:, UPB : UPB + 4].reshape(CHUNKS, HIDDEN)).astype(f32),
        "weights": jnp.stack(
            [wqkv[:, D * p : D * (p + 1)] for p in range(PAIRS)]
            + [wout]
            + [wup[:, HIDDEN * c : HIDDEN * (c + 1)] for c in range(CHUNKS)]
            + list(wdown.reshape(CHUNKS, HIDDEN, D))
        ),
    }
    inputs = {key: "v" for key in values}
    inputs.update(frames="s", assign="s", visible="h", cotangent="h")
    outputs = dict(big)
    outputs["piece_acc"] = (sds((PIECES, 1, D, D), f32), "v")
    outputs["gsm"] = (sds((SMALL, D), f32), "v")
    out, gvis, gpieces, gsm = call(False, n, part, inputs, outputs, scratch, list(values.values()))
    gpieces = gpieces[:, 0]
    gdown = gpieces[DOWN:].reshape(D, FF)
    gsmall = gsm.T.at[:, UPB : UPB + 4].set(gsm[UPB : UPB + 4].reshape(D, 4))
    grads = jnp.concatenate([*gpieces[:DOWN], gdown, gsmall], axis=1)
    share = lax.psum_scatter(grads, "clip", scatter_dimension=0, tiled=True)
    share = lax.psum(share.astype(bf16), "tm").astype(f32)
    sqkv, sout, sup, sdown, ssmall = (share[:, i:j] for i, j in zip(cuts[:-1], cuts[1:]))
    sqkv = jnp.concatenate(
        [sqkv[:, D * p + PW * t : D * p + PW * (t + 1)] for t in range(3) for p in range(PAIRS)], axis=1
    )
    one = {name: ssmall[:, AT[name]] for name in VECTORS}
    return (
        out, gvis, one["mask_token"], ssmall[:, TIME : TIME + 8].T, ssmall[:, :FT].T, one["norm1_gain"],
        one["norm1_bias"], sqkv, one["bias_query"], one["bias_value"], sout, one["bias_out"], one["norm2_gain"],
        one["norm2_bias"], sup, ssmall[:, UPB : UPB + 4].reshape(-1), sdown.reshape(-1, D), one["bias_down"],
    )


def solution(mesh):
    rows = P(None, ("clip", "tm"), None)
    vec = P("clip")
    mat = P("clip", None)
    cols = P(None, "clip")
    in_specs = (
        rows, P(None, ("clip", "tm")), P(), cols, rows,
        vec, cols, cols, vec, vec, mat, vec, vec, mat, vec, vec, vec, mat, vec, mat, vec,
    )
    out_specs = (
        rows, rows, vec, cols, cols, vec, vec, mat, vec, vec, mat, vec, vec, vec, mat, vec, mat, vec,
    )
    return jax.shard_map(local, mesh=mesh, in_specs=in_specs, out_specs=out_specs, check_vma=False)
```

```python
import functools
import math
from types import SimpleNamespace

import jax
import jax.numpy as jnp
from jax import lax
from jax.experimental import pallas as pl
from jax.experimental.pallas import tpu as pltpu
from jax.sharding import PartitionSpec as P

D = 384
FF = 1536
FT = 196
FD = 4
MB = 2
NB = MB * FD
ROWS = 208
BOTH = MB * ROWS
WIN = 3 * ROWS
EPS = 1e-06
NEG = -1000000000.0
PAIRS = 3
PW = 128
SMALL = 256
TIME = 208
VEC = 216
UPB = 225
MESH = pl.DeviceIdType.MESH
f32 = jnp.float32
bf16 = jnp.bfloat16

OUT = 3
UP = 4
DOWN = 8
PIECES = 12
SMALLS = PIECES
HIDDEN = 384
CHUNKS = FF // HIDDEN
VECTORS = (
    "mask_token", "norm1_gain", "norm1_bias", "bias_query", "bias_value", "bias_out", "norm2_gain", "norm2_bias",
    "bias_down",
)
AT = {name: VEC + i for i, name in enumerate(VECTORS)}


def contract(a, b, ca, cb, precision=None):
    return lax.dot_general(
        a, b, (((ca,), (cb,)), ((), ())), preferred_element_type=f32, precision=precision
    )


def norm_stats(x):
    c = x - jnp.mean(x, axis=-1, keepdims=True)
    r = lax.rsqrt(jnp.mean(c * c, axis=-1, keepdims=True) + EPS)
    return c * r, r


def norm_back(g, xhat, r, gain):
    d = g * gain
    first = jnp.mean(d, axis=-1, keepdims=True)
    second = jnp.mean(d * xhat, axis=-1, keepdims=True)
    return r * (d - first - xhat * second)


def col_sum(x):
    return jnp.sum(x.astype(f32), axis=0, keepdims=True)


def iota(shape, dim):
    return lax.broadcasted_iota(jnp.int32, shape, dim)


def time_weights(shape, frame_dim, tm, lengths):
    block = iota(shape, frame_dim)
    row = iota(shape, 1 - frame_dim).astype(f32)
    length = jnp.where(block < FD, lengths[0].astype(f32), lengths[1].astype(f32))
    frame = (jnp.where(block < FD, block, block - FD) + FD * tm).astype(f32)
    den = jnp.maximum(length - 1.0, 1.0)
    num = frame * 7.0
    whole = jnp.floor((num + 0.5) / den)
    low = jnp.minimum(whole, 7.0)
    high = jnp.minimum(low + 1.0, 7.0)
    part = (num - whole * den) / den
    return jnp.where(row == low, 1.0 - part, 0.0) + jnp.where(row == high, part, 0.0)


class Exchange:
    def __init__(self, r, n, part):
        self.r, self.high, self.part = r, n // 4, part
        me = lax.axis_index("clip")
        self.tm = lax.axis_index("tm")
        self.h, self.mid, self.lo = me // 4, (me // 2) % 2, me % 2

    def device(self, h, mid, lo):
        return {"clip": (h * 2 + mid) * 2 + lo}

    def others(self):
        return [(self.h + d) % self.high for d in range(1, self.high)]

    def greet(self):
        barrier = pltpu.get_barrier_semaphore()
        peers = [self.device(h, self.mid, self.lo) for h in self.others()]
        peers += [self.device(self.h, 1 - self.mid, self.lo), self.device(self.h, self.mid, 1 - self.lo)]
        peers.append({"tm": 1 - self.tm})
        for peer in peers:
            pl.semaphore_signal(barrier, inc=1, device_id=peer, device_id_type=MESH)
        pl.semaphore_wait(barrier, len(peers))

    def copy(self, src, dst, send, recv, device):
        return pltpu.make_async_remote_copy(
            src_ref=src, dst_ref=dst, send_sem=send, recv_sem=recv, device_id=device, device_id_type=MESH
        )

    def of(self, key, i):
        if isinstance(i, int) and i == SMALLS:
            return getattr(self.r, "small_" + key)
        return getattr(self.r, "piece_" + key).at[i]

    def g1(self, i, sender, d, h):
        r, slot = self.r, self.of("whole", i).at[sender, self.mid, self.lo]
        return self.copy(slot, slot, r.g1s.at[i, d], r.g1r.at[i, sender], self.device(h, self.mid, self.lo))

    def g2(self, i, mid):
        r, part = self.r, self.of("whole", i).at[:, mid, self.lo]
        return self.copy(part, part, r.g2s.at[i], r.g2r.at[i], self.device(self.h, 1 - self.mid, self.lo))

    def g3(self, i, lo):
        r, part = self.r, self.of("whole", i).at[:, :, lo]
        return self.copy(part, part, r.g3s.at[i], r.g3r.at[i], self.device(self.h, self.mid, 1 - self.lo))

    def gather_1(self, i):
        for d, h in enumerate(self.others()):
            self.g1(i, self.h, d, h).start()

    def gather_2(self, i):
        for d, h in enumerate(self.others()):
            self.g1(i, h, d, h).wait_recv()
        self.g2(i, self.mid).start()

    def gather_3(self, i):
        self.g2(i, 1 - self.mid).wait_recv()
        self.g3(i, self.lo).start()

    def gather_4(self, i):
        self.g3(i, 1 - self.lo).wait_recv()

    def gather_sent(self, i):
        for d, h in enumerate(self.others()):
            self.g1(i, self.h, d, h).wait_send()
        self.g2(i, self.mid).wait_send()
        self.g3(i, self.lo).wait_send()

    def own(self, i, h, mid):
        return self.of("acc", i).at[(h * 2 + mid) * 2 + self.lo]

    def s1(self, i):
        r = self.r
        return self.copy(
            self.of("snd", i), self.of("rcv1", i), r.s1s.at[i], r.s1r.at[i], self.device(self.h, self.mid, 1 - self.lo)
        )

    def s2(self, i):
        r = self.r
        return self.copy(
            self.of("snd", i).at[0], self.of("rcv2", i), r.s2s.at[i], r.s2r.at[i],
            self.device(self.h, 1 - self.mid, self.lo),
        )

    def s3(self, i, h, slot, d):
        r = self.r
        return self.copy(
            self.of("snd", i).at[1, h], self.of("rcv3", i).at[slot], r.s3s.at[i, d], r.s3r.at[i, slot],
            self.device(h, self.mid, self.lo),
        )

    def s4(self, i):
        r = self.r
        return self.copy(self.of("snd4", i), self.of("rcv4", i), r.s4s.at[i], r.s4r.at[i], {"tm": 1 - self.tm})

    def sum_1(self, i):
        acc, snd = self.of("acc", i), self.of("snd", i)
        for h in range(self.high):
            for mid in range(2):
                snd[mid, h] = acc[(h * 2 + mid) * 2 + 1 - self.lo].astype(bf16)
        self.s1(i).start()

    def sum_2(self, i):
        snd, rcv = self.of("snd", i), self.of("rcv1", i)
        self.s1(i).wait()
        for h in range(self.high):
            snd[0, h] = (self.own(i, h, 1 - self.mid)[...] + rcv[1 - self.mid, h].astype(f32)).astype(bf16)
        self.s2(i).start()
        for h in range(self.high):
            self.own(i, h, self.mid)[...] += rcv[self.mid, h].astype(f32)

    def sum_3(self, i):
        snd, rcv = self.of("snd", i), self.of("rcv2", i)
        self.s2(i).wait_recv()
        for d, h in enumerate(self.others()):
            snd[1, h] = (self.own(i, h, self.mid)[...] + rcv[h].astype(f32)).astype(bf16)
            self.s3(i, h, self.h, d).start()

    def sum_4(self, i):
        rcv = self.of("rcv3", i)
        total = self.own(i, self.h, self.mid)[...] + self.of("rcv2", i)[self.h].astype(f32)
        for d, h in enumerate(self.others()):
            self.s3(i, h, h, d).wait_recv()
            total = total + rcv[h].astype(f32)
        self.of("snd4", i)[...] = total.astype(bf16)
        self.s4(i).start()

    def sum_5(self, i):
        self.s4(i).wait_recv()
        return self.of("snd4", i)[...].astype(f32) + self.of("rcv4", i)[...].astype(f32)

    def sum_sent(self, i):
        self.s2(i).wait_send()
        for d, h in enumerate(self.others()):
            self.s3(i, h, self.h, d).wait_send()
        self.s4(i).wait_send()


def body(names, fused, n, part, *refs):
    r = SimpleNamespace()
    for key, ref in zip(names, refs, strict=True):
        setattr(r, key, ref)
    tm = lax.axis_index("tm")
    peer = {"tm": 1 - tm}
    table = r.table

    lengths = [r.frames[r.assign[m]] for m in range(MB)]
    first_head = iota((1, PW), 1) < 64
    row_ok = (iota((ROWS, 1), 0) < FT).astype(f32)
    pad = jnp.zeros((ROWS - FT, D), f32)

    def vector(name):
        return table[AT[name] : AT[name] + 1, :]

    def valid_of(m, j):
        return jnp.where(FD * tm + j < lengths[m], 1.0, 0.0).astype(f32)

    def valid_rows(j):
        return jnp.concatenate([row_ok * valid_of(m, j) for m in range(MB)], axis=0)

    def near_last(jj):
        return jj + tm * (FD - 1 - 2 * jj)

    def span(m):
        return slice(ROWS * m, ROWS * (m + 1))

    def run_steps(steps, t):
        if fused and t in steps:
            for stage, item in steps[t]:
                getattr(x, stage)(item)

    def steps_at(steps, p, t):
        for k in range(PAIRS):
            if fused and t in steps[k]:

                @pl.when(p == k)
                def _():
                    run_steps(steps[k], t)

    def spread_pairs(ref, j, rows, value):
        for p in range(PAIRS):
            ref[p, j, rows] = value[:, PW * p : PW * (p + 1)].astype(ref.dtype)

    def join_pairs(ref, j):
        return jnp.concatenate([ref[p, j] for p in range(PAIRS)], axis=1)

    def settle(i, rows=None):
        whole = x.of("whole", i)
        for k in range(n // 2):
            two = jnp.concatenate([whole[k // 2, k % 2, 0].astype(f32), whole[k // 2, k % 2, 1].astype(f32)], axis=0)
            r.weights[i, 2 * part * k : 2 * part * (k + 1)] = two.astype(bf16)

    gsm, qkv = r.gsm, r.qkv
    if fused:
        x = Exchange(r, n, part)
        h, mid, lo = x.h, x.mid, x.lo

    def prelude(raw):
        load_seen = pltpu.make_async_copy(r.visible, raw, r.local_sem.at[0])
        load_top = pltpu.make_async_copy(r.cotangent, raw, r.local_sem.at[0])
        load_seen.start()
        if fused:
            loads = []
            for p in range(PAIRS):
                for t in range(3):
                    c = D * t + PW * p
                    loads.append((r.w_qkv.at[:, c : c + PW], (p, slice(PW * t, PW * (t + 1)))))
            loads.append((r.w_out, (OUT, slice(None))))
            for c in range(CHUNKS):
                loads.append((r.w_down.at[part * c : part * (c + 1)], (DOWN + c, slice(None))))
            loads = [
                pltpu.make_async_copy(src, r.piece_whole.at[i, h, mid, lo, :, cols], r.local_sem.at[1 + k])
                for k, (src, (i, cols)) in enumerate(loads)
            ]
            for load in loads:
                load.start()
            r.rows[...] = jnp.zeros_like(r.rows)
            r.rows[0:8, :part] = r.time_embed[...].astype(f32)
            for i, name in enumerate(VECTORS):
                r.rows[8 + i : 9 + i, :part] = getattr(r, name)[...].astype(f32).reshape(1, part)
            up = r.bias_up[...].astype(f32).reshape(1, 4 * part)
            for c in range(CHUNKS):
                r.rows[UPB - TIME + c : UPB - TIME + c + 1, :part] = up[:, part * c : part * (c + 1)]
            r.cols[...] = jnp.zeros_like(r.cols)
            r.cols[:, :FT] = r.space_embed[...].astype(f32)
            r.cols[:, TIME : TIME + 32] = jnp.transpose(r.rows[...])[:part]
            r.small_whole[h, mid, lo] = r.cols[...].astype(bf16)
            x.greet()
            x.gather_1(SMALLS)
            for load in loads:
                load.wait()
            for i in (0, 1, 2, OUT):
                x.gather_1(i)
            up = r.w_up[...].astype(f32)
            for c in range(CHUNKS):
                for i in range(n):
                    at = part * (4 * i + c)
                    r.shuffle[c, :, part * i : part * (i + 1)] = up[:, at : at + part]
                r.piece_whole[UP + c, h, mid, lo] = r.shuffle[c].astype(bf16)
            for c in range(CHUNKS):
                x.gather_1(UP + c)
                x.gather_1(DOWN + c)
        else:
            barrier = pltpu.get_barrier_semaphore()
            pl.semaphore_signal(barrier, inc=1, device_id=peer, device_id_type=MESH)
            pl.semaphore_wait(barrier, 1)

        flags = r.mask_flags[...].astype(f32)
        r.flag_rows[...] = jnp.zeros_like(r.flag_rows)
        for m in range(MB):
            for j in range(FD):
                r.flag_rows[j : j + 1, ROWS * m : ROWS * m + FT] = flags[m : m + 1, FT * j : FT * (j + 1)]
        r.flag_cols[...] = jnp.transpose(r.flag_rows[...])

        def unpack(m, j):
            return jnp.concatenate([raw[m, FT * j : FT * (j + 1), :].astype(f32), pad], axis=0)

        load_seen.wait()
        for m in range(MB):
            for j in range(FD):
                r.x0s[j, span(m)] = unpack(m, j)
        load_top.start()
        if fused:
            x.gather_2(SMALLS)
            x.gather_2(0)
        gsm[...] = jnp.zeros_like(gsm)
        for m in range(MB):
            qkv[:, (FD + 1) * tm, m] = jnp.zeros((PAIRS, ROWS, D), bf16)
        if fused:
            x.gather_3(SMALLS)
            x.gather_2(1)
            x.gather_3(0)
        load_top.wait()
        for m in range(MB):
            for j in range(FD):
                spread_pairs(r.tops, j, span(m), unpack(m, j) * (row_ok * valid_of(m, j)))

    pl.run_scoped(prelude, pltpu.VMEM((MB, FD * FT, D), bf16))
    r.piece_acc[OUT] = jnp.zeros_like(r.piece_acc[OUT])
    if fused:
        x.gather_4(SMALLS)
        for k in range(n // 2):
            for e in range(2):
                r.small_acc[2 * k + e] = r.small_whole[k // 2, k % 2, e].astype(f32)
        table[...] = jnp.transpose(r.small_acc[...].reshape(D, SMALL))
    for p in range(PAIRS):
        for k, name in enumerate(("bias_query", "bias_value")):
            r.pair_bias[p, k : k + 1] = vector(name)[:, PW * p : PW * (p + 1)]

    blend = time_weights((NB, 8), 0, tm, lengths)
    total = jnp.zeros((NB, D), f32)
    for t in range(8):
        total = total + blend[:, t : t + 1] * table[TIME + t : TIME + t + 1, :]
    r.temporal[...] = total
    for j in range(FD):
        for m in range(MB):
            b = m * FD + j
            base = jnp.where(r.flag_cols[span(m), j : j + 1] > 0.5, vector("mask_token"), r.x0s[j, span(m)])
            base = base + r.temporal[b : b + 1, :] + table[:ROWS, :]
            x0 = base * (row_ok * valid_of(m, j))
            r.x0s[j, span(m)] = x0
            xhat, _ = norm_stats(x0)
            r.a1s[j, span(m)] = (xhat * vector("norm1_gain") + vector("norm1_bias")).astype(bf16)

    key = iota((1, WIN), 1)
    slot = (key >= ROWS).astype(jnp.int32) + (key >= 2 * ROWS).astype(jnp.int32)
    key_real = key - slot * ROWS < FT
    ones = jnp.ones((WIN, PW), bf16)

    def stack_heads(v):
        zero = jnp.zeros_like(v)
        return jnp.concatenate([jnp.where(first_head, v, zero), jnp.where(first_head, zero, v)], axis=0)

    def join_heads(v):
        return jnp.where(first_head, v[:ROWS], v[ROWS:])

    def window(p, m, j, k):
        return qkv[p, pl.ds(j, 3), m, :, PW * k : PW * (k + 1)].reshape(WIN, PW)

    def halo(p):
        cols = slice(PW, D)
        return pltpu.make_async_remote_copy(
            src_ref=qkv.at[p, FD - (FD - 1) * tm, :, :, cols], dst_ref=qkv.at[p, (FD + 1) * tm, :, :, cols],
            send_sem=r.halo_sem.at[0, p], recv_sem=r.halo_sem.at[1, p], device_id=peer, device_id_type=MESH,
        )

    def project(p):
        for jj in range(FD):
            j = near_last(FD - 1 - jj)
            y = contract(r.a1s[j], r.weights[p], 1, 0)
            q = (y[:, :PW] + r.pair_bias[p, 0:1]).astype(bf16).astype(f32)
            v = y[:, 2 * PW :] + r.pair_bias[p, 1:2]
            for m in range(MB):
                qkv[p, j + 1, m, :, :PW] = (q[span(m)] * 0.125).astype(bf16)
                qkv[p, j + 1, m, :, PW : 2 * PW] = y[span(m), PW : 2 * PW].astype(bf16)
                qkv[p, j + 1, m, :, 2 * PW :] = v[span(m)].astype(bf16)

    def prepare(p):
        if fused:
            x.gather_4(p)
            settle(p)
        project(p)

    def attend(p, probs, scale, steps):
        order = [(jj, m) for jj in range(FD) for m in range(MB)]
        scores = {}
        for t in range(NB + 2):
            steps_at(steps, p, t)
            if t < NB:
                jj, m = order[t]
                j = near_last(jj)
                if t == NB - MB:

                    @pl.when(p < PAIRS - 1)
                    def _():
                        prepare(p + 1)

                    halo(p).wait()

                    @pl.when(p < PAIRS - 1)
                    def _():
                        halo(p + 1).start()

                frame = FD * tm + j
                key_frame = frame - 1 + slot
                allowed = ((key_frame >= 0) & (key_frame < lengths[m])) | (frame >= lengths[m])
                bias = jnp.where(allowed & key_real, 0.0, NEG)
                scores[t] = contract(stack_heads(qkv[p, j + 1, m, :, :PW]), window(p, m, j, 1), 1, 1) + bias
            if 0 <= t - 1 < NB:
                jj, m = order[t - 1]
                s = scores.pop(t - 1)
                e = jnp.exp(s - jnp.max(s, axis=-1, keepdims=True))
                probs[p, near_last(jj), m] = e.astype(bf16)
            if 0 <= t - 2 < NB:
                jj, m = order[t - 2]
                j = near_last(jj)
                values = jnp.concatenate([window(p, m, j, 2), ones], axis=1)
                both = contract(probs[p, j, m], values, 1, 0)
                inverse = 1.0 / join_heads(both[:, PW:])
                r.os[p, j, span(m)] = join_heads(both[:, :PW]) * inverse
                scale[p, j, span(m)] = inverse

    def pieces(stage, *items):
        return [(stage, i) for i in items]

    U, W = UP, DOWN
    forward_steps = [
        {
            0: pieces("gather_2", 2, OUT) + pieces("gather_3", 1),
            4: pieces("gather_2", U),
            8: pieces("gather_2", W) + pieces("gather_3", 2),
        },
        {
            0: pieces("gather_2", U + 1) + pieces("gather_3", OUT),
            5: pieces("gather_2", W + 1) + pieces("gather_3", U),
        },
        {
            0: pieces("gather_2", U + 2) + pieces("gather_3", W),
            5: pieces("gather_2", W + 2) + pieces("gather_3", U + 1),
        },
    ]

    def add_grad(i, value, first=False):
        acc = r.piece_acc
        value = value.reshape(acc.shape[1:])
        acc[i] = value if first else acc[i] + value

    def small_grad(name, value):
        gsm[AT[name] : AT[name] + 1, :] += col_sum(value)

    def mix(j):
        o = join_pairs(r.os, j).astype(bf16)
        return o, r.x0s[j] + contract(o, r.weights[OUT], 1, 0) + vector("bias_out")

    def feed_start(j, x2s, ga2s, a2s):
        _, x1 = mix(j)
        xhat, _ = norm_stats(x1)
        a2s[j] = (xhat * vector("norm2_gain") + vector("norm2_bias")).astype(bf16)
        x2s[j] = x1 + vector("bias_down")
        ga2s[j] = jnp.zeros((BOTH, D), f32)

    def feed(c, x2s, ga2s, a2s):
        bias = table[pl.ds(UPB + c, 1), :]

        def products(j):
            g2 = join_pairs(r.tops, j)
            return contract(a2s[j], r.weights[UP + c], 1, 0) + bias, g2, contract(g2, r.weights[DOWN + c], 1, 1)

        bias_grad = jnp.zeros((1, D), f32)
        ready = products(0)
        for j in range(FD):
            u, g2, gz = ready
            if j + 1 < FD:
                ready = products(j + 1)
            if fused:
                if j == 2:

                    @pl.when(c > 0)
                    def _():
                        x.sum_2(UP + c - 1)
                        x.sum_2(DOWN + c - 1)

                if j == 1:

                    @pl.when(c == 0)
                    def _():
                        run_steps({1: pieces("gather_2", U + 3, W + 3) + pieces("gather_3", W + 1)}, 1)

                if j == 3:

                    @pl.when(c > 1)
                    def _():
                        x.sum_3(UP + c - 2)
                        x.sum_3(DOWN + c - 2)

                if j == 3:

                    @pl.when(c > 2)
                    def _():
                        x.sum_4(UP + c - 3)
                        x.sum_4(DOWN + c - 3)

                    @pl.when(c < CHUNKS - 2)
                    def _():
                        x.gather_3(UP + c + 2)
                        x.gather_3(DOWN + c + 2)

            cdf = 0.5 + 0.5 * lax.erf(u * (1.0 / math.sqrt(2.0)))
            pdf = jnp.exp(u * u * -0.5) * (1.0 / math.sqrt(2.0 * math.pi))
            z = (u * cdf).astype(bf16)
            gu = (gz * (cdf + u * pdf)).astype(bf16)
            bias_grad = bias_grad + col_sum(gu)
            x2s[j] += contract(z, r.weights[DOWN + c], 1, 0)
            ga2s[j] += contract(gu, r.weights[UP + c], 1, 1)
            add_grad(DOWN + c, contract(z, g2, 0, 0), j == 0)
            add_grad(UP + c, contract(a2s[j], gu, 0, 0), j == 0)
        gsm[pl.ds(UPB + c, 1), :] = bias_grad
        if fused:
            x.sum_1(UP + c)
            x.sum_1(DOWN + c)

    def feed_end(j, raw, scale, x2s, ga2s):
        o, x1 = mix(j)
        xhat, rstd = norm_stats(x1)
        y = (x2s[j] * valid_rows(j)).astype(bf16)
        for k in range(FD):

            @pl.when(j == k)
            def _():
                for m in range(MB):
                    raw[m, FT * k : FT * (k + 1), :] = y[ROWS * m : ROWS * m + FT]

        g2, ga2 = join_pairs(r.tops, j), ga2s[j]
        small_grad("bias_down", g2)
        small_grad("norm2_gain", ga2 * xhat)
        small_grad("norm2_bias", ga2)
        gx1 = g2.astype(f32) + norm_back(ga2, xhat, rstd, vector("norm2_gain"))
        gy = gx1.astype(bf16)
        small_grad("bias_out", gy)
        add_grad(OUT, contract(o, gy, 0, 0))
        go = contract(gy, r.weights[OUT], 1, 1).astype(bf16).astype(f32)
        spread_pairs(r.tops, j, slice(0, BOTH), go * join_pairs(scale, j))
        spread_pairs(r.gx1s, j, slice(0, BOTH), gx1)

    near = FD - (FD - 1) * tm
    away = (FD + 1) * (1 - tm)

    def back(p):
        return pltpu.make_async_remote_copy(
            src_ref=r.back_out, dst_ref=r.back_in.at[p],
            send_sem=r.back_sem.at[0, p], recv_sem=r.back_sem.at[1, p], device_id=peer, device_id_type=MESH,
        )

    def attend_back(p, probs, gkv, steps):
        gkv[...] = jnp.zeros_like(gkv)
        order = [(FD - 1 - jj, m) for jj in range(FD) for m in range(MB)]
        diffs, slopes = {}, {}
        for t in range(NB + 2):
            steps_at(steps, p, t)
            if t < NB:
                jj, m = order[t]
                j = near_last(jj)
                o = r.os[p, j, span(m)]
                go = stack_heads(r.tops[p, j, span(m)])
                delta = jnp.sum(go.astype(f32) * jnp.concatenate([o, o], axis=0), axis=-1, keepdims=True)
                diffs[t] = contract(go, window(p, m, j, 2), 1, 1) - delta
                gv = jnp.transpose(contract(go, probs[p, j, m], 0, 0)).reshape(3, ROWS, PW)
                gkv[pl.ds(j, 3), m, :, PW:] += gv
            if 0 <= t - 1 < NB:
                jj, m = order[t - 1]
                slopes[t - 1] = (probs[p, near_last(jj), m].astype(f32) * diffs.pop(t - 1)).astype(bf16)
            if 0 <= t - 2 < NB:
                jj, m = order[t - 2]
                j = near_last(jj)
                gs = slopes.pop(t - 2)
                q = stack_heads(qkv[p, j + 1, m, :, :PW])
                gk = jnp.transpose(contract(q, gs, 0, 0)).reshape(3, ROWS, PW)
                gkv[pl.ds(j, 3), m, :, :PW] += gk
                gq = join_heads(contract(gs, window(p, m, j, 1), 1, 0))
                qkv[p, j + 1, m, :, :PW] = (gq * 0.125).astype(bf16)
            if t == MB + 1:
                r.back_out[...] = gkv[away].astype(bf16)
                back(p).start()
        back(p).wait_send()

        @pl.when(p > 0)
        def _():
            complete(p - 1)

        r.near_acc[...] = gkv[near]
        qkv[p, 1 : FD + 1, :, :, PW:] = gkv[1 : FD + 1].astype(bf16)

    def complete(p):
        back(p).wait_recv()
        qkv[p, near, :, :, PW:] = (r.near_acc[...] + r.back_in[p].astype(f32)).astype(bf16)
        total = 0.0
        for j in range(FD):
            total = total + contract(r.a1s[j], qkv[p, j + 1].reshape(BOTH, D), 0, 0)
        r.piece_acc[p] = total.reshape(r.piece_acc.shape[1:])
        if fused:
            x.sum_1(p)

    backward_steps = [
        {
            1: pieces("sum_2", OUT),
            8: pieces("sum_3", U + 3, W + 3),
        },
        {
            0: pieces("sum_4", U + 2, W + 2),
            5: pieces("sum_3", OUT),
        },
        {
            1: pieces("sum_2", 0) + pieces("sum_4", U + 3, W + 3),
            8: pieces("sum_3", 0) + pieces("sum_4", OUT),
        },
    ]

    def middle(probs, raw):
        scale = r.gx1s

        def forward(p, carry):
            attend(p, probs, scale, forward_steps)
            return carry

        prepare(0)
        halo(0).start()
        lax.fori_loop(0, PAIRS, forward, 0)
        if fused:
            x.gather_4(OUT)
            settle(OUT)

        def feeding(x2s, ga2s, a2s):
            def start(j, carry):
                feed_start(j, x2s, ga2s, a2s)
                return carry

            def one(c, carry):
                if fused:
                    for i in (UP + c, DOWN + c):
                        x.gather_4(i)
                        settle(i)
                feed(c, x2s, ga2s, a2s)
                return carry

            def end(j, carry):
                feed_end(j, raw, scale, x2s, ga2s)
                return carry

            lax.fori_loop(0, FD, start, 0)
            lax.fori_loop(0, CHUNKS, one, 0)
            lax.fori_loop(0, 2, end, 0)
            run_steps({0: pieces("sum_2", U + 3, W + 3) + pieces("sum_3", U + 2, W + 2)}, 0)
            lax.fori_loop(2, FD, end, 0)
            pltpu.make_async_copy(raw, r.block_output, r.local_sem.at[0]).start()
            run_steps({0: pieces("sum_1", OUT) + pieces("sum_4", U + 1, W + 1)}, 0)

        pl.run_scoped(
            feeding, pltpu.VMEM((FD, BOTH, D), f32), pltpu.VMEM((FD, BOTH, D), f32), pltpu.VMEM((FD, BOTH, D), bf16)
        )

        def backward(gkv):
            def step(p, carry):
                attend_back(p, probs, gkv, backward_steps)
                return carry

            lax.fori_loop(0, PAIRS, step, 0)
            complete(PAIRS - 1)
            pltpu.make_async_copy(raw, r.block_output, r.local_sem.at[0]).wait()

        pl.run_scoped(backward, pltpu.VMEM((FD + 2, MB, ROWS, 2 * PW), f32))

    pl.run_scoped(
        middle, pltpu.VMEM((PAIRS, FD, MB, BOTH, WIN), bf16), pltpu.VMEM((MB, FD * FT, D), bf16)
    )

    final_steps = {
        0: pieces("sum_2", 1),
        1: pieces("sum_2", 2),
        3: pieces("sum_4", 0),
    }

    def last(gvis):
        for j in range(FD):
            run_steps(final_steps, j)
            xhat, rstd = norm_stats(r.x0s[j])
            ga1 = 0.0
            for p in range(PAIRS):
                gp = qkv[p, j + 1].reshape(BOTH, D)
                sums = col_sum(gp)
                cols = slice(PW * p, PW * (p + 1))
                gsm[AT["bias_query"] : AT["bias_query"] + 1, cols] += sums[:, :PW]
                gsm[AT["bias_value"] : AT["bias_value"] + 1, cols] += sums[:, 2 * PW :]
                ga1 = ga1 + contract(gp, r.weights[p], 1, 1)
            small_grad("norm1_gain", ga1 * xhat)
            small_grad("norm1_bias", ga1)
            gb = (join_pairs(r.gx1s, j) + norm_back(ga1, xhat, rstd, vector("norm1_gain"))) * valid_rows(j)
            masked = r.flag_cols[:BOTH, j : j + 1] > 0.5
            small_grad("mask_token", jnp.where(masked, gb, 0.0))
            seen = jnp.where(masked, 0.0, gb)
            for m in range(MB):
                gsm[:ROWS, :] += gb[span(m)]
                r.sumgb[m * FD + j : m * FD + j + 1, :] = col_sum(gb[span(m)])
                gvis[m, FT * j : FT * (j + 1), :] = seen[ROWS * m : ROWS * m + FT]
        store_seen = pltpu.make_async_copy(gvis, r.grad_visible, r.local_sem.at[0])
        store_seen.start()
        blend = time_weights((8, NB), 1, tm, lengths)
        total = jnp.zeros((8, D), f32)
        for b in range(NB):
            total = total + blend[:, b : b + 1] * r.sumgb[b : b + 1, :]
        gsm[TIME : TIME + 8, :] = total
        if fused:
            r.small_acc[...] = jnp.transpose(gsm[...]).reshape(r.small_acc.shape)
            x.sum_1(SMALLS)
            x.sum_3(1)
            x.sum_2(SMALLS)
            x.sum_3(2)
            for c in range(2):
                share = x.sum_5(UP + c)
                for i in range(n):
                    at = part * (4 * i + c)
                    r.grad_w_up[:, at : at + part] = share[:, part * i : part * (i + 1)]
                r.grad_w_down[part * c : part * (c + 1)] = x.sum_5(DOWN + c)
            x.sum_3(SMALLS)
            x.sum_4(1)
            x.sum_4(2)
            for c in range(2, CHUNKS):
                share = x.sum_5(UP + c)
                for i in range(n):
                    at = part * (4 * i + c)
                    r.grad_w_up[:, at : at + part] = share[:, part * i : part * (i + 1)]
                r.grad_w_down[part * c : part * (c + 1)] = x.sum_5(DOWN + c)
            r.grad_w_out[...] = x.sum_5(OUT)
            for p in range(PAIRS):
                share = x.sum_5(p)
                for t in range(3):
                    c = D * t + PW * p
                    r.grad_w_qkv[:, c : c + PW] = share[:, PW * t : PW * (t + 1)]
            x.sum_4(SMALLS)
            r.grad_small[...] = x.sum_5(SMALLS)
        store_seen.wait()
        if fused:

            def sent(i, carry):
                x.gather_sent(i)
                x.sum_sent(i)
                return carry

            lax.fori_loop(0, PIECES, sent, 0)
            x.gather_sent(SMALLS)
            x.sum_sent(SMALLS)

    pl.run_scoped(last, pltpu.VMEM((MB, FD * FT, D), f32))


def unpack_body(names, part, *refs):
    r = SimpleNamespace(**dict(zip(names, refs, strict=True)))
    parts = [(r.out_in.at[m], r.buf_block.at[m], r.block_output.at[m]) for m in range(MB)]
    parts += [
        (r.seen_in.at[m, rows], r.buf_seen.at[m, rows], r.grad_visible.at[m, rows])
        for m in range(MB)
        for rows in (slice(0, FD * FT // 2), slice(FD * FT // 2, FD * FT))
    ]
    parts += [
        (getattr(r, "w_%s_in" % name), getattr(r, "buf_" + name), getattr(r, "grad_w_" + name))
        for name in ("qkv", "out", "up", "down")
    ]
    loads = [pltpu.make_async_copy(src, buf, r.sem.at[0, i]) for i, (src, buf, _) in enumerate(parts)]
    stores = [pltpu.make_async_copy(buf, dst, r.sem.at[1, i]) for i, (_, buf, dst) in enumerate(parts)]
    load_small = pltpu.make_async_copy(r.small_in, r.buf_small, r.small_sem)
    load_small.start()
    for load in loads:
        load.start()
    load_small.wait()
    small = r.buf_small[...]
    r.tmp_space_embed[...] = small[:, :FT]
    r.wide[:part] = small
    rows = jnp.transpose(r.wide[:, PW:])
    r.tmp_time_embed[...] = rows[TIME - PW : TIME - PW + 8, :part]
    for name in VECTORS:
        at = AT[name] - PW
        getattr(r, "tmp_" + name)[...] = rows[at : at + 1, :part].reshape(part)
    for c in range(CHUNKS):
        r.line[0:1, part * c : part * (c + 1)] = rows[UPB + c - PW : UPB + c + 1 - PW, :part]
    r.tmp_bias_up[...] = r.line[0:1, : 4 * part].reshape(4 * part)
    tables = ("space_embed", "time_embed", "bias_up") + VECTORS
    hand_on = [
        pltpu.make_async_copy(getattr(r, "tmp_" + name), getattr(r, "grad_" + name), r.table_sem.at[i])
        for i, name in enumerate(tables)
    ]
    for copy in hand_on:
        copy.start()
    for load, store in zip(loads, stores):
        load.wait()
        store.start()
    for store in stores + hand_on:
        store.wait()


def call(fused, n, part, inputs, outputs, scratch, arrays):
    smem = pl.BlockSpec(memory_space=pltpu.SMEM)
    vmem = pl.BlockSpec(memory_space=pltpu.VMEM)
    hbm = pl.BlockSpec(memory_space=pl.ANY)
    spec = {"s": smem, "v": vmem, "h": hbm}
    names = list(inputs) + list(outputs) + list(scratch)
    return pl.pallas_call(
        functools.partial(body, names, fused, n, part),
        out_shape=tuple(shape for shape, _ in outputs.values()),
        in_specs=[spec[where] for where in inputs.values()],
        out_specs=tuple(spec[where] for _, where in outputs.values()),
        scratch_shapes=list(scratch.values()),
        compiler_params=pltpu.CompilerParams(
            collective_id=0, has_side_effects=True, vmem_limit_bytes=64 * 2**20 - 2**16
        ),
    )(*arrays)


def common_scratch():
    V, S = pltpu.VMEM, pltpu.SemaphoreType.DMA
    return {
        "flag_rows": V((8, 512), f32),
        "flag_cols": V((512, 8), f32),
        "pair_bias": V((PAIRS, 8, PW), f32),
        "x0s": V((FD, BOTH, D), f32),
        "gx1s": V((PAIRS, FD, BOTH, PW), f32),
        "tops": V((PAIRS, FD, BOTH, PW), bf16),
        "os": V((PAIRS, FD, BOTH, PW), f32),
        "a1s": V((FD, BOTH, D), bf16),
        "qkv": V((PAIRS, FD + 2, MB, ROWS, D), bf16),
        "temporal": V((NB, D), f32),
        "sumgb": V((NB, D), f32),
        "back_out": V((MB, ROWS, 2 * PW), bf16),
        "back_in": V((PAIRS, MB, ROWS, 2 * PW), bf16),
        "near_acc": V((MB, ROWS, 2 * PW), f32),
        "halo_sem": S((2, PAIRS)),
        "back_sem": S((2, PAIRS)),
        "local_sem": S((24,)),
    }


def whole_weights(shards, part):
    s = shards
    small = jnp.concatenate(
        [s.space_embed.T, jnp.zeros((part, TIME - FT), bf16), s.time_embed.T]
        + [getattr(s, name)[:, None] for name in VECTORS]
        + [s.bias_up.reshape(part, 4), jnp.zeros((part, SMALL - UPB - 4), bf16)],
        axis=1,
    )
    pairs = [s.w_qkv[:, D * t + PW * p : D * t + PW * (p + 1)] for p in range(PAIRS) for t in range(3)]
    pack = jnp.concatenate(pairs + [s.w_out, s.w_up, s.w_down.reshape(part, FF), small], axis=1)
    return lax.all_gather(pack, "clip", axis=0, tiled=True)


def local(*args):
    keys = (
        "visible", "mask_flags", "frames", "assign", "cotangent", "mask_token", "time_embed", "space_embed",
        "norm1_gain", "norm1_bias", "w_qkv", "bias_query", "bias_value", "w_out", "bias_out", "norm2_gain",
        "norm2_bias", "w_up", "bias_up", "w_down", "bias_down",
    )
    a = SimpleNamespace(**dict(zip(keys, args, strict=True)))
    n = lax.axis_size("clip")
    part = D // n
    V, S, sds = pltpu.VMEM, pltpu.SemaphoreType.DMA, jax.ShapeDtypeStruct
    scratch = common_scratch()
    big = {"block_output": (sds(a.visible.shape, bf16), "h"), "grad_visible": (sds(a.visible.shape, f32), "h")}

    if part % 8 == 0 and n % 16 == 0:
        high = n // 4
        a.assign = a.assign.reshape(MB)
        a.space_embed = a.space_embed.T
        inputs = {key: "v" for key in keys}
        inputs.update(frames="s", assign="s", visible="h", cotangent="h", w_qkv="h", w_out="h", w_down="h")
        grads = {"grad_" + key: sds(getattr(a, key).shape, f32) for key in keys[5:]}
        outputs = dict(big)
        for key in ("grad_w_qkv", "grad_w_out", "grad_w_up", "grad_w_down"):
            outputs[key] = (grads[key], "v")
        outputs["grad_small"] = (sds((part, SMALL), f32), "v")
        scratch.update(
            {
                "rows": V((32, PW), f32),
                "cols": V((part, SMALL), f32),
                "table": V((SMALL, D), f32),
                "shuffle": V((CHUNKS, part, D), f32),
                "weights": V((PIECES, D, D), bf16),
                "gsm": V((SMALL, D), f32),
            }
        )
        for kind, count, width in (("piece_", (PIECES,), D), ("small_", (), SMALL)):
            scratch[kind + "whole"] = V((*count, high, 2, 2, part, width), bf16)
            scratch[kind + "acc"] = V((*count, n, part, width), f32)
            for key, lead in (("snd", (2, high)), ("rcv1", (2, high)), ("rcv2", (high,)), ("rcv3", (high,)), ("snd4", ()), ("rcv4", ())):
                scratch[kind + key] = V((*count, *lead, part, width), bf16)
        for key in ("g2s", "g2r", "g3s", "g3r", "s1s", "s1r", "s2s", "s2r", "s4s", "s4r"):
            scratch[key] = S((PIECES + 1,))
        for key in ("g1s", "g1r", "s3s", "s3r"):
            scratch[key] = S((PIECES + 1, high))
        results = call(True, n, part, inputs, outputs, scratch, [getattr(a, key) for key in keys])
        where = ["h"] * 7
        finals = {"block_output": big["block_output"], "grad_visible": big["grad_visible"]}
        finals.update({key: (shape, "h") for key, shape in grads.items()})
        names = ["out_in", "seen_in", "w_qkv_in", "w_out_in", "w_up_in", "w_down_in", "small_in"]
        spec = {"v": pl.BlockSpec(memory_space=pltpu.VMEM), "h": pl.BlockSpec(memory_space=pl.ANY)}
        held = {"wide": V((PW, SMALL), f32), "line": V((8, 4 * part), f32), "sem": S((2, 10))}
        for name, key in (("out", "w_out"), ("qkv", "w_qkv"), ("up", "w_up"), ("down", "w_down")):
            held["buf_" + name] = V(grads["grad_" + key].shape, f32)
        for key, shape in grads.items():
            if "_w_" not in key:
                held["tmp_" + key[5:]] = V(shape.shape, f32)
        held.update({"buf_small": V((part, SMALL), f32), "small_sem": S(()), "table_sem": S((len(grads),))})
        held["buf_block"] = V(a.visible.shape, bf16)
        held["buf_seen"] = V(a.visible.shape, f32)
        final = pl.pallas_call(
            functools.partial(unpack_body, names + list(finals) + list(held), part),
            out_shape=tuple(shape for shape, _ in finals.values()),
            in_specs=[spec[w] for w in where],
            out_specs=tuple(spec[w] for _, w in finals.values()),
            scratch_shapes=list(held.values()),
        )(*results)
        final = dict(zip(finals, final, strict=True))
        final["grad_space_embed"] = final["grad_space_embed"].T
        return tuple(final.values())

    whole = whole_weights(a, part)
    cuts = (0, 3 * D, 4 * D, 4 * D + FF, 4 * D + 2 * FF, 4 * D + 2 * FF + SMALL)
    wqkv, wout, wup, wdown, wsmall = (whole[:, i:j] for i, j in zip(cuts[:-1], cuts[1:]))
    values = {
        "frames": a.frames, "assign": a.assign.reshape(MB), "visible": a.visible, "mask_flags": a.mask_flags,
        "cotangent": a.cotangent,
        "table": wsmall.T.at[UPB : UPB + 4].set(wsmall[:, UPB : UPB + 4].reshape(CHUNKS, HIDDEN)).astype(f32),
        "weights": jnp.stack(
            [wqkv[:, D * p : D * (p + 1)] for p in range(PAIRS)]
            + [wout]
            + [wup[:, HIDDEN * c : HIDDEN * (c + 1)] for c in range(CHUNKS)]
            + list(wdown.reshape(CHUNKS, HIDDEN, D))
        ),
    }
    inputs = {key: "v" for key in values}
    inputs.update(frames="s", assign="s", visible="h", cotangent="h")
    outputs = dict(big)
    outputs["piece_acc"] = (sds((PIECES, 1, D, D), f32), "v")
    outputs["gsm"] = (sds((SMALL, D), f32), "v")
    out, gvis, gpieces, gsm = call(False, n, part, inputs, outputs, scratch, list(values.values()))
    gpieces = gpieces[:, 0]
    gdown = gpieces[DOWN:].reshape(D, FF)
    gsmall = gsm.T.at[:, UPB : UPB + 4].set(gsm[UPB : UPB + 4].reshape(D, 4))
    grads = jnp.concatenate([*gpieces[:DOWN], gdown, gsmall], axis=1)
    share = lax.psum_scatter(grads, "clip", scatter_dimension=0, tiled=True)
    share = lax.psum(share.astype(bf16), "tm").astype(f32)
    sqkv, sout, sup, sdown, ssmall = (share[:, i:j] for i, j in zip(cuts[:-1], cuts[1:]))
    sqkv = jnp.concatenate(
        [sqkv[:, D * p + PW * t : D * p + PW * (t + 1)] for t in range(3) for p in range(PAIRS)], axis=1
    )
    one = {name: ssmall[:, AT[name]] for name in VECTORS}
    return (
        out, gvis, one["mask_token"], ssmall[:, TIME : TIME + 8].T, ssmall[:, :FT].T, one["norm1_gain"],
        one["norm1_bias"], sqkv, one["bias_query"], one["bias_value"], sout, one["bias_out"], one["norm2_gain"],
        one["norm2_bias"], sup, ssmall[:, UPB : UPB + 4].reshape(-1), sdown.reshape(-1, D), one["bias_down"],
    )


def solution(mesh):
    rows = P(None, ("clip", "tm"), None)
    vec = P("clip")
    mat = P("clip", None)
    cols = P(None, "clip")
    in_specs = (
        rows, P(None, ("clip", "tm")), P(), cols, rows,
        vec, cols, cols, vec, vec, mat, vec, vec, mat, vec, vec, vec, mat, vec, mat, vec,
    )
    out_specs = (
        rows, rows, vec, cols, cols, vec, vec, mat, vec, vec, mat, vec, vec, vec, mat, vec, mat, vec,
    )
    return jax.shard_map(local, mesh=mesh, in_specs=in_specs, out_specs=out_specs, check_vma=False)
```
